32 devices in a mesh: fsdp: 8 (over z, y), seq: 4 (over x, core).
Axes of the slice: x: 2, y: 2, z: 4, core: 2. Of those that a mesh axis runs over, the one named last changes fastest.
Arguments:
- tokens: bfloat16 [64, 320, 1024], P('fsdp', 'seq'), may hold values from -6 to 6
- lengths: int32 [64], P('fsdp'), may hold values from 200 to 320, as said below
- attn_gain: bfloat16 [1024], P('fsdp'), may hold values from 0.5 to 1.5
- attn_shift: bfloat16 [1024], P('fsdp'), may hold values from -4 to 4
- attn_weight: bfloat16 [1024, 3072], P('fsdp'), may hold values from -0.1875 to 0.1875
- attn_bias: bfloat16 [2048], P('fsdp'), may hold values from -4 to 4
- out_weight: bfloat16 [1024, 1024], P('fsdp'), may hold values from -0.75 to 0.75
- out_bias: bfloat16 [1024], P('fsdp'), may hold values from -4 to 4
- mlp_gain: bfloat16 [1024], P('fsdp'), may hold values from 0.5 to 1.5
- mlp_shift: bfloat16 [1024], P('fsdp'), may hold values from -4 to 4
- up_weight: bfloat16 [1024, 4096], P('fsdp'), may hold values from -0.1875 to 0.1875
- up_bias: bfloat16 [4096], P('fsdp'), may hold values from -4 to 4
- down_weight: bfloat16 [4096, 1024], P('fsdp'), may hold values from -0.09375 to 0.09375
- down_bias: bfloat16 [1024], P('fsdp'), may hold values from -4 to 4
- cotangent: bfloat16 [64, 320, 1024], P('fsdp', 'seq'), may hold values from -6 to 6
Outputs:
- layer_out: bfloat16 [64, 320, 1024], P('fsdp', 'seq')
- input_grad: bfloat16 [64, 320, 1024], P('fsdp', 'seq')
- attn_gain_grad: float32 [1024], P('fsdp')
- attn_shift_grad: float32 [1024], P('fsdp')
- attn_weight_grad: float32 [1024, 3072], P('fsdp')
- attn_bias_grad: float32 [2048], P('fsdp')
- out_weight_grad: float32 [1024, 1024], P('fsdp')
- out_bias_grad: float32 [1024], P('fsdp')
- mlp_gain_grad: float32 [1024], P('fsdp')
- mlp_shift_grad: float32 [1024], P('fsdp')
- up_weight_grad: float32 [1024, 4096], P('fsdp')
- up_bias_grad: float32 [4096], P('fsdp')
- down_weight_grad: float32 [4096, 1024], P('fsdp')
- down_bias_grad: float32 [1024], P('fsdp')
The draws below stay inside these ranges and needn't reach their ends.
Inputs may be any that keep to these rules, and one draw needn't show every extreme that they name: `lengths`: valid slots come first in each image; among the 8 images of each index of fsdp one has exactly 320 valid slots; some image has 200.
All inputs are finite; a program needn't handle non-finite values.
Results may differ from the reference program's by a relative error of at most 0.015.
Values may be sent and summed in bfloat16 or wider, within the bound.
No kernel may reach another device: no remote copies, remote signals or barrier semaphores. Data moves between devices by JAX's collectives and lax.ppermute only.
A program may use at most 192 MiB of HBM per device.

```python
from functools import partial
import jax
import jax.numpy as jnp
from jax import lax

D = 1024
HEADS = 16
HEAD_DIM = 64
FF = 4096
SLOTS = 320
IMG_DEV = 8
IMAGES = 64
N_FSDP = 8


def draw_lengths(key, part):
    low_len = SLOTS * 5 // 8
    groups = IMAGES // IMG_DEV
    first_key = jax.random.fold_in(key, 11)
    second_key = jax.random.fold_in(key, 23)
    values = jax.random.randint(first_key, (groups, IMG_DEV), low_len, SLOTS + 1)
    chosen = jax.random.randint(second_key, (groups, 1), 0, IMG_DEV)
    columns = jnp.arange(IMG_DEV, dtype=jnp.int32)[None, :]
    row_ids = jnp.arange(groups, dtype=jnp.int32)[:, None]
    values = jnp.where(columns == chosen, SLOTS, values)
    short_col = (chosen[0:1, :] + 1) % IMG_DEV
    values = jnp.where((row_ids == 0) & (columns == short_col), low_len, values)
    return values.reshape(IMAGES).astype(jnp.int32)


def levels(own_key, shape, shards, low, largest):
    def one(dim, shards_of):
        steps = jax.random.uniform(jax.random.fold_in(jax.random.fold_in(own_key, 6), dim), (shards_of,), jnp.float32, low / len(shards), largest / len(shards))
        return jnp.repeat(jnp.exp(steps), shape[dim] // shards_of).reshape((-1,) + (1,) * (len(shape) - dim - 1))

    level = one(*shards[0])
    for cut in shards[1:]:
        level = level * one(*cut)
    return level


def normal_values(key, dims, width, limit, pieces=(), kind=jnp.bfloat16):
    entries = width * jax.random.normal(key, dims, jnp.float32)
    if pieces:
        entries = entries * levels(key, dims, pieces, -0.22, 0.18)
    return jnp.clip(entries, -limit, limit).astype(kind)


def setup_inputs(seed: int = 0) -> dict:
    key_of = jax.random.split(jax.random.key(seed), 16)
    tokens = normal_values(key_of[0], (IMAGES, SLOTS, D), 1.0, 6.0, ((0, 8), (1, 4)))
    lengths = draw_lengths(jax.random.fold_in(key_of[15], 71), 0)
    attn_gain = jnp.clip(1.0 + 0.1 * jax.random.normal(key_of[2], (D,), jnp.float32), 0.5, 1.5).astype(jnp.bfloat16)
    attn_shift = normal_values(key_of[3], (D,), 0.3, 4.0, ((0, 8),))
    attn_weight = normal_values(key_of[4], (D, 3 * D), D ** -0.5, 0.1875, ((0, 8),))
    attn_bias = normal_values(key_of[5], (2 * D,), 0.3, 4.0, ((0, 8),))
    out_weight = normal_values(key_of[6], (D, D), (D // 16) ** -0.5, 0.75, ((0, 8),))
    out_bias = normal_values(key_of[7], (D,), 0.3, 4.0, ((0, 8),))
    mlp_gain = jnp.clip(1.0 + 0.1 * jax.random.normal(key_of[8], (D,), jnp.float32), 0.5, 1.5).astype(jnp.bfloat16)
    mlp_shift = normal_values(key_of[9], (D,), 0.3, 4.0, ((0, 8),))
    up_weight = normal_values(key_of[10], (D, FF), D ** -0.5, 0.1875, ((0, 8),))
    up_bias = normal_values(key_of[11], (FF,), 0.3, 4.0, ((0, 8),))
    down_weight = normal_values(key_of[12], (FF, D), FF ** -0.5, 0.09375, ((0, 8),))
    down_bias = normal_values(key_of[13], (D,), 0.3, 4.0, ((0, 8),))
    cotangent = normal_values(key_of[14], (IMAGES, SLOTS, D), 1.0, 6.0, ((0, 8), (1, 4)))
    return dict(tokens=tokens, lengths=lengths, attn_gain=attn_gain, attn_shift=attn_shift, attn_weight=attn_weight, attn_bias=attn_bias, out_weight=out_weight, out_bias=out_bias, mlp_gain=mlp_gain, mlp_shift=mlp_shift, up_weight=up_weight, up_bias=up_bias, down_weight=down_weight, down_bias=down_bias, cotangent=cotangent)


@jax.custom_vjp
def low(v):
    return lax.optimization_barrier(v.astype(jnp.bfloat16)).astype(jnp.float32)

@jax.custom_vjp
def low_back(v):
    return v

def low_keep(v):
    return (low(v), None)

def low_pass(kept, grad):
    return (grad,)

def back_keep(v):
    return (v, None)

def back_low(kept, grad):
    return (low(grad),)
low.defvjp(low_keep, low_pass)
low_back.defvjp(back_keep, back_low)
epsilon = 1e-06
highest = lax.Precision.HIGHEST

def layer_norm(values, gain, shift):
    center = values - lax.optimization_barrier(jnp.mean(values, axis=-1, keepdims=True))
    spread = lax.optimization_barrier(jnp.mean(center * center, axis=-1, keepdims=True))
    return center * lax.rsqrt(spread + epsilon) * gain + shift

def matmul(left, right):
    return jnp.dot(left, right, precision=highest)

def image_block(params, block_tokens, block_lengths):
    gain_attn, shift_attn, qkv_full, qv_bias, proj_out, bias_out, gain_mlp, shift_mlp, up_full, bias_up, down_full, bias_down = params
    image_count = block_tokens.shape[0]
    key_mask = jnp.arange(SLOTS, dtype=jnp.int32)[None, :] < block_lengths[:, None]
    normed_a = low(layer_norm(block_tokens, gain_attn, shift_attn))
    bias_joint = jnp.concatenate([qv_bias[:D], jnp.zeros((D,), qv_bias.dtype), qv_bias[D:]])
    joint_proj = low_back(low(matmul(normed_a, qkv_full) + bias_joint))
    joint_proj = joint_proj.reshape(image_count, SLOTS, 3, HEADS, HEAD_DIM)
    query_part = joint_proj[:, :, 0]
    keyset = joint_proj[:, :, 1]
    value_part = joint_proj[:, :, 2]
    raw_scores = low_back(jnp.einsum('gqhe,gkhe->ghqk', query_part, keyset, precision=highest))
    scaled = jnp.where(key_mask[:, None, None, :], raw_scores * HEAD_DIM ** (-0.5), -1000000000.0)
    probs = jax.nn.softmax(scaled, axis=-1)
    context = jnp.einsum('ghqk,gkhe->gqhe', low(probs), value_part, precision=highest)
    context = low_back(low(context.reshape(image_count, SLOTS, D)))
    branch = low_back(matmul(context, proj_out) + bias_out)
    middle = block_tokens + branch
    normed_b = low(layer_norm(middle, gain_mlp, shift_mlp))
    hidden_pre = low_back(matmul(normed_b, up_full) + bias_up)
    hidden = low(jax.nn.gelu(hidden_pre, approximate=False))
    result = middle + matmul(hidden, down_full) + bias_down
    return jnp.where(key_mask[:, :, None], result, 0.0)

def reference(tokens, lengths, attn_gain, attn_shift, attn_weight, attn_bias, out_weight, out_bias, mlp_gain, mlp_shift, up_weight, up_bias, down_weight, down_bias, cotangent):
    params = tuple((weight_arg.astype(jnp.float32) for weight_arg in (attn_gain, attn_shift, attn_weight, attn_bias, out_weight, out_bias, mlp_gain, mlp_shift, up_weight, up_bias, down_weight, down_bias)))
    tokens_wide = tokens.astype(jnp.float32)
    grouped_lengths = lengths.reshape(N_FSDP, IMG_DEV).astype(jnp.int32)

    def forward(params, tokens_wide):
        block_fn = jax.checkpoint(partial(image_block, params))

        def run_group(inputs):
            return block_fn(inputs[0], inputs[1])
        shaped = tokens_wide.reshape(N_FSDP, IMG_DEV, SLOTS, D)
        outputs = lax.map(run_group, (shaped, grouped_lengths))
        return outputs.reshape(IMAGES, SLOTS, D)
    output, pullback = jax.vjp(forward, params, tokens_wide)
    grad_params, grad_tokens = pullback(cotangent.astype(jnp.float32))
    return (output.astype(jnp.bfloat16), grad_tokens.astype(jnp.bfloat16), grad_params[0], grad_params[1], grad_params[2], grad_params[3], grad_params[4], grad_params[5], grad_params[6], grad_params[7], grad_params[8], grad_params[9], grad_params[10], grad_params[11])
```

```python
import functools

import jax
import jax.numpy as jnp
from jax import lax
from jax.experimental import pallas as pl
from jax.experimental.pallas import tpu as pltpu
from jax.sharding import PartitionSpec as P

HEAD_DIM = 64
LANES = 128
EPSILON = 1e-06
BF16 = jnp.bfloat16
F32 = jnp.float32
ALL = ("fsdp", "seq")


def layer_stats(values):
    center = values - jnp.mean(values, axis=-1, keepdims=True)
    inv_std = lax.rsqrt(jnp.mean(center * center, axis=-1, keepdims=True) + EPSILON)
    return center * inv_std, inv_std


def norm_back(grad_norm, gain, normal, inv_std):
    scaled = grad_norm * gain
    return inv_std * (
        scaled
        - jnp.mean(scaled, axis=-1, keepdims=True)
        - normal * jnp.mean(scaled * normal, axis=-1, keepdims=True)
    )


def contract(a, b, ca, cb):
    return lax.dot_general(a, b, (((ca,), (cb,)), ((), ())), preferred_element_type=F32)


def head_probs(q, k, head, lane, key_ok):
    q_own = jnp.where(lane == head, q, jnp.zeros_like(q))
    scores = contract(q_own, k, 1, 1) * HEAD_DIM ** (-0.5)
    scores = jnp.where(key_ok, scores, -1000000000.0)
    top = jnp.max(scores, axis=-1, keepdims=True)
    exps = jnp.exp(scores - top)
    return exps * (1.0 / jnp.sum(exps, axis=-1, keepdims=True))


def masks(length, slots):
    lane = lax.broadcasted_iota(jnp.int32, (slots, LANES), 1) // HEAD_DIM
    key_ok = lax.broadcasted_iota(jnp.int32, (slots, slots), 1) < length
    return lane, key_ok


def attend_kernel(len_ref, q_ref, k_ref, v_ref, out_ref):
    q, k, v = q_ref[0], k_ref[0], v_ref[0]
    lane, key_ok = masks(len_ref[pl.program_id(0)], q.shape[0])
    context = jnp.zeros(q.shape, F32)
    for head in range(LANES // HEAD_DIM):
        probs = head_probs(q, k, head, lane, key_ok).astype(BF16)
        context = jnp.where(lane == head, contract(probs, v, 1, 0), context)
    out_ref[0] = context.astype(BF16)


def attend_back_kernel(len_ref, q_ref, k_ref, v_ref, g_ref, dq_ref, dk_ref, dv_ref):
    q, k, v, g = q_ref[0], k_ref[0], v_ref[0], g_ref[0]
    lane, key_ok = masks(len_ref[pl.program_id(0)], q.shape[0])
    dq, dk, dv = (jnp.zeros(q.shape, F32) for _ in range(3))
    for head in range(LANES // HEAD_DIM):
        own = lane == head
        probs = head_probs(q, k, head, lane, key_ok)
        g_own = jnp.where(own, g, jnp.zeros_like(g))
        grad_probs = contract(g_own, v, 1, 1)
        inner = jnp.sum(grad_probs * probs, axis=-1, keepdims=True)
        grad_scores = (probs * (grad_probs - inner) * HEAD_DIM ** (-0.5)).astype(BF16)
        dq = jnp.where(own, contract(grad_scores, k, 1, 0), dq)
        dk = jnp.where(own, contract(grad_scores, q, 0, 0), dk)
        dv = jnp.where(own, contract(probs.astype(BF16), g, 0, 0), dv)
    dq_ref[0], dk_ref[0], dv_ref[0] = dq.astype(BF16), dk.astype(BF16), dv.astype(BF16)


def attention(lengths, joint, grad_context=None):
    images, slots, width = joint.shape[0], joint.shape[1], joint.shape[2] // 3
    pairs = width // LANES
    block = (1, slots, LANES)
    specs = [pl.BlockSpec(block, functools.partial(lambda b, i, h, n: (i, 0, b + h), b * pairs)) for b in range(3)]
    plain = pl.BlockSpec(block, lambda i, h, n: (i, 0, h))
    shape = jax.ShapeDtypeStruct((images, slots, width), BF16)
    back = grad_context is not None
    flops = 2 * images * pairs * 2 * slots * slots * LANES * (5 if back else 2)
    return pl.pallas_call(
        attend_back_kernel if back else attend_kernel,
        grid_spec=pltpu.PrefetchScalarGridSpec(
            num_scalar_prefetch=1,
            grid=(images, pairs),
            in_specs=specs + ([plain] if back else []),
            out_specs=[plain] * 3 if back else plain,
        ),
        out_shape=[shape] * 3 if back else shape,
        cost_estimate=pl.CostEstimate(
            flops=flops,
            bytes_accessed=images * slots * width * 2 * (7 if back else 4),
            transcendentals=images * pairs * 2 * slots * slots,
        ),
    )(lengths, joint, joint, joint, *([grad_context] if back else []))


def gather_weight(weight):
    parts = lax.axis_size("seq")
    rows = weight.shape[0] // parts
    mine = lax.dynamic_slice_in_dim(weight, lax.axis_index("seq") * rows, rows, 0)
    return lax.all_gather(mine, ALL, axis=0, tiled=True)


def scatter_grad(grad):
    mine = lax.psum_scatter(grad, ALL, scatter_dimension=0, tiled=True)
    return lax.all_gather(mine, "seq", axis=0, tiled=True).astype(F32)


def shards(
    tokens,
    lengths,
    attn_gain,
    attn_shift,
    attn_weight,
    attn_bias,
    out_weight,
    out_bias,
    mlp_gain,
    mlp_shift,
    up_weight,
    up_bias,
    down_weight,
    down_bias,
    cotangent,
):
    width = tokens.shape[2]
    members = lax.axis_size("seq")
    images = tokens.shape[0] // members
    slots = tokens.shape[1] * members
    rows = images * slots

    small = (attn_gain, attn_shift, attn_bias, out_bias, mlp_gain, mlp_shift, up_bias, down_bias)
    sizes = [v.shape[0] for v in small]
    small_all = lax.all_gather(jnp.concatenate(small), "fsdp", axis=0).astype(F32)
    cuts = [sum(sizes[:i]) for i in range(len(sizes))]
    gain_a, shift_a, bias_qv, bias_out, gain_b, shift_b, bias_up, bias_down = (
        small_all[:, c : c + n].reshape(-1) for c, n in zip(cuts, sizes)
    )
    qkv_full, out_full, up_full, down_full = (
        gather_weight(w) for w in (attn_weight, out_weight, up_weight, down_weight)
    )

    lens = lax.dynamic_slice_in_dim(lengths, lax.axis_index("seq") * images, images, 0)
    valid = jnp.arange(slots, dtype=jnp.int32)[None, :] < lens[:, None]
    valid = valid.reshape(rows, 1)
    by_image = functools.partial(
        lax.all_to_all, axis_name="seq", split_axis=0, concat_axis=1, tiled=True
    )
    by_slot = functools.partial(
        lax.all_to_all, axis_name="seq", split_axis=1, concat_axis=0, tiled=True
    )
    wide = by_image(tokens).reshape(rows, width).astype(F32)
    cot = by_image(cotangent).reshape(rows, width)

    normal_a, inv_a = layer_stats(wide)
    normed_a = (normal_a * gain_a + shift_a).astype(BF16)
    bias_joint = jnp.concatenate([bias_qv[:width], jnp.zeros((width,), F32), bias_qv[width:]])
    joint = (contract(normed_a, qkv_full, 1, 0) + bias_joint).astype(BF16)
    joint = joint.reshape(images, slots, 3 * width)
    context = attention(lens, joint).reshape(rows, width)
    middle = wide + (contract(context, out_full, 1, 0) + bias_out)
    normal_b, inv_b = layer_stats(middle)
    normed_b = (normal_b * gain_b + shift_b).astype(BF16)
    pre = contract(normed_b, up_full, 1, 0) + bias_up
    cumul = 0.5 * (1.0 + lax.erf(pre * 0.7071067811865476))
    hidden = (pre * cumul).astype(BF16)
    slope = (cumul + pre * jnp.exp(-0.5 * pre * pre) * 0.3989422804014327).astype(BF16)
    result = middle + contract(hidden, down_full, 1, 0) + bias_down
    layer_out = jnp.where(valid, result, 0.0).astype(BF16)
    layer_out = by_slot(layer_out.reshape(images, slots, width))

    grad_out = jnp.where(valid, cot, jnp.zeros_like(cot))
    grad_out_wide = grad_out.astype(F32)
    g_bias_down = jnp.sum(grad_out_wide, axis=0)
    g_down = scatter_grad(contract(hidden, grad_out, 0, 0).astype(BF16))
    grad_pre = (contract(grad_out, down_full, 1, 1) * slope.astype(F32)).astype(BF16)
    g_bias_up = jnp.sum(grad_pre.astype(F32), axis=0)
    g_up = scatter_grad(contract(normed_b, grad_pre, 0, 0).astype(BF16))
    grad_nb = contract(grad_pre, up_full, 1, 1)
    g_gain_b = jnp.sum(grad_nb * normal_b, axis=0)
    g_shift_b = jnp.sum(grad_nb, axis=0)
    grad_middle = grad_out_wide + norm_back(grad_nb, gain_b, normal_b, inv_b)
    grad_branch = grad_middle.astype(BF16)
    g_bias_out = jnp.sum(grad_branch.astype(F32), axis=0)
    g_out = scatter_grad(contract(context, grad_branch, 0, 0).astype(BF16))
    grad_context = contract(grad_branch, out_full, 1, 1).astype(BF16)
    grad_parts = attention(lens, joint, grad_context.reshape(images, slots, width))
    grad_joint = jnp.concatenate(grad_parts, axis=2).reshape(rows, 3 * width)
    joint_sums = jnp.sum(grad_joint.astype(F32), axis=0)
    g_bias_qv = jnp.concatenate([joint_sums[:width], joint_sums[2 * width :]])
    g_qkv = scatter_grad(contract(normed_a, grad_joint, 0, 0).astype(BF16))
    grad_na = contract(grad_joint, qkv_full, 1, 1)
    g_gain_a = jnp.sum(grad_na * normal_a, axis=0)
    g_shift_a = jnp.sum(grad_na, axis=0)
    input_grad = (grad_middle + norm_back(grad_na, gain_a, normal_a, inv_a)).astype(BF16)
    input_grad = by_slot(input_grad.reshape(images, slots, width))

    shard_count = lax.axis_size("fsdp")
    small_grads = (g_gain_a, g_shift_a, g_bias_qv, g_bias_out, g_gain_b, g_shift_b, g_bias_up, g_bias_down)
    packed = jnp.concatenate([v.reshape(shard_count, -1) for v in small_grads], axis=1)
    packed = lax.psum(packed, ALL)
    packed = lax.dynamic_slice_in_dim(packed, lax.axis_index("fsdp"), 1, 0)[0]
    (g_gain_a, g_shift_a, g_bias_qv, g_bias_out, g_gain_b, g_shift_b, g_bias_up, g_bias_down) = (
        packed[c : c + n] for c, n in zip(cuts, sizes)
    )
    return (
        layer_out,
        input_grad,
        g_gain_a,
        g_shift_a,
        g_qkv,
        g_bias_qv,
        g_out,
        g_bias_out,
        g_gain_b,
        g_shift_b,
        g_up,
        g_bias_up,
        g_down,
        g_bias_down,
    )


def solution(mesh):
    rows, vector, matrix = P("fsdp", "seq", None), P("fsdp"), P("fsdp", None)
    weights = (vector, vector, matrix, vector, matrix, vector, vector, vector, matrix, vector, matrix, vector)
    return jax.shard_map(
        shards,
        mesh=mesh,
        in_specs=(rows, vector) + weights + (rows,),
        out_specs=(rows, rows) + weights,
        check_vma=False,
    )
```

```python
import functools

import jax
import jax.numpy as jnp
from jax import lax
from jax.experimental import pallas as pl
from jax.experimental.pallas import tpu as pltpu
from jax.sharding import Mesh
from jax.sharding import PartitionSpec as P

HEAD_DIM = 64
LANES = 128
EPSILON = 1e-06
BF16 = jnp.bfloat16
F32 = jnp.float32
FSDP, SEQ = ("z", "y"), ("x", "c")


def layer_stats(values):
    center = values - jnp.mean(values, axis=-1, keepdims=True)
    inv_std = lax.rsqrt(jnp.mean(center * center, axis=-1, keepdims=True) + EPSILON)
    return center * inv_std, inv_std


def norm_back(grad_norm, gain, normal, inv_std):
    scaled = grad_norm * gain
    return inv_std * (
        scaled
        - jnp.mean(scaled, axis=-1, keepdims=True)
        - normal * jnp.mean(scaled * normal, axis=-1, keepdims=True)
    )


def contract(a, b, ca, cb):
    return lax.dot_general(a, b, (((ca,), (cb,)), ((), ())), preferred_element_type=F32)


def head_probs(q, k, head, lane, key_ok):
    q_own = jnp.where(lane == head, q, jnp.zeros_like(q))
    scores = contract(q_own, k, 1, 1) * HEAD_DIM ** (-0.5)
    scores = jnp.where(key_ok, scores, -1000000000.0)
    top = jnp.max(scores, axis=-1, keepdims=True)
    exps = jnp.exp(scores - top)
    return exps * (1.0 / jnp.sum(exps, axis=-1, keepdims=True))


def masks(length, slots):
    lane = lax.broadcasted_iota(jnp.int32, (slots, LANES), 1) // HEAD_DIM
    key_ok = lax.broadcasted_iota(jnp.int32, (slots, slots), 1) < length
    return lane, key_ok


def attend_kernel(len_ref, q_ref, k_ref, v_ref, out_ref):
    q, k, v = q_ref[0], k_ref[0], v_ref[0]
    lane, key_ok = masks(len_ref[pl.program_id(0)], q.shape[0])
    context = jnp.zeros(q.shape, F32)
    for head in range(LANES // HEAD_DIM):
        probs = head_probs(q, k, head, lane, key_ok).astype(BF16)
        context = jnp.where(lane == head, contract(probs, v, 1, 0), context)
    out_ref[0] = context.astype(BF16)


def attend_back_kernel(len_ref, q_ref, k_ref, v_ref, g_ref, out_ref):
    q, k, v, g = q_ref[0], k_ref[0], v_ref[0], g_ref[0]
    lane, key_ok = masks(len_ref[pl.program_id(0)], q.shape[0])
    dq, dk, dv = (jnp.zeros(q.shape, F32) for _ in range(3))
    for head in range(LANES // HEAD_DIM):
        own = lane == head
        probs = head_probs(q, k, head, lane, key_ok)
        g_own = jnp.where(own, g, jnp.zeros_like(g))
        grad_probs = contract(g_own, v, 1, 1)
        inner = jnp.sum(grad_probs * probs, axis=-1, keepdims=True)
        grad_scores = (probs * (grad_probs - inner) * HEAD_DIM ** (-0.5)).astype(BF16)
        dq = jnp.where(own, contract(grad_scores, k, 1, 0), dq)
        dk = jnp.where(own, contract(grad_scores, q, 0, 0), dk)
        dv = jnp.where(own, contract(probs.astype(BF16), g, 0, 0), dv)
    width = out_ref.shape[2] // 3
    for block, value in enumerate((dq, dk, dv)):
        start = pl.multiple_of(block * width + pl.program_id(1) * LANES, LANES)
        out_ref[0, :, pl.ds(start, LANES)] = value.astype(BF16)


def attention(lengths, joint, grad_context=None):
    images, slots, width = joint.shape[0], joint.shape[1], joint.shape[2] // 3
    pairs = width // LANES
    block = (1, slots, LANES)
    specs = [pl.BlockSpec(block, functools.partial(lambda b, i, h, n: (i, 0, b + h), b * pairs)) for b in range(3)]
    plain = pl.BlockSpec(block, lambda i, h, n: (i, 0, h))
    back = grad_context is not None
    flops = 2 * images * pairs * 2 * slots * slots * LANES * (5 if back else 2)
    return pl.pallas_call(
        attend_back_kernel if back else attend_kernel,
        grid_spec=pltpu.PrefetchScalarGridSpec(
            num_scalar_prefetch=1,
            grid=(images, pairs),
            in_specs=specs + ([plain] if back else []),
            out_specs=pl.BlockSpec((1, slots, 3 * width), lambda i, h, n: (i, 0, 0)) if back else plain,
        ),
        out_shape=jax.ShapeDtypeStruct((images, slots, 3 * width if back else width), BF16),
        cost_estimate=pl.CostEstimate(
            flops=flops,
            bytes_accessed=images * slots * width * 2 * (7 if back else 4),
            transcendentals=images * pairs * 2 * slots * slots,
        ),
    )(lengths, joint, joint, joint, *([grad_context] if back else []))


def swap(value, axis):
    return lax.ppermute(value, axis, [(0, 1), (1, 0)])


def exchange(blocks, axis):
    return lax.all_to_all(blocks, axis, split_axis=0, concat_axis=0, tiled=True)


def after(value, *others):
    return lax.optimization_barrier((value,) + others)[0]


def my_place():
    return jnp.stack([lax.axis_index(n) for n in ("y", "x", "c")]).astype(jnp.int32)


class Split:
    def __init__(self, shard, by_rows):
        self.shard_rows, self.columns = shard
        self.by_rows = by_rows
        self.rows = self.shard_rows // 4 if by_rows else self.shard_rows // 2
        self.wide = self.columns if by_rows else self.columns // 2
        self.via_y = self.rows * 3 // 4


class Gather:
    def __init__(self, weight, by_rows=False):
        self.cut = Split(weight.shape, by_rows)
        self.weight = weight

    def over_z(self, *before):
        cut = self.cut
        x, c = lax.axis_index("x"), lax.axis_index("c")
        at = (c * 2 * cut.rows + x * cut.rows, 0) if cut.by_rows else (x * cut.rows, c * cut.wide)
        piece = lax.dynamic_slice(self.weight, at, (cut.rows, cut.wide))
        if before:
            piece = after(piece, *before)
        depth = lax.axis_size("z")
        self.z = exchange(jnp.broadcast_to(piece[None], (depth,) + piece.shape), "z")
        return self.z

    def over_plane(self, *before):
        start = after(self.z, *before) if before else self.z
        self.x, self.y = swap(start, "x"), swap(start, "y")
        return self.x, self.y

    def over_corner(self, *before):
        x = after(self.x, *before) if before else self.x
        cut = self.cut
        self.d = (swap(x[:, : cut.via_y], "y"), swap(self.y[:, cut.via_y :], "x"))
        return self.d

    def whole(self):
        cut = self.cut
        mine = (self.z, self.x, self.y) + self.d
        pieces = mine + tuple(swap(v, "c") for v in mine)
        depth = self.z.shape[0]
        return pl.pallas_call(
            functools.partial(place_kernel, cut),
            grid_spec=pltpu.PrefetchScalarGridSpec(
                num_scalar_prefetch=1,
                grid=(1,),
                in_specs=[pl.BlockSpec(memory_space=pl.ANY)] * len(pieces),
                out_specs=pl.BlockSpec(memory_space=pltpu.VMEM),
                scratch_shapes=[pltpu.SemaphoreType.DMA],
            ),
            out_shape=jax.ShapeDtypeStruct((2 * depth * cut.shard_rows, cut.columns), BF16),
            cost_estimate=pl.CostEstimate(
                flops=0, bytes_accessed=8 * depth * cut.shard_rows * cut.columns, transcendentals=0
            ),
        )(my_place(), *pieces)


def place_kernel(cut, place_ref, *refs):
    *pieces, out_ref, sem = refs
    y, x, c = place_ref[0], place_ref[1], place_ref[2]
    copies = []
    for core in range(2):
        at, far_y, far_x, far_1, far_2 = pieces[5 * core : 5 * core + 5]
        core_at = jnp.where(c == core, 0, 1)
        for z in range(at.shape[0]):
            for ref, other_y, other_x, off, rows in (
                (at, 0, 0, 0, cut.rows),
                (far_y, 0, 1, 0, cut.rows),
                (far_x, 1, 0, 0, cut.rows),
                (far_1, 1, 1, 0, cut.via_y),
                (far_2, 1, 1, cut.via_y, cut.rows - cut.via_y),
            ):
                yy = jnp.where(y == other_y, 0, 1)
                xx = jnp.where(x == other_x, 0, 1)
                start = (2 * z + yy) * cut.shard_rows + xx * cut.rows + off
                if cut.by_rows:
                    start = start + core_at * 2 * cut.rows
                rows_at = pl.ds(pl.multiple_of(start, 16), rows)
                if cut.by_rows:
                    target = out_ref.at[rows_at]
                else:
                    target = out_ref.at[rows_at, pl.ds(pl.multiple_of(core_at * cut.wide, 128), cut.wide)]
                copies.append(pltpu.make_async_copy(ref.at[z], target, sem))
    for copy in copies:
        copy.start()
    for copy in copies:
        copy.wait()


def parts_of(place_ref, by_y, rows, via_y, refs):
    y, x = place_ref[0], place_ref[1]
    near = jnp.where(y == 0, by_y[0], by_y[1]).astype(BF16)
    far = jnp.where(y == 0, by_y[1], by_y[0]).astype(BF16)
    own_ref, to_x_ref, to_y_ref, corner_1_ref, corner_2_ref = refs
    low, high = near[:, :rows], near[:, rows:]
    own_ref[...] = jnp.where(x == 0, low, high)
    to_x_ref[...] = jnp.where(x == 0, high, low)
    low, high = far[:, :rows], far[:, rows:]
    to_y_ref[...] = jnp.where(x == 0, low, high)
    corner = jnp.where(x == 0, high, low)
    corner_1_ref[...] = corner[:, :via_y]
    corner_2_ref[...] = corner[:, via_y:]


def grad_columns_kernel(cut, place_ref, a_ref, a_sib_ref, g_ref, g_sib_ref, *out_refs):
    total = contract(a_ref[...], g_ref[...], 0, 0) + contract(a_sib_ref[...], g_sib_ref[...], 0, 0)
    total = total.reshape(-1, 2, cut.shard_rows, total.shape[1])
    parts_of(place_ref, (total[:, 0], total[:, 1]), cut.rows, cut.via_y, out_refs)


def grad_rows_kernel(cut, place_ref, a0_ref, a1_ref, a_sib_ref, g_ref, g_sib_ref, *out_refs):
    half = 2 * cut.rows
    by_y = [
        (
            contract(ref[...], g_ref[...], 0, 0)
            + contract(a_sib_ref[:, yy * half : (yy + 1) * half], g_sib_ref[...], 0, 0)
        )[None]
        for yy, ref in enumerate((a0_ref, a1_ref))
    ]
    parts_of(place_ref, by_y, cut.rows, cut.via_y, out_refs)


def grad_parts(cut, depth, a, a_sib, g, g_sib, step=512):
    tokens = a.shape[0]
    all_rows = lambda n: pl.BlockSpec((tokens, n), lambda j, place: (0, 0))
    if cut.by_rows:
        half = 2 * cut.rows
        grid = (depth,)
        in_specs = [
            pl.BlockSpec((tokens, half), lambda j, place: (0, 4 * j + place[2])),
            pl.BlockSpec((tokens, half), lambda j, place: (0, 4 * j + 2 + place[2])),
            pl.BlockSpec((tokens, 2 * half), lambda j, place: (0, j)),
            all_rows(cut.wide),
            all_rows(cut.wide),
        ]
        out_spec = lambda rows: pl.BlockSpec((1, rows, cut.wide), lambda j, place: (j, 0, 0))
        operands, kernel = (a, a, a_sib, g, g_sib), grad_rows_kernel
    else:
        steps = cut.wide // step
        grid = (steps,)
        in_specs = [
            all_rows(a.shape[1]),
            all_rows(a.shape[1]),
            pl.BlockSpec((tokens, step), lambda j, place: (0, place[2] * steps + j)),
            pl.BlockSpec((tokens, step), lambda j, place: (0, j)),
        ]
        out_spec = lambda rows: pl.BlockSpec((depth, rows, step), lambda j, place: (0, 0, j))
        operands, kernel = (a, a_sib, g, g_sib), grad_columns_kernel
    sizes = (cut.rows,) * 3 + (cut.via_y, cut.rows - cut.via_y)
    total = 8 * depth * cut.rows * cut.wide
    return pl.pallas_call(
        functools.partial(kernel, cut),
        grid_spec=pltpu.PrefetchScalarGridSpec(
            num_scalar_prefetch=1,
            grid=grid,
            in_specs=in_specs,
            out_specs=[out_spec(n) for n in sizes],
        ),
        out_shape=[jax.ShapeDtypeStruct((depth, n, cut.wide), BF16) for n in sizes],
        compiler_params=pltpu.CompilerParams(vmem_limit_bytes=48 << 20),
        cost_estimate=pl.CostEstimate(
            flops=2 * total * tokens,
            bytes_accessed=2 * total + sum(2 * v.size for v in (a, g)),
            transcendentals=0,
        ),
    )(my_place(), *operands)


class Scatter:
    def __init__(self, cut, a, a_sib, g, g_sib):
        self.cut = cut
        depth = lax.axis_size("z")
        self.own, self.to_x, self.to_y, self.c1, self.c2 = grad_parts(cut, depth, a, a_sib, g, g_sib)

    def over_corner(self):
        self.e1, self.e2 = swap(self.c1, "y"), swap(self.c2, "x")
        return self.e1, self.e2

    def over_plane(self):
        n = self.cut.via_y
        add = lambda u, v: (u.astype(F32) + v.astype(F32)).astype(BF16)
        to_x = jnp.concatenate([add(self.to_x[:, :n], self.e1), self.to_x[:, n:]], axis=1)
        to_y = jnp.concatenate([self.to_y[:, :n], add(self.to_y[:, n:], self.e2)], axis=1)
        self.x, self.y = swap(to_x, "x"), swap(to_y, "y")
        return self.x, self.y

    def over_z(self):
        total = sum(v.astype(F32) for v in (self.own, self.x, self.y)).astype(BF16)
        self.z = exchange(total, "z")
        return self.z

    def whole(self):
        x, c = lax.axis_index("x"), lax.axis_index("c")
        mine = jnp.sum(self.z.astype(F32), axis=0).astype(BF16)
        theirs = swap(mine, "x")
        ours = jnp.concatenate(
            [jnp.where(x == 0, mine, theirs), jnp.where(x == 0, theirs, mine)], axis=0
        )
        theirs = swap(ours, "c")
        first, second = jnp.where(c == 0, ours, theirs), jnp.where(c == 0, theirs, ours)
        return jnp.concatenate([first, second], axis=0 if self.cut.by_rows else 1).astype(F32)


def for_sibling(value, groups):
    half = value.shape[1] // groups // 2
    first = lax.axis_index("c") == 0
    cuts = [value[:, i * half : (i + 1) * half] for i in range(2 * groups)]
    picked = [jnp.where(first, cuts[2 * i + 1], cuts[2 * i]) for i in range(groups)]
    return swap(jnp.concatenate(picked, axis=1), "c")


def gather_vectors(packed):
    depth = lax.axis_size("z")
    own_y = exchange(jnp.broadcast_to(packed[None], (depth,) + packed.shape), "z")
    other_y = swap(own_y, "y")
    y = lax.axis_index("y")
    rows = [jnp.where(y == 0, own_y, other_y), jnp.where(y == 0, other_y, own_y)]
    return jnp.stack(rows, axis=1).reshape(2 * depth, -1)


def scatter_vectors(packed):
    y = lax.axis_index("y")
    packed = packed + swap(packed, "c")
    packed = packed + swap(packed, "x")
    packed = packed.reshape(lax.axis_size("z"), 2, -1)
    row = lambda yy: lax.dynamic_slice_in_dim(packed, yy, 1, 1)[:, 0]
    packed = row(y) + swap(row(1 - y), "y")
    return jnp.sum(exchange(packed, "z"), axis=0)


class Plain:
    def __init__(self, a, g):
        self.grad = contract(a, g, 0, 0).astype(BF16)

    def whole(self):
        grad = lax.psum_scatter(self.grad, FSDP, scatter_dimension=0, tiled=True)
        return lax.psum(grad, SEQ).astype(F32)


def gather_all(qkv, out, up, down):
    qkv, out, up, down = Gather(qkv), Gather(out), Gather(up), Gather(down, by_rows=True)
    first = qkv.over_z()
    second = out.over_z(first)
    plane = qkv.over_plane()
    third = up.over_z(second, *plane)
    corner = qkv.over_corner()
    out_plane = out.over_plane(*plane)
    down.over_z(third, *corner, *out_plane)
    up_plane = up.over_plane(*corner, *out_plane)
    out.over_corner()
    down.over_plane(*up_plane)
    up_corner = up.over_corner()
    down.over_corner(*up_corner)
    return [w.whole() for w in (qkv, out, up, down)]


def shards(
    tokens,
    lengths,
    attn_gain,
    attn_shift,
    attn_weight,
    attn_bias,
    out_weight,
    out_bias,
    mlp_gain,
    mlp_shift,
    up_weight,
    up_bias,
    down_weight,
    down_bias,
    cotangent,
):
    width = tokens.shape[2]
    members = lax.axis_size(SEQ)
    staged = lax.axis_size("z") <= 8 and attn_weight.shape[0] % 128 == 0
    images = tokens.shape[0] // members
    slots = tokens.shape[1] * members
    rows = images * slots

    small = (attn_gain, attn_shift, attn_bias, out_bias, mlp_gain, mlp_shift, up_bias, down_bias)
    sizes = [v.shape[0] for v in small]
    small_all = gather_vectors(jnp.concatenate(small)).astype(F32)
    cuts = [sum(sizes[:i]) for i in range(len(sizes))]
    gain_a, shift_a, bias_qv, bias_out, gain_b, shift_b, bias_up, bias_down = (
        small_all[:, c : c + n].reshape(-1) for c, n in zip(cuts, sizes)
    )
    matrices = (attn_weight, out_weight, up_weight, down_weight)
    if staged:
        qkv_full, out_full, up_full, down_full = gather_all(*matrices)
    else:
        qkv_full, out_full, up_full, down_full = (
            lax.all_gather(w, FSDP, axis=0, tiled=True) for w in matrices
        )

    lens = lax.dynamic_slice_in_dim(lengths, lax.axis_index(SEQ) * images, images, 0)
    valid = jnp.arange(slots, dtype=jnp.int32)[None, :] < lens[:, None]
    valid = valid.reshape(rows, 1)
    few = tokens.shape[1]

    def by_image(value):
        value = exchange(value, SEQ).reshape(members, images, few, width)
        return value.transpose(1, 0, 2, 3).reshape(rows, width)

    def by_slot(value):
        value = value.reshape(images, members, few, width).transpose(1, 0, 2, 3)
        return exchange(value.reshape(members * images, few, width), SEQ)

    tokens = by_image(tokens)
    wide = tokens.astype(F32)
    cot = by_image(after(cotangent, tokens))

    normal_a, inv_a = layer_stats(wide)
    normed_a = (normal_a * gain_a + shift_a).astype(BF16)
    bias_joint = jnp.concatenate([bias_qv[:width], jnp.zeros((width,), F32), bias_qv[width:]])
    joint = (contract(normed_a, qkv_full, 1, 0) + bias_joint).astype(BF16)
    joint = joint.reshape(images, slots, 3 * width)
    context = attention(lens, joint).reshape(rows, width)
    middle = wide + (contract(context, out_full, 1, 0) + bias_out)
    normal_b, inv_b = layer_stats(middle)
    normed_b = (normal_b * gain_b + shift_b).astype(BF16)
    pre = contract(normed_b, up_full, 1, 0) + bias_up
    cumul = 0.5 * (1.0 + lax.erf(pre * 0.7071067811865476))
    hidden = (pre * cumul).astype(BF16)
    slope = (cumul + pre * jnp.exp(-0.5 * pre * pre) * 0.3989422804014327).astype(BF16)
    result = middle + contract(hidden, down_full, 1, 0) + bias_down
    layer_out = jnp.where(valid, result, 0.0).astype(BF16)
    layer_out = by_slot(layer_out)

    grad_out = jnp.where(valid, cot, jnp.zeros_like(cot))
    grad_out_wide = grad_out.astype(F32)
    shard_count = lax.axis_size(FSDP)

    def scatter(weight, a, g, by_rows=False):
        if not staged:
            return Plain(a, g)
        cut = Split(weight.shape, by_rows)
        if by_rows:
            return Scatter(cut, a, for_sibling(a, shard_count), g, swap(g, "c"))
        return Scatter(cut, a, swap(a, "c"), g, for_sibling(g, 1))

    g_bias_down = jnp.sum(grad_out_wide, axis=0)
    s_down = scatter(down_weight, hidden, grad_out, by_rows=True)
    grad_pre = (contract(grad_out, down_full, 1, 1) * slope.astype(F32)).astype(BF16)
    if staged:
        grad_pre = after(grad_pre, *s_down.over_corner())
    g_bias_up = jnp.sum(grad_pre.astype(F32), axis=0)
    s_up = scatter(up_weight, normed_b, grad_pre)
    grad_nb = contract(grad_pre, up_full, 1, 1)
    if staged:
        grad_nb = after(grad_nb, s_up.own)
    g_gain_b = jnp.sum(grad_nb * normal_b, axis=0)
    g_shift_b = jnp.sum(grad_nb, axis=0)
    grad_middle = grad_out_wide + norm_back(grad_nb, gain_b, normal_b, inv_b)
    grad_branch = grad_middle.astype(BF16)
    g_bias_out = jnp.sum(grad_branch.astype(F32), axis=0)
    s_out = scatter(out_weight, context, grad_branch)
    grad_context = contract(grad_branch, out_full, 1, 1).astype(BF16)
    if staged:
        s_up.over_corner()
        s_out.over_corner()
        grad_context = after(grad_context, *s_down.over_plane(), s_out.own)
    grad_joint = attention(lens, joint, grad_context.reshape(images, slots, width))
    grad_joint = grad_joint.reshape(rows, 3 * width)
    if staged:
        s_down.over_z()
        s_up.over_plane()
        s_out.over_plane()
        grad_joint = after(grad_joint, s_up.e1, s_up.e2, s_out.e1, s_out.e2)
    joint_sums = jnp.sum(grad_joint.astype(F32), axis=0)
    g_bias_qv = jnp.concatenate([joint_sums[:width], joint_sums[2 * width :]])
    s_qkv = scatter(attn_weight, normed_a, grad_joint)
    grad_na = contract(grad_joint, qkv_full, 1, 1)
    if staged:
        s_qkv.over_corner()
        grad_na = after(grad_na, s_up.x, s_up.y, s_out.x, s_out.y, s_down.z, s_qkv.own)
    g_gain_a = jnp.sum(grad_na * normal_a, axis=0)
    g_shift_a = jnp.sum(grad_na, axis=0)
    input_grad = (grad_middle + norm_back(grad_na, gain_a, normal_a, inv_a)).astype(BF16)
    input_grad = by_slot(input_grad)
    if staged:
        s_up.over_z()
        s_out.over_z()
        s_qkv.over_plane()
        s_qkv.over_z()
    g_down, g_up, g_out, g_qkv = (v.whole() for v in (s_down, s_up, s_out, s_qkv))

    small_grads = (g_gain_a, g_shift_a, g_bias_qv, g_bias_out, g_gain_b, g_shift_b, g_bias_up, g_bias_down)
    packed = jnp.concatenate([v.reshape(shard_count, -1) for v in small_grads], axis=1)
    packed = scatter_vectors(packed)
    (g_gain_a, g_shift_a, g_bias_qv, g_bias_out, g_gain_b, g_shift_b, g_bias_up, g_bias_down) = (
        packed[c : c + n] for c, n in zip(cuts, sizes)
    )
    return (
        layer_out,
        input_grad,
        g_gain_a,
        g_shift_a,
        g_qkv,
        g_bias_qv,
        g_out,
        g_bias_out,
        g_gain_b,
        g_shift_b,
        g_up,
        g_bias_up,
        g_down,
        g_bias_down,
    )


def solution(mesh):
    shard_count, members = mesh.devices.shape
    fine = Mesh(mesh.devices.reshape(shard_count // 2, 2, members // 2, 2), FSDP + SEQ)
    rows, vector, matrix = P(FSDP, SEQ, None), P(FSDP), P(FSDP, None)
    weights = (vector, vector, matrix, vector, matrix, vector, vector, vector, matrix, vector, matrix, vector)
    return jax.shard_map(
        shards,
        mesh=fine,
        in_specs=(rows, vector) + weights + (rows,),
        out_specs=(rows, rows) + weights,
        check_vma=False,
    )
```

```python
import functools

import jax
import jax.numpy as jnp
from jax import lax
from jax.experimental import pallas as pl
from jax.experimental.pallas import tpu as pltpu
from jax.sharding import Mesh
from jax.sharding import PartitionSpec as P

HEAD_DIM = 64
LANES = 128
GROUPS = 2
EPSILON = 1e-06
BF16 = jnp.bfloat16
F32 = jnp.float32
FSDP, SEQ = ("z", "y"), ("x", "c")


def cost(microseconds, nbytes=0):
    return pl.CostEstimate(flops=int(microseconds * 1.1e9), bytes_accessed=nbytes, transcendentals=0)


def norm_back(grad_norm, gain, normal, inv_std):
    scaled = grad_norm * gain
    return inv_std * (
        scaled
        - jnp.mean(scaled, axis=-1, keepdims=True)
        - normal * jnp.mean(scaled * normal, axis=-1, keepdims=True)
    )


def contract(a, b, ca, cb):
    return lax.dot_general(a, b, (((ca,), (cb,)), ((), ())), preferred_element_type=F32)


def head_probs(q, k, head, lane, key_ok):
    q_own = jnp.where(lane == head, q, jnp.zeros_like(q))
    scores = contract(q_own, k, 1, 1) * HEAD_DIM ** (-0.5)
    scores = jnp.where(key_ok, scores, -1000000000.0)
    top = jnp.max(scores, axis=-1, keepdims=True)
    exps = jnp.exp(scores - top)
    return exps * (1.0 / jnp.sum(exps, axis=-1, keepdims=True))


def masks(key_valid, slots):
    lane = lax.broadcasted_iota(jnp.int32, (slots, LANES), 1) // HEAD_DIM
    return lane, jnp.broadcast_to(key_valid, (slots, slots)) > 0.5


def attend_kernel(mask_ref, q_ref, k_ref, v_ref, out_ref):
    q, k, v = q_ref[0], k_ref[0], v_ref[0]
    lane, key_ok = masks(mask_ref[0], q.shape[0])
    context = jnp.zeros(q.shape, F32)
    for head in range(LANES // HEAD_DIM):
        probs = head_probs(q, k, head, lane, key_ok).astype(BF16)
        context = jnp.where(lane == head, contract(probs, v, 1, 0), context)
    out_ref[0] = context.astype(BF16)


def attend_back_kernel(mask_ref, q_ref, k_ref, v_ref, g_ref, out_ref):
    q, k, v, g = q_ref[0], k_ref[0], v_ref[0], g_ref[0]
    lane, key_ok = masks(mask_ref[0], q.shape[0])
    dq, dk, dv = (jnp.zeros(q.shape, F32) for _ in range(3))
    for head in range(LANES // HEAD_DIM):
        own = lane == head
        probs = head_probs(q, k, head, lane, key_ok)
        g_own = jnp.where(own, g, jnp.zeros_like(g))
        grad_probs = contract(g_own, v, 1, 1)
        inner = jnp.sum(grad_probs * probs, axis=-1, keepdims=True)
        grad_scores = (probs * (grad_probs - inner) * HEAD_DIM ** (-0.5)).astype(BF16)
        dq = jnp.where(own, contract(grad_scores, k, 1, 0), dq)
        dk = jnp.where(own, contract(grad_scores, q, 0, 0), dk)
        dv = jnp.where(own, contract(probs.astype(BF16), g, 0, 0), dv)
    width = out_ref.shape[2] // 3
    for block, value in enumerate((dq, dk, dv)):
        start = pl.multiple_of(block * width + pl.program_id(1) * LANES, LANES)
        out_ref[0, :, pl.ds(start, LANES)] = value.astype(BF16)


def attention(key_valid, joint, grad_context=None, group=0):
    images, slots, width = joint.shape[0], joint.shape[1], joint.shape[2] // 3
    in_group = width // LANES // GROUPS
    back = grad_context is not None
    pairs = in_group if back else in_group * GROUPS
    block = (1, slots, LANES)

    def spec(part):
        def index(i, h):
            h = h + group * in_group
            return i, 0, (h // in_group * 3 + part) * in_group + h % in_group

        return pl.BlockSpec(block, index)

    plain = pl.BlockSpec(block, lambda i, h: (i, 0, h + group * in_group))
    mask = pl.BlockSpec((1, 1, slots), lambda i, h: (i, 0, 0))
    whole = pl.BlockSpec((1, slots, 3 * pairs * LANES), lambda i, h: (i, 0, 0))
    columns = (3 if back else 1) * pairs * LANES
    return pl.pallas_call(
        attend_back_kernel if back else attend_kernel,
        grid=(images, pairs),
        in_specs=[mask] + [spec(part) for part in range(3)] + ([plain] if back else []),
        out_specs=whole if back else plain,
        out_shape=jax.ShapeDtypeStruct((images, slots, columns), BF16),
        cost_estimate=cost((1.9 if back else 1.2) * images * pairs),
    )(key_valid, joint, joint, joint, *([grad_context] if back else []))


STEP = 512


def stats(values):
    center = values - jnp.mean(values, axis=-1, keepdims=True)
    inv_std = lax.rsqrt(jnp.mean(center * center, axis=-1, keepdims=True) + EPSILON)
    return center * inv_std, inv_std


def column_sums(values):
    return jnp.sum(values, axis=0, keepdims=True)


def whole_spec(array):
    return pl.BlockSpec(array.shape, lambda j: (0,) * len(array.shape))


def columns_spec(rows, step=STEP):
    return pl.BlockSpec((rows, step), lambda j: (0, j))


def stepped(kernel, steps, in_specs, operands, out_specs, out_shape, scratch, microseconds):
    return pl.pallas_call(
        kernel,
        grid=(steps,),
        in_specs=in_specs,
        out_specs=out_specs,
        out_shape=out_shape,
        scratch_shapes=scratch,
        compiler_params=pltpu.CompilerParams(vmem_limit_bytes=54 << 20),
        cost_estimate=cost(microseconds),
    )(*operands)


def project_kernel(tokens_ref, gain_ref, shift_ref, weight_ref, bias_ref, normed_ref, joint_ref):
    j = pl.program_id(0)

    @pl.when(j == 0)
    def _():
        normal, _ = stats(tokens_ref[...].astype(F32))
        normed_ref[...] = (normal * gain_ref[...] + shift_ref[...]).astype(BF16)

    bias = jnp.where(j % 3 == 1, 0.0, bias_ref[...])
    joint_ref[...] = (contract(normed_ref[...], weight_ref[...], 1, 0) + bias).astype(BF16)


def project(tokens, gain, shift, weight, bias_qv):
    rows, width = tokens.shape
    assert width // GROUPS == STEP
    bias_spec = pl.BlockSpec((1, STEP), lambda j: (0, j // 3 + jnp.where(j % 3 == 2, GROUPS, 0)))
    return stepped(
        project_kernel,
        3 * width // STEP,
        [whole_spec(tokens), whole_spec(gain), whole_spec(shift), columns_spec(width), bias_spec],
        (tokens, gain, shift, weight, bias_qv),
        [whole_spec(tokens), columns_spec(rows)],
        [jax.ShapeDtypeStruct((rows, width), BF16), jax.ShapeDtypeStruct((rows, 3 * width), BF16)],
        [],
        11,
    )


def expand_kernel(
    tokens_ref, context_ref, out_ref, bias_out_ref, gain_ref, shift_ref, up_ref, bias_ref,
    middle_ref, normed_ref, hidden_ref, slope_ref,
):
    @pl.when(pl.program_id(0) == 0)
    def _():
        branch = contract(context_ref[...], out_ref[...], 1, 0) + bias_out_ref[...]
        middle = tokens_ref[...].astype(F32) + branch
        middle_ref[...] = middle
        normal, _ = stats(middle)
        normed_ref[...] = (normal * gain_ref[...] + shift_ref[...]).astype(BF16)

    pre = contract(normed_ref[...], up_ref[...], 1, 0) + bias_ref[...]
    cumul = 0.5 * (1.0 + lax.erf(pre * 0.7071067811865476))
    hidden_ref[...] = (pre * cumul).astype(BF16)
    slope = cumul + pre * (jnp.exp(-0.5 * pre * pre) * 0.3989422804014327)
    slope_ref[...] = slope.astype(BF16)


def expand(tokens, context, out_full, bias_out, gain, shift, up_full, bias_up):
    rows, width = tokens.shape
    hidden = up_full.shape[1]
    return stepped(
        expand_kernel,
        hidden // STEP,
        [whole_spec(v) for v in (tokens, context, out_full, bias_out, gain, shift)]
        + [columns_spec(width), columns_spec(1)],
        (tokens, context, out_full, bias_out, gain, shift, up_full, bias_up),
        [whole_spec(tokens)] * 2 + [columns_spec(rows)] * 2,
        [jax.ShapeDtypeStruct((rows, width), F32), jax.ShapeDtypeStruct((rows, width), BF16)]
        + [jax.ShapeDtypeStruct((rows, hidden), BF16)] * 2,
        [],
        20,
    )


def finish_kernel(hidden_ref, down_ref, middle_ref, bias_ref, valid_ref, result_ref, total_ref):
    j = pl.program_id(0)
    part = contract(hidden_ref[...], down_ref[...], 1, 0)

    @pl.when(j == 0)
    def _():
        total_ref[...] = middle_ref[...] + bias_ref[...] + part

    @pl.when(j > 0)
    def _():
        total_ref[...] += part

    @pl.when(j == pl.num_programs(0) - 1)
    def _():
        result_ref[...] = jnp.where(valid_ref[...] > 0.5, total_ref[...], 0.0).astype(BF16)


def finish(hidden, down_full, middle, bias_down, valid):
    rows, width = middle.shape
    return stepped(
        finish_kernel,
        hidden.shape[1] // STEP,
        [columns_spec(rows), pl.BlockSpec((STEP, width), lambda j: (j, 0))]
        + [whole_spec(v) for v in (middle, bias_down, valid)],
        (hidden, down_full, middle, bias_down, valid),
        whole_spec(middle),
        jax.ShapeDtypeStruct((rows, width), BF16),
        [pltpu.VMEM((rows, width), F32)],
        9,
    )


def back_kernel(
    grad_ref, down_ref, slope_ref, up_ref, middle_ref, gain_ref, out_ref,
    pre_ref, bias_up_ref, grad_middle_ref, branch_ref, context_ref, sums_ref, total_ref,
):
    j = pl.program_id(0)
    pre = (contract(grad_ref[...], down_ref[...], 1, 1) * slope_ref[...].astype(F32)).astype(BF16)
    pre_ref[...] = pre
    bias_up_ref[...] = column_sums(pre.astype(F32))
    part = contract(pre, up_ref[...], 1, 1)

    @pl.when(j == 0)
    def _():
        total_ref[...] = part

    @pl.when(j > 0)
    def _():
        total_ref[...] += part

    @pl.when(j == pl.num_programs(0) - 1)
    def _():
        normal, inv_std = stats(middle_ref[...])
        total = total_ref[...]
        grad_middle = grad_ref[...].astype(F32) + norm_back(total, gain_ref[...], normal, inv_std)
        grad_middle_ref[...] = grad_middle
        branch = grad_middle.astype(BF16)
        branch_ref[...] = branch
        context_ref[...] = contract(branch, out_ref[...], 1, 1).astype(BF16)
        sums_ref[0:1] = column_sums(total * normal)
        sums_ref[1:2] = column_sums(total)
        sums_ref[2:3] = column_sums(branch.astype(F32))


def back(grad_out, down_full, slope, up_full, middle, gain, out_full):
    rows, width = middle.shape
    hidden = slope.shape[1]
    return stepped(
        back_kernel,
        hidden // STEP,
        [
            whole_spec(grad_out),
            pl.BlockSpec((STEP, width), lambda j: (j, 0)),
            columns_spec(rows),
            columns_spec(width),
            whole_spec(middle),
            whole_spec(gain),
            whole_spec(out_full),
        ],
        (grad_out, down_full, slope, up_full, middle, gain, out_full),
        [columns_spec(rows), columns_spec(1)]
        + [whole_spec(middle)] * 3
        + [pl.BlockSpec((8, width), lambda j: (0, 0))],
        [
            jax.ShapeDtypeStruct((rows, hidden), BF16),
            jax.ShapeDtypeStruct((1, hidden), F32),
            jax.ShapeDtypeStruct((rows, width), F32),
            jax.ShapeDtypeStruct((rows, width), BF16),
            jax.ShapeDtypeStruct((rows, width), BF16),
            jax.ShapeDtypeStruct((8, width), F32),
        ],
        [pltpu.VMEM((rows, width), F32)],
        20,
    )


def input_kernel(joint_0_ref, joint_1_ref, weight_ref, tokens_ref, gain_ref, grad_middle_ref, input_ref, bias_ref, sums_ref, total_ref):
    j = pl.program_id(0)
    first = jnp.broadcast_to(j < 3, joint_0_ref.shape)
    joint = jnp.where(first, joint_0_ref[...], joint_1_ref[...])
    bias_ref[...] = column_sums(joint.astype(F32))
    part = contract(joint, weight_ref[...], 1, 1)

    @pl.when(j == 0)
    def _():
        total_ref[...] = part

    @pl.when(j > 0)
    def _():
        total_ref[...] += part

    @pl.when(j == pl.num_programs(0) - 1)
    def _():
        normal, inv_std = stats(tokens_ref[...].astype(F32))
        total = total_ref[...]
        grad = grad_middle_ref[...] + norm_back(total, gain_ref[...], normal, inv_std)
        input_ref[...] = grad.astype(BF16)
        sums_ref[0:1] = column_sums(total * normal)
        sums_ref[1:2] = column_sums(total)


def back_input(joint_0, joint_1, weight, tokens, gain, grad_middle):
    rows, width = tokens.shape
    return stepped(
        input_kernel,
        3 * width // STEP,
        [
            pl.BlockSpec((rows, STEP), lambda j: (0, jnp.minimum(j, 2))),
            pl.BlockSpec((rows, STEP), lambda j: (0, jnp.maximum(j - 3, 0))),
            columns_spec(width),
            whole_spec(tokens),
            whole_spec(gain),
            whole_spec(grad_middle),
        ],
        (joint_0, joint_1, weight, tokens, gain, grad_middle),
        [whole_spec(tokens), columns_spec(1), pl.BlockSpec((8, width), lambda j: (0, 0))],
        [
            jax.ShapeDtypeStruct((rows, width), BF16),
            jax.ShapeDtypeStruct((1, 3 * width), F32),
            jax.ShapeDtypeStruct((8, width), F32),
        ],
        [pltpu.VMEM((rows, width), F32)],
        14,
    )


def grouped(value):
    width = value.shape[-1] // 3
    part = width // GROUPS
    return jnp.concatenate(
        [value[..., t * width + g * part :][..., :part] for g in range(GROUPS) for t in range(3)], axis=-1
    )


def ungrouped(values):
    part = values[0].shape[-1] // 3
    return jnp.concatenate(
        [v[..., t * part : (t + 1) * part] for t in range(3) for v in values], axis=-1
    )


def swap(value, axis):
    return lax.ppermute(value, axis, [(0, 1), (1, 0)])


def send(value, axis, step):
    return lax.ppermute(value, axis, [(i, i ^ step) for i in range(lax.axis_size(axis))])


def pick(blocks, index):
    return lax.dynamic_index_in_dim(blocks, index, 0, keepdims=False)


def tie(*values):
    return lax.optimization_barrier(values)


def after(value, *others):
    return lax.optimization_barrier((value,) + others)[0]


def my_place():
    return jnp.stack([lax.axis_index(n) for n in ("y", "x", "c")]).astype(jnp.int32)


class Split:
    def __init__(self, shard, by_rows=False, columns=None):
        self.shard_rows, self.columns = shard[0], columns or shard[1]
        self.by_rows = by_rows
        self.rows = self.shard_rows // 4 if by_rows else self.shard_rows // 2
        self.wide = self.columns if by_rows else self.columns // 2

def exchange(blocks, axis):
    return lax.all_to_all(blocks, axis, split_axis=0, concat_axis=0, tiled=True)


def pieces_kernel(depth, rows, place_ref, qkv_ref, out_ref, up_ref, down_ref, *refs):
    *vector_refs, first_ref, second_ref, third_ref = refs
    x, c = place_ref[1], place_ref[2]
    at = pl.ds(pl.multiple_of(x * rows, rows), rows)

    def put(ref, lane, value):
        for z in range(depth):
            ref[z, : value.shape[0], lane : lane + value.shape[1]] = value
        return lane + value.shape[1]

    def columns(ref, start, count):
        return ref[at, pl.ds(pl.multiple_of(start, LANES), count)]

    width = out_ref.shape[1]
    part = width // 2
    lane = 0
    for t in range(3):
        lane = put(first_ref, lane, columns(qkv_ref, t * width + c * part, part))
    lane = put(first_ref, lane, columns(out_ref, c * part, part))
    packed = jnp.concatenate([ref[...] for ref in vector_refs], axis=0)
    padding = jnp.zeros((rows - packed.shape[0], LANES), packed.dtype)
    put(first_ref, lane, jnp.concatenate([packed, padding], axis=0))
    half = up_ref.shape[1] // 2
    put(second_ref, 0, columns(up_ref, c * half, half))
    blocks = down_ref.shape[0] // 4 // rows
    lane = 0
    for block in range(blocks):
        start = ((2 * c + x) * blocks + block) * rows
        lane = put(third_ref, lane, down_ref[pl.ds(pl.multiple_of(start, rows), rows), :])


def pieces(qkv, out, up, down, vectors):
    depth, rows = lax.axis_size("z"), qkv.shape[0] // 2
    vectors = [v.reshape(-1, LANES) for v in vectors]
    width = out.shape[1]
    wide = (2 * width + LANES, up.shape[1] // 2, down.shape[0] // 4 // rows * width)
    vmem = pl.BlockSpec(memory_space=pltpu.VMEM)
    return pl.pallas_call(
        functools.partial(pieces_kernel, depth, rows),
        in_specs=[pl.BlockSpec(memory_space=pltpu.SMEM)] + [vmem] * (4 + len(vectors)),
        out_specs=[vmem] * 3,
        out_shape=[jax.ShapeDtypeStruct((depth, rows, n), BF16) for n in wide],
        cost_estimate=cost(3),
    )(my_place(), qkv, out, up, down, *vectors)


def whole_weights(cuts, mine, others):
    pieces = tuple(mine) + tuple(others)
    shards = 2 * pieces[0].shape[0]
    return pl.pallas_call(
        functools.partial(place_kernel, cuts),
        grid_spec=pltpu.PrefetchScalarGridSpec(
            num_scalar_prefetch=1,
            grid=(1,),
            in_specs=[pl.BlockSpec(memory_space=pl.ANY)] * len(pieces),
            out_specs=[pl.BlockSpec(memory_space=pltpu.VMEM)] * len(cuts),
            scratch_shapes=[pltpu.SemaphoreType.DMA],
        ),
        out_shape=[jax.ShapeDtypeStruct((shards * cut.shard_rows, cut.columns), BF16) for cut in cuts],
        cost_estimate=cost(sum(shards * cut.shard_rows * cut.columns for cut in cuts) * 1.8e-6),
    )(my_place(), *pieces)


def my_place():
    return jnp.stack([lax.axis_index(n) for n in ("y", "x", "c")]).astype(jnp.int32)


def place_kernel(cuts, place_ref, *refs):
    pieces, out_refs, sem = refs[:8], refs[8:-1], refs[-1]
    y, x, c = place_ref[0], place_ref[1], place_ref[2]
    rows = pieces[0].shape[1]
    copies = []
    for core in range(2):
        core_at = jnp.where(c == core, 0, 1)
        for i, ref in enumerate(pieces[4 * core : 4 * core + 4]):
            yy = jnp.where(y == i // 2, 0, 1)
            xx = jnp.where(x == i % 2, 0, 1)
            for z in range(ref.shape[0]):
                lane = 0
                for cut, out_ref in zip(cuts, out_refs):
                    start = (2 * z + yy) * cut.shard_rows + xx * cut.rows
                    if cut.by_rows:
                        start = start + core_at * 2 * cut.rows
                    for block in range(cut.rows // rows):
                        target = out_ref.at[pl.ds(pl.multiple_of(start + block * rows, 16), rows)]
                        if not cut.by_rows:
                            columns = pl.ds(pl.multiple_of(core_at * cut.wide, 128), cut.wide)
                            target = target.at[:, columns]
                        source = ref.at[z, :, pl.ds(lane, cut.wide)]
                        copies.append(pltpu.make_async_copy(source, target, sem))
                        lane += cut.wide
    for copy in copies:
        copy.start()
    for copy in copies:
        copy.wait()


def part_refs(x, near, far, rows, refs, at):
    own_ref, to_x_ref, to_y_ref, corner_ref = refs
    low, high = near[:rows], near[rows:]
    own_ref[at] = jnp.where(x == 0, low, high)
    to_x_ref[at] = jnp.where(x == 0, high, low)
    low, high = far[:rows], far[rows:]
    to_y_ref[at] = jnp.where(x == 0, low, high)
    corner_ref[at] = jnp.where(x == 0, high, low)


def grad_columns_kernel(ends, cut, place_ref, *refs):
    y, x = place_ref[0], place_ref[1]
    out_refs = refs[-4:]

    def one(a_ref, a_sib_ref, g_ref, g_sib_ref):
        total = contract(a_ref[...], g_ref[...], 0, 0) + contract(a_sib_ref[...], g_sib_ref[...], 0, 0)
        total = total.reshape(-1, 2, cut.shard_rows, total.shape[1])
        for z in range(total.shape[0]):
            near = jnp.where(y == 0, total[z, 0], total[z, 1]).astype(BF16)
            far = jnp.where(y == 0, total[z, 1], total[z, 0]).astype(BF16)
            part_refs(x, near, far, cut.rows, out_refs, z)

    if len(ends) == 1:
        one(*refs[:4])
        return
    j = pl.program_id(0)
    for i, end in enumerate(ends):
        inside = j < end if i == 0 else (j >= ends[i - 1]) & (j < end)
        pl.when(inside)(functools.partial(one, *refs[4 * i : 4 * i + 4]))


def grad_rows_kernel(cut, place_ref, a0_ref, a1_ref, a0_sib_ref, a1_sib_ref, g_ref, g_sib_ref, *out_refs):
    y, x = place_ref[0], place_ref[1]
    by_y = [
        contract(ref[...], g_ref[...], 0, 0)
        + contract(sib_ref[...], g_sib_ref[...], 0, 0)
        for ref, sib_ref in ((a0_ref, a0_sib_ref), (a1_ref, a1_sib_ref))
    ]
    near = jnp.where(y == 0, by_y[0], by_y[1]).astype(BF16)
    far = jnp.where(y == 0, by_y[1], by_y[0]).astype(BF16)
    part_refs(x, near, far, cut.rows, out_refs, 0)


def grad_parts(jobs, cut, depth, step=512):
    tokens = jobs[0][0].shape[0]
    specs, operands, ends = [], [], []
    if cut.by_rows:
        ((a, a_sib, g, g_sib),) = jobs
        half = 2 * cut.rows
        every = pl.BlockSpec((tokens, cut.wide), lambda j, place: (0, 0))
        specs = [
            pl.BlockSpec((tokens, half), lambda j, place: (0, 4 * j + place[2])),
            pl.BlockSpec((tokens, half), lambda j, place: (0, 4 * j + 2 + place[2])),
            pl.BlockSpec((tokens, half), lambda j, place: (0, 4 * j + place[2])),
            pl.BlockSpec((tokens, half), lambda j, place: (0, 4 * j + 2 + place[2])),
            every,
            every,
        ]
        operands, kernel, grid, wide = [a, a, a_sib, a_sib, g, g_sib], functools.partial(grad_rows_kernel, cut), depth, cut.wide
        out_spec = lambda n: pl.BlockSpec((1, n, wide), lambda j, place: (j, 0, 0))
    else:
        grid = 0
        for a, a_sib, g, g_sib in jobs:
            steps = g.shape[1] // 2 // step
            every = pl.BlockSpec((tokens, a.shape[1]), lambda j, place: (0, 0))
            at = lambda j, first=grid, steps=steps: jnp.clip(j - first, 0, steps - 1)
            specs += [
                every,
                every,
                pl.BlockSpec((tokens, step), lambda j, place, at=at, steps=steps: (0, place[2] * steps + at(j))),
                pl.BlockSpec((tokens, step), lambda j, place, at=at, steps=steps: (0, place[2] * steps + at(j))),
            ]
            operands += [a, a_sib, g, g_sib]
            grid += steps
            ends.append(grid)
        kernel, wide = functools.partial(grad_columns_kernel, ends, cut), grid * step
        out_spec = lambda n: pl.BlockSpec((depth, n, step), lambda j, place: (0, 0, j))
    total = 8 * depth * cut.rows * wide
    return pl.pallas_call(
        kernel,
        grid_spec=pltpu.PrefetchScalarGridSpec(
            num_scalar_prefetch=1,
            grid=(grid,),
            in_specs=specs,
            out_specs=[out_spec(cut.rows)] * 4,
        ),
        out_shape=[jax.ShapeDtypeStruct((depth, cut.rows, wide), BF16)] * 4,
        compiler_params=pltpu.CompilerParams(vmem_limit_bytes=52 << 20),
        cost_estimate=cost(total * 2.8e-6),
    )(my_place(), *operands)


def add(one, other):
    return (one.astype(F32) + other.astype(F32)).astype(BF16)


def grad_z(parts, from_x, from_y):
    return exchange(sum(v.astype(F32) for v in (parts[0], from_x, from_y)).astype(BF16), "z")


def grad_x(blocks):
    mine = jnp.sum(blocks.astype(F32), axis=0).astype(BF16)
    return in_order(lax.axis_index("x"), mine, swap(mine, "x"), 0)


def grad_core(ours, by_rows=False):
    return in_order(lax.axis_index("c"), ours, swap(ours, "c"), 0 if by_rows else 1)


def in_order(index, mine, theirs, axis):
    first, second = jnp.where(index == 0, mine, theirs), jnp.where(index == 0, theirs, mine)
    return jnp.concatenate([first, second], axis=axis)


def order_vectors(own_y, other_y):
    y = lax.axis_index("y")
    rows = [jnp.where(y == 0, own_y, other_y), jnp.where(y == 0, other_y, own_y)]
    return jnp.stack(rows, axis=1).reshape(2 * own_y.shape[0], -1)


def over_pairs(packed):
    y = lax.axis_index("y")
    packed = packed + swap(packed, "c")
    packed = packed + swap(packed, "x")
    packed = packed.reshape(lax.axis_size("z"), 2, -1)
    row = lambda yy: lax.dynamic_index_in_dim(packed, yy, 1, keepdims=False)
    return row(y) + swap(row(1 - y), "y")


def over_line(packed):
    z = lax.axis_index("z")
    return pick(packed, z) + sum(send(pick(packed, z ^ k), "z", k) for k in range(1, lax.axis_size("z")))


def scatter_plain(a, g):
    grad = lax.psum_scatter(contract(a, g, 0, 0).astype(BF16), FSDP, scatter_dimension=0, tiled=True)
    return lax.psum(grad, SEQ).astype(F32)


def shards(
    tokens,
    lengths,
    attn_gain,
    attn_shift,
    attn_weight,
    attn_bias,
    out_weight,
    out_bias,
    mlp_gain,
    mlp_shift,
    up_weight,
    up_bias,
    down_weight,
    down_bias,
    cotangent,
):
    width = tokens.shape[2]
    members = lax.axis_size(SEQ)
    staged = lax.axis_size("z") <= 8 and attn_weight.shape[0] % 128 == 0
    images = tokens.shape[0] // members
    slots = tokens.shape[1] * members
    rows = images * slots

    small = (attn_gain, attn_shift, attn_bias, out_bias, mlp_gain, mlp_shift, up_bias, down_bias)
    sizes = [v.shape[0] for v in small]
    cuts = [sum(sizes[:i]) for i in range(len(sizes))]
    packed = jnp.concatenate(small)

    few = tokens.shape[1]
    here = lax.axis_index(SEQ)
    lens = lax.dynamic_slice_in_dim(lengths, here * images, images, 0)
    slot = jnp.arange(slots, dtype=jnp.int32)
    slot = (slot // few ^ here) * few + slot % few
    valid = slot[None, :] < lens[:, None]
    key_valid = valid.astype(F32)[:, None, :]
    valid = valid.reshape(rows, 1)

    def by_image(value):
        value = value.reshape(members, images, few, width)
        return [send(pick(value, here ^ k), SEQ, k) if k else pick(value, here) for k in range(members)]

    def by_slot(value):
        value = value.reshape(images, members, few, width)
        return [send(value[:, k], SEQ, k) if k else value[:, 0] for k in range(members)]

    def in_images(blocks):
        return jnp.stack(blocks, axis=1).reshape(rows, width)

    def in_slots(blocks):
        blocks = jnp.stack(blocks)
        return jnp.concatenate([pick(blocks, here ^ k) for k in range(members)], axis=0)

    def unpack(vectors):
        vectors = vectors.astype(F32)
        return [vectors[:, c : c + n].reshape(1, -1) for c, n in zip(cuts, sizes)]

    if staged:
        cut_qkv, cut_out, cut_up = (Split(w.shape) for w in (attn_weight, out_weight, up_weight))
        cut_down = Split(down_weight.shape, by_rows=True)
        cut_group = Split(attn_weight.shape, columns=3 * width // GROUPS)
        first, second, third = pieces(attn_weight, out_weight, up_weight, down_weight, small)
        tokens, z1, second, third = tie(by_image(tokens), exchange(first, "z"), second, third)
        tokens = in_images(tokens)
        x1, y1, z2, z1, third = tie(swap(z1, "x"), swap(z1, "y"), exchange(second, "z"), z1, third)
        vec_z, vec_y = (v[:, : sum(sizes) // LANES, -LANES:].reshape(v.shape[0], -1) for v in (z1, y1))
        vectors = unpack(order_vectors(vec_z, vec_y))
        d1, x2, z3, c1, z2, vectors = tie(
            swap(x1, "y"), swap(z2, "x"), exchange(third, "z"), [swap(v, "c") for v in (z1, x1, y1)], z2, vectors
        )
        gain_a, shift_a, bias_qv, bias_out, gain_b, shift_b, bias_up, bias_down = vectors
        qkv_full, out_full = whole_weights((cut_qkv, cut_out), (z1, x1, y1, d1), (*c1, swap(d1, "c")))
        normed_a, joint = project(tokens, gain_a, shift_a, qkv_full, bias_qv)
        joint, out_full, y2, x3, c2, z2, z3, x2, normed_a = tie(
            joint, out_full, swap(z2, "y"), swap(z3, "x"), swap(z2, "c"), z2, z3, x2, normed_a
        )
        joint = joint.reshape(images, slots, 3 * width)
        context = attention(key_valid, joint).reshape(rows, width)
        context, d2, d3, c2, y2, x3, z3, cotangent = tie(
            context, swap(y2, "x"), swap(x3, "y"), (c2, swap(x2, "c"), swap(y2, "c")), y2, x3, z3, cotangent
        )
        (up_full,) = whole_weights((cut_up,), (z2, x2, y2, d2), (*c2, swap(d2, "c")))
        middle, normed_b, hidden, slope = expand(
            tokens, context, out_full, bias_out, gain_b, shift_b, up_full, bias_up
        )
        hidden, slope, y3, cot, c3, normed_sib, z3, x3, d3 = tie(
            hidden, slope, swap(z3, "y"), by_image(cotangent), [swap(v, "c") for v in (z3, x3, d3)], swap(normed_a, "c"), z3, x3, d3
        )
        cot = in_images(cot)
    else:
        vectors = unpack(lax.all_gather(packed, FSDP, axis=0))
        gain_a, shift_a, bias_qv, bias_out, gain_b, shift_b, bias_up, bias_down = vectors
        qkv_full, out_full, up_full, down_full = (
            lax.all_gather(w, FSDP, axis=0, tiled=True)
            for w in (grouped(attn_weight), out_weight, up_weight, down_weight)
        )
        tokens = in_images(by_image(tokens))
        cot = in_images(by_image(cotangent))
        normed_a, joint = project(tokens, gain_a, shift_a, qkv_full, bias_qv)
        joint = joint.reshape(images, slots, 3 * width)
        context = attention(key_valid, joint).reshape(rows, width)
        middle, normed_b, hidden, slope = expand(
            tokens, context, out_full, bias_out, gain_b, shift_b, up_full, bias_up
        )

    grad_out = jnp.where(valid, cot, jnp.zeros_like(cot))
    g_bias_down = jnp.sum(grad_out.astype(F32), axis=0)
    valid_wide = valid.astype(F32)

    def back_attention(grad_context, group):
        grad = attention(key_valid, joint, grad_context, group)
        return grad.reshape(rows, 3 * width // GROUPS)

    shard_count = lax.axis_size(FSDP)
    depth = lax.axis_size("z")
    if staged:
        (down_full,) = whole_weights((cut_down,), (z3, x3, y3, d3), (c3[0], c3[1], swap(y3, "c"), c3[2]))
        down_parts = grad_parts([(hidden, swap(hidden, "c"), grad_out, swap(grad_out, "c"))], cut_down, depth)
        down_parts, down_full, slope, context_sib, normed_sib_b = tie(
            down_parts, down_full, slope, swap(context, "c"), swap(normed_b, "c")
        )
        grad_pre, bias_up_sums, grad_middle, grad_branch, grad_context, sums_b = back(
            grad_out, down_full, slope, up_full, middle, gain_b, out_full
        )
        grad_pre, down_e, grad_context, grad_branch, hidden = tie(
            grad_pre, swap(down_parts[3], "x"), grad_context, grad_branch, hidden
        )
        grad_context = grad_context.reshape(images, slots, width)
        pre_sib, branch_sib = swap(grad_pre, "c"), swap(grad_branch, "c")
        down_x, down_y = swap(down_parts[1], "x"), swap(add(down_parts[2], down_e), "y")
        up_parts = grad_parts(
            [(normed_b, normed_sib_b, grad_pre, pre_sib), (context, context_sib, grad_branch, branch_sib)],
            cut_up,
            depth,
        )
        up_parts, grad_context = tie(up_parts, grad_context)
        up_e = swap(up_parts[3], "y")
        joint_0 = back_attention(grad_context, 0)
        joint_0, down_x, down_y, grad_context = tie(joint_0, down_x, down_y, grad_context)
        down_b = grad_z(down_parts, down_x, down_y)
        parts_0 = grad_parts([(normed_a, normed_sib, joint_0, swap(joint_0, "c"))], cut_group, depth, cut_group.wide)
        parts_0, grad_context = tie(parts_0, grad_context)
        e_0 = swap(parts_0[3], "x")
        joint_1 = back_attention(grad_context, 1)
        joint_1, e_0, up_e, hidden = tie(joint_1, e_0, up_e, hidden)
        up_x, up_y = swap(add(up_parts[1], up_e), "x"), swap(up_parts[2], "y")
        x_0, y_0 = swap(parts_0[1], "x"), swap(add(parts_0[2], e_0), "y")
        parts_1 = grad_parts([(normed_a, normed_sib, joint_1, swap(joint_1, "c"))], cut_group, depth, cut_group.wide)
        parts_1, joint_1, down_b, hidden = tie(parts_1, joint_1, down_b, hidden)
        e_1 = swap(parts_1[3], "y")
        result = finish(hidden, down_full, middle, bias_down, valid_wide)
        result, e_1, x_0, y_0, up_x, up_y = tie(result, e_1, x_0, y_0, up_x, up_y)
        input_grad, joint_sums, sums_a = back_input(joint_0, joint_1, qkv_full, tokens, gain_a, grad_middle)
        x_1, y_1 = swap(add(parts_1[1], e_1), "x"), swap(parts_1[2], "y")
        up_b = grad_z(up_parts, up_x, up_y)
    else:
        grad_pre, bias_up_sums, grad_middle, grad_branch, grad_context, sums_b = back(
            grad_out, down_full, slope, up_full, middle, gain_b, out_full
        )
        grad_context = grad_context.reshape(images, slots, width)
        joint_0, joint_1 = (back_attention(grad_context, g) for g in range(GROUPS))
        input_grad, joint_sums, sums_a = back_input(joint_0, joint_1, qkv_full, tokens, gain_a, grad_middle)
        grad_joint = jnp.concatenate([joint_0, joint_1], axis=1)
        layer_out = by_slot(finish(hidden, down_full, middle, bias_down, valid_wide))

    group = 3 * width // GROUPS
    joint_sums = ungrouped([joint_sums[:, g * group : (g + 1) * group] for g in range(GROUPS)])
    g_bias_qv = jnp.concatenate([joint_sums[:, :width], joint_sums[:, 2 * width :]], axis=1)
    g_gain_a, g_shift_a = sums_a[0], sums_a[1]
    g_gain_b, g_shift_b, g_bias_out = sums_b[0], sums_b[1], sums_b[2]
    g_bias_up = bias_up_sums
    small_grads = (g_gain_a, g_shift_a, g_bias_qv, g_bias_out, g_gain_b, g_shift_b, g_bias_up, g_bias_down)
    packed = jnp.concatenate([v.reshape(shard_count, -1) for v in small_grads], axis=1)
    if staged:
        x_1, y_1, up_b, layer_out, input_grad, packed = tie(x_1, y_1, up_b, by_slot(result), input_grad, packed)
        qkv_b = grad_z(
            tuple(jnp.concatenate([p, q], axis=2) for p, q in zip(parts_0[:1], parts_1[:1])),
            jnp.concatenate([x_0, x_1], axis=2),
            jnp.concatenate([y_0, y_1], axis=2),
        )
        qkv_b, up_g, down_g, input_grad, packed = tie(
            qkv_b, grad_x(up_b), grad_x(down_b), by_slot(input_grad), over_pairs(packed)
        )
        packed = over_line(packed)
        g_down = grad_core(down_g, by_rows=True).astype(F32)
        g_up = grad_core(up_g[:, : cut_up.wide]).astype(F32)
        g_out = grad_core(up_g[:, cut_up.wide :]).astype(F32)
        ours = grad_x(qkv_b)
        theirs = swap(ours, "c")
        halves = [(v[:, : cut_group.wide], v[:, cut_group.wide :]) for v in (ours, theirs)]
        g_qkv = ungrouped([in_order(lax.axis_index("c"), p, q, 1) for p, q in zip(*halves)]).astype(F32)
    else:
        input_grad = by_slot(input_grad)
        packed = lax.psum_scatter(packed, FSDP, scatter_dimension=0)
        packed = lax.psum(packed, SEQ)
        g_qkv, g_out, g_up, g_down = (
            scatter_plain(a, g)
            for a, g in ((normed_a, grad_joint), (context, grad_branch), (normed_b, grad_pre), (hidden, grad_out))
        )
        g_qkv = ungrouped([g_qkv[:, : 3 * width // GROUPS], g_qkv[:, 3 * width // GROUPS :]])
    layer_out, input_grad = in_slots(layer_out), in_slots(input_grad)
    (g_gain_a, g_shift_a, g_bias_qv, g_bias_out, g_gain_b, g_shift_b, g_bias_up, g_bias_down) = (
        packed[c : c + n] for c, n in zip(cuts, sizes)
    )
    return (
        layer_out,
        input_grad,
        g_gain_a,
        g_shift_a,
        g_qkv,
        g_bias_qv,
        g_out,
        g_bias_out,
        g_gain_b,
        g_shift_b,
        g_up,
        g_bias_up,
        g_down,
        g_bias_down,
    )


def solution(mesh):
    shard_count, members = mesh.devices.shape
    fine = Mesh(mesh.devices.reshape(shard_count // 2, 2, members // 2, 2), FSDP + SEQ)
    rows, vector, matrix = P(FSDP, SEQ, None), P(FSDP), P(FSDP, None)
    weights = (vector, vector, matrix, vector, matrix, vector, vector, vector, matrix, vector, matrix, vector)
    return jax.shard_map(
        shards,
        mesh=fine,
        in_specs=(rows, vector) + weights + (rows,),
        out_specs=(rows, rows) + weights,
        check_vma=False,
    )
```

```python
import functools

import jax
import jax.numpy as jnp
from jax import lax
from jax.experimental import pallas as pl
from jax.experimental.pallas import tpu as pltpu
from jax.sharding import Mesh
from jax.sharding import PartitionSpec as P

HEAD_DIM = 64
LANES = 128
GROUPS = 2
TILES = 2
EPSILON = 1e-06
BF16 = jnp.bfloat16
F32 = jnp.float32
FSDP, SEQ = ("z", "y"), ("x", "c")


def cost(microseconds, nbytes=0):
    return pl.CostEstimate(flops=int(microseconds * 1.1e9), bytes_accessed=nbytes, transcendentals=0)


def norm_back(grad_norm, gain, normal, inv_std):
    scaled = grad_norm * gain
    return inv_std * (
        scaled
        - jnp.mean(scaled, axis=-1, keepdims=True)
        - normal * jnp.mean(scaled * normal, axis=-1, keepdims=True)
    )


def contract(a, b, ca, cb):
    return lax.dot_general(a, b, (((ca,), (cb,)), ((), ())), preferred_element_type=F32)


def lanes_of(shape):
    lane = lax.broadcasted_iota(jnp.int32, shape, 1)
    return lane // HEAD_DIM, lane % HEAD_DIM


def spread_over(places, place, columns, rest=0.0):
    out = jnp.full(place.shape, rest, F32)
    for i in places:
        out = jnp.where(place == i, columns[i], out)
    return out


def parts_of(value, count):
    parts = []
    for _ in range(count):
        parts.append(value.astype(BF16).astype(F32))
        value = value - parts[-1]
    return parts


SCALE = HEAD_DIM ** (-0.5)


def attend_kernel(bias_ref, q_ref, k_ref, v_ref, out_ref, lse_ref):
    bias = bias_ref[0]
    for tile in range(q_ref.shape[2] // LANES):
        at = slice(tile * LANES, (tile + 1) * LANES)
        q, k, v = (ref[0, :, at].astype(F32) for ref in (q_ref, k_ref, v_ref))
        head_of, place = lanes_of(q.shape)
        context, lse = jnp.zeros(q.shape, F32), jnp.zeros(q.shape, F32)
        for head in range(LANES // HEAD_DIM):
            own = head_of == head
            left = jnp.where(own, q * SCALE, spread_over((0,), place, (1.0,))).astype(BF16)
            right = jnp.where(own, k, spread_over((0,), place, (bias,))).astype(BF16)
            scores = contract(left, right, 1, 1)
            top = jnp.max(scores, axis=-1, keepdims=True)
            exps = jnp.exp(scores - top).astype(BF16)
            both = contract(exps, jnp.where(own, v, 1.0).astype(BF16), 1, 0)
            other = (1 - head) * HEAD_DIM
            total = both[:, other : other + 1]
            context = jnp.where(own, both * (1.0 / total), context)
            lse = jnp.where(own, lse, top + jnp.log(total))
        out_ref[0, :, at] = context.astype(BF16)
        lse_ref[0, :, at] = lse


def attend_back_kernel(bias_ref, q_ref, k_ref, v_ref, lse_ref, context_ref, g_ref, out_ref):
    bias = bias_ref[0]
    tiles = q_ref.shape[2] // LANES
    width = out_ref.shape[2] // 3
    for tile in range(tiles):
        at = slice(tile * LANES, (tile + 1) * LANES)
        q_low, k_low, g_low = q_ref[0, :, at], k_ref[0, :, at], g_ref[0, :, at]
        q, k, v, g, context = (ref[0, :, at].astype(F32) for ref in (q_ref, k_ref, v_ref, g_ref, context_ref))
        head_of, place = lanes_of(q.shape)
        dq, dk, dv = (jnp.zeros(q.shape, F32) for _ in range(3))
        lse_parts = [-part for part in parts_of(lse_ref[0, :, at], 3)] + [1.0]
        product = g * context
        for head in range(LANES // HEAD_DIM):
            own = head_of == head
            left = jnp.where(own, q * SCALE, spread_over(range(4), place, lse_parts)).astype(BF16)
            right = jnp.where(own, k, spread_over(range(4), place, (1.0, 1.0, 1.0, bias))).astype(BF16)
            probs = jnp.exp(contract(left, right, 1, 1))
            inner = jnp.sum(jnp.where(own, product, 0.0), axis=-1, keepdims=True)
            inner_parts = [-part for part in parts_of(inner, 2)]
            left = jnp.where(own, g, spread_over(range(2), place, inner_parts)).astype(BF16)
            right = jnp.where(own, v, spread_over(range(2), place, (1.0, 1.0))).astype(BF16)
            grad_scores = (probs * contract(left, right, 1, 1)).astype(BF16)
            dq = jnp.where(own, contract(grad_scores, k_low, 1, 0), dq)
            dk = jnp.where(own, contract(grad_scores, q_low, 0, 0), dk)
            dv = jnp.where(own, contract(probs.astype(BF16), g_low, 0, 0), dv)
        for block, value in enumerate((dq * SCALE, dk * SCALE, dv)):
            start = block * width + (pl.program_id(1) * tiles + tile) * LANES
            out_ref[0, :, pl.ds(pl.multiple_of(start, LANES), LANES)] = value.astype(BF16)


def attention(key_bias, joint, saved=(), group=0):
    images, slots, width = joint.shape[0], joint.shape[1], joint.shape[2] // 3
    lanes = TILES * LANES
    in_group = width // lanes // GROUPS
    back = len(saved) > 0
    pairs = in_group if back else in_group * GROUPS
    block = (1, slots, lanes)

    def spec(part):
        def index(i, h):
            h = h + group * in_group
            return i, 0, (h // in_group * 3 + part) * in_group + h % in_group

        return pl.BlockSpec(block, index)

    plain = pl.BlockSpec(block, lambda i, h: (i, 0, h + group * in_group))
    bias = pl.BlockSpec((1, slots, 1), lambda i, h: (i, 0, 0))
    whole = pl.BlockSpec((1, slots, 3 * pairs * lanes), lambda i, h: (i, 0, 0))
    shape = lambda columns, kind: jax.ShapeDtypeStruct((images, slots, columns), kind)
    return pl.pallas_call(
        attend_back_kernel if back else attend_kernel,
        grid=(images, pairs),
        in_specs=[bias] + [spec(part) for part in range(3)] + [plain] * len(saved),
        out_specs=whole if back else [plain, plain],
        out_shape=shape(3 * pairs * lanes, BF16) if back else [shape(width, BF16), shape(width, F32)],
        cost_estimate=cost((1.3 if back else 0.8) * images * pairs * TILES),
    )(key_bias, joint, joint, joint, *saved)


STEP = 512


def stats(values):
    center = values - jnp.mean(values, axis=-1, keepdims=True)
    inv_std = lax.rsqrt(jnp.mean(center * center, axis=-1, keepdims=True) + EPSILON)
    return center * inv_std, inv_std


def column_sums(values):
    return jnp.sum(values, axis=0, keepdims=True)


def block_spec(shape, index=lambda j: 0, at=1):
    def position(j, place):
        value = index(j, place) if index.__code__.co_argcount == 2 else index(j)
        return (0, value) if at else (value, 0)

    return pl.BlockSpec(shape, position)


def whole_spec(array):
    return block_spec(array.shape)


def columns_spec(rows, index=lambda j: j):
    return block_spec((rows, STEP), index)


class Weight:
    def __init__(self, arrays, by_rows=False, base=0, blocks=None):
        self.arrays, self.by_rows, self.base, self.blocks = tuple(arrays), by_rows, base, blocks

    def specs(self):
        return [pl.BlockSpec(memory_space=pl.ANY)] * len(self.arrays)

    def copies(self, refs, place_ref, j, block, buf, sem):
        copy = lambda source, target: pltpu.make_async_copy(source, target, sem)
        if len(refs) == 1:
            at = pl.ds(pl.multiple_of(block * STEP, STEP), STEP)
            return [(None, [copy(refs[0].at[at] if self.by_rows else refs[0].at[:, at], buf)])]
        y, x, c = place_ref[0], place_ref[1], place_ref[2]
        depth, rows = refs[0].shape[0], refs[0].shape[1]

        def piece(owner, i, z):
            five = refs[5 * owner : 5 * owner + 5]
            if i < 3:
                return five[i].at[z]
            return five[3].at[z] if z < depth // 2 else five[4].at[z - depth // 2]

        found = []
        if not self.by_rows:
            half = self.blocks // 2
            lanes = pl.ds(pl.multiple_of(self.base + block % half * STEP, LANES), STEP)
            for owner in range(2):
                some = []
                for i in range(4):
                    for z in range(depth):
                        row = (2 * z + (y ^ (i // 2))) * 2 * rows + (x ^ (i % 2)) * rows
                        target = buf.at[pl.ds(pl.multiple_of(row, rows), rows)]
                        some.append(copy(piece(owner, i, z).at[:, lanes], target))
                found.append(((block // half == c) == (owner == 0), some))
            return found
        width = buf.shape[1]
        segments = refs[0].shape[2] // width
        for z in range(depth):
            for far in range(2):
                some = []
                for owner in range(2):
                    for i in range(2):
                        for k in range(segments):
                            row = ((c ^ owner) * 2 + (x ^ i)) * segments * rows + k * rows
                            source = piece(owner, 2 * far + i, z).at[:, pl.ds(k * width, width)]
                            some.append(copy(source, buf.at[pl.ds(pl.multiple_of(row, rows), rows)]))
                found.append((j == 2 * z + far, some))
        return found

    def start(self, *where):
        for condition, some in self.copies(*where):
            go = lambda some=some: [one.start() for one in some] and None
            go() if condition is None else pl.when(condition)(go)

    def wait(self, *where):
        for condition, some in self.copies(*where):
            go = lambda some=some: [one.wait() for one in some] and None
            go() if condition is None else pl.when(condition)(go)


def shard_block(j, place):
    return j // 2 * 2 + (place[0] ^ (j % 2))


def stream(weight, refs, place_ref, block, buf, sems):
    j = pl.program_id(0)

    def where(step):
        slot = step % 2
        return refs, place_ref, step, block(step), buf.at[slot], sems.at[slot]

    @pl.when(j == 0)
    def _():
        weight.start(*where(j))

    @pl.when(j + 1 < pl.num_programs(0))
    def _():
        weight.start(*where(j + 1))

    weight.wait(*where(j))
    return buf[j % 2]


def split_refs(refs, weights):
    groups = []
    for weight in weights:
        groups.append(refs[: len(weight.arrays)])
        refs = refs[len(weight.arrays) :]
    return groups, refs


def stepped(kernel, steps, place, weights, in_specs, operands, out_specs, out_shape, scratch, microseconds):
    specs = [spec for weight in weights for spec in weight.specs()]
    arrays = [v for weight in weights for v in weight.arrays]
    return pl.pallas_call(
        functools.partial(kernel, weights),
        grid_spec=pltpu.PrefetchScalarGridSpec(
            num_scalar_prefetch=1,
            grid=(steps,),
            in_specs=specs + in_specs,
            out_specs=out_specs,
            scratch_shapes=scratch,
        ),
        out_shape=out_shape,
        compiler_params=pltpu.CompilerParams(vmem_limit_bytes=56 << 20),
        cost_estimate=cost(microseconds),
    )(place, *arrays, *operands)


def streamed(rows, columns):
    return [pltpu.VMEM((2, rows, columns), BF16), pltpu.SemaphoreType.DMA((2,))]


def project_kernel(weights, place_ref, *refs):
    (weight_refs,), refs = split_refs(refs, weights)
    tokens_ref, gain_ref, shift_ref, bias_ref, normed_ref, joint_ref, buf, sems = refs
    j = pl.program_id(0)

    @pl.when(j == 0)
    def _():
        normal, _ = stats(tokens_ref[...].astype(F32))
        normed_ref[...] = (normal * gain_ref[...] + shift_ref[...]).astype(BF16)

    weight = stream(weights[0], weight_refs, place_ref, lambda step: step, buf, sems)
    bias = jnp.where(j % 3 == 1, 0.0, bias_ref[...])
    joint_ref[...] = (contract(normed_ref[...], weight, 1, 0) + bias).astype(BF16)


def project(place, tokens, gain, shift, weight, bias_qv):
    rows, width = tokens.shape
    assert width // GROUPS == STEP
    return stepped(
        project_kernel,
        3 * width // STEP,
        place,
        [weight],
        [whole_spec(tokens), whole_spec(gain), whole_spec(shift)]
        + [columns_spec(1, lambda j: j // 3 + jnp.where(j % 3 == 2, GROUPS, 0))],
        (tokens, gain, shift, bias_qv),
        [whole_spec(tokens), columns_spec(rows)],
        [jax.ShapeDtypeStruct((rows, width), BF16), jax.ShapeDtypeStruct((rows, 3 * width), BF16)],
        streamed(width, STEP),
        11,
    )


def out_blocks(weight, refs, place_ref, buf, sem):
    for block in range(buf.shape[0]):
        yield weight, (refs, place_ref, 0, block, buf.at[block], sem)


def expand_kernel(weights, place_ref, *refs):
    (up_refs, out_w_refs), refs = split_refs(refs, weights)
    tokens_ref, context_ref, bias_out_ref, gain_ref, shift_ref, bias_ref, *refs = refs
    middle_ref, normed_ref, hidden_ref, slope_ref, buf, sems, out_buf, out_sem = refs

    @pl.when(pl.program_id(0) == 0)
    def _():
        blocks = list(out_blocks(weights[1], out_w_refs, place_ref, out_buf, out_sem))
        for weight, where in blocks:
            weight.start(*where)
        for weight, where in blocks:
            weight.wait(*where)
        context = context_ref[...]
        branch = jnp.concatenate([contract(context, out_buf[b], 1, 0) for b in range(out_buf.shape[0])], axis=1)
        middle = tokens_ref[...].astype(F32) + (branch + bias_out_ref[...])
        middle_ref[...] = middle
        normal, _ = stats(middle)
        normed_ref[...] = (normal * gain_ref[...] + shift_ref[...]).astype(BF16)

    weight = stream(weights[0], up_refs, place_ref, lambda step: step, buf, sems)
    pre = contract(normed_ref[...], weight, 1, 0) + bias_ref[...]
    cumul = 0.5 * (1.0 + lax.erf(pre * 0.7071067811865476))
    hidden_ref[...] = (pre * cumul).astype(BF16)
    slope = cumul + pre * (jnp.exp(-0.5 * pre * pre) * 0.3989422804014327)
    slope_ref[...] = slope.astype(BF16)


def expand(place, tokens, context, out_weight, bias_out, gain, shift, up, bias_up):
    rows, width = tokens.shape
    hidden = bias_up.shape[1]
    return stepped(
        expand_kernel,
        hidden // STEP,
        place,
        [up, out_weight],
        [whole_spec(v) for v in (tokens, context, bias_out, gain, shift)] + [columns_spec(1)],
        (tokens, context, bias_out, gain, shift, bias_up),
        [whole_spec(tokens)] * 2 + [columns_spec(rows)] * 2,
        [jax.ShapeDtypeStruct((rows, width), F32), jax.ShapeDtypeStruct((rows, width), BF16)]
        + [jax.ShapeDtypeStruct((rows, hidden), BF16)] * 2,
        streamed(width, STEP) + [pltpu.VMEM((width // STEP, width, STEP), BF16), pltpu.SemaphoreType.DMA],
        20,
    )


def accumulate(total_ref, part, first=None):
    j = pl.program_id(0)

    @pl.when(j == 0)
    def _():
        total_ref[...] = part if first is None else first() + part

    @pl.when(j > 0)
    def _():
        total_ref[...] += part


def finish_kernel(weights, place_ref, *refs):
    (down_refs,), refs = split_refs(refs, weights)
    hidden_ref, middle_ref, bias_ref, valid_ref, result_ref, total_ref, buf, sems = refs
    block = lambda step: shard_block(step, place_ref)
    weight = stream(weights[0], down_refs, place_ref, block, buf, sems)
    part = contract(hidden_ref[...], weight, 1, 0)
    accumulate(total_ref, part, lambda: middle_ref[...] + bias_ref[...])

    @pl.when(pl.program_id(0) == pl.num_programs(0) - 1)
    def _():
        result_ref[...] = jnp.where(valid_ref[...] > 0.5, total_ref[...], 0.0).astype(BF16)


def finish(place, hidden, down, middle, bias_down, valid):
    rows, width = middle.shape
    return stepped(
        finish_kernel,
        hidden.shape[1] // STEP,
        place,
        [down],
        [columns_spec(rows, shard_block)] + [whole_spec(v) for v in (middle, bias_down, valid)],
        (hidden, middle, bias_down, valid),
        whole_spec(middle),
        jax.ShapeDtypeStruct((rows, width), BF16),
        [pltpu.VMEM((rows, width), F32)] + streamed(STEP, width),
        11,
    )


def back_kernel(weights, place_ref, *refs):
    (down_refs, up_refs, out_w_refs), refs = split_refs(refs, weights)
    grad_ref, slope_ref, middle_ref, gain_ref, *refs = refs
    pre_ref, bias_up_ref, grad_middle_ref, branch_ref, context_ref, sums_ref, total_ref, *refs = refs
    down_buf, down_sems, up_buf, up_sems, out_buf, out_sem = refs
    j = pl.program_id(0)
    blocks = lambda: out_blocks(weights[2], out_w_refs, place_ref, out_buf, out_sem)

    @pl.when(j == 0)
    def _():
        for weight, where in blocks():
            weight.start(*where)

    block = lambda step: shard_block(step, place_ref)
    down = stream(weights[0], down_refs, place_ref, block, down_buf, down_sems)
    up = stream(weights[1], up_refs, place_ref, block, up_buf, up_sems)
    pre = (contract(grad_ref[...], down, 1, 1) * slope_ref[...].astype(F32)).astype(BF16)
    pre_ref[...] = pre
    bias_up_ref[...] = column_sums(pre.astype(F32))
    accumulate(total_ref, contract(pre, up, 1, 1))

    @pl.when(j == pl.num_programs(0) - 1)
    def _():
        for weight, where in blocks():
            weight.wait(*where)
        normal, inv_std = stats(middle_ref[...])
        total = total_ref[...]
        grad_middle = grad_ref[...].astype(F32) + norm_back(total, gain_ref[...], normal, inv_std)
        grad_middle_ref[...] = grad_middle
        branch = grad_middle.astype(BF16)
        branch_ref[...] = branch
        context_ref[...] = sum(
            contract(branch[:, b * STEP : (b + 1) * STEP], out_buf[b], 1, 1) for b in range(out_buf.shape[0])
        ).astype(BF16)
        sums_ref[0:1] = column_sums(total * normal)
        sums_ref[1:2] = column_sums(total)
        sums_ref[2:3] = column_sums(branch.astype(F32))


def back(place, grad_out, down, slope, up, middle, gain, out_weight):
    rows, width = middle.shape
    hidden = slope.shape[1]
    return stepped(
        back_kernel,
        hidden // STEP,
        place,
        [down, up, out_weight],
        [whole_spec(grad_out), columns_spec(rows, shard_block), whole_spec(middle), whole_spec(gain)],
        (grad_out, slope, middle, gain),
        [columns_spec(rows, shard_block), columns_spec(1, shard_block)]
        + [whole_spec(middle)] * 3
        + [block_spec((8, width))],
        [
            jax.ShapeDtypeStruct((rows, hidden), BF16),
            jax.ShapeDtypeStruct((1, hidden), F32),
            jax.ShapeDtypeStruct((rows, width), F32),
            jax.ShapeDtypeStruct((rows, width), BF16),
            jax.ShapeDtypeStruct((rows, width), BF16),
            jax.ShapeDtypeStruct((8, width), F32),
        ],
        [pltpu.VMEM((rows, width), F32)]
        + streamed(STEP, width)
        + streamed(width, STEP)
        + [pltpu.VMEM((width // STEP, width, STEP), BF16), pltpu.SemaphoreType.DMA],
        23,
    )


def input_kernel(weights, place_ref, *refs):
    (weight_refs,), refs = split_refs(refs, weights)
    joint_0_ref, joint_1_ref, tokens_ref, gain_ref, grad_middle_ref, *refs = refs
    input_ref, bias_ref, sums_ref, total_ref, buf, sems = refs
    j = pl.program_id(0)
    first = jnp.broadcast_to(j < 3, joint_0_ref.shape)
    joint = jnp.where(first, joint_0_ref[...], joint_1_ref[...])
    bias_ref[...] = column_sums(joint.astype(F32))
    weight = stream(weights[0], weight_refs, place_ref, lambda step: step, buf, sems)
    accumulate(total_ref, contract(joint, weight, 1, 1))

    @pl.when(j == pl.num_programs(0) - 1)
    def _():
        normal, inv_std = stats(tokens_ref[...].astype(F32))
        total = total_ref[...]
        grad = grad_middle_ref[...] + norm_back(total, gain_ref[...], normal, inv_std)
        input_ref[...] = grad.astype(BF16)
        sums_ref[0:1] = column_sums(total * normal)
        sums_ref[1:2] = column_sums(total)


def back_input(place, joint_0, joint_1, weight, tokens, gain, grad_middle):
    rows, width = tokens.shape
    return stepped(
        input_kernel,
        3 * width // STEP,
        place,
        [weight],
        [columns_spec(rows, lambda j: jnp.minimum(j, 2)), columns_spec(rows, lambda j: jnp.maximum(j - 3, 0))]
        + [whole_spec(v) for v in (tokens, gain, grad_middle)],
        (joint_0, joint_1, tokens, gain, grad_middle),
        [whole_spec(tokens), columns_spec(1), block_spec((8, width))],
        [
            jax.ShapeDtypeStruct((rows, width), BF16),
            jax.ShapeDtypeStruct((1, 3 * width), F32),
            jax.ShapeDtypeStruct((8, width), F32),
        ],
        [pltpu.VMEM((rows, width), F32)] + streamed(width, STEP),
        14,
    )


def grouped(value):
    width = value.shape[-1] // 3
    part = width // GROUPS
    return jnp.concatenate(
        [value[..., t * width + g * part :][..., :part] for g in range(GROUPS) for t in range(3)], axis=-1
    )


def ungrouped(values):
    part = values[0].shape[-1] // 3
    return jnp.concatenate(
        [v[..., t * part : (t + 1) * part] for t in range(3) for v in values], axis=-1
    )


def swap(value, axis):
    return lax.ppermute(value, axis, [(0, 1), (1, 0)])


def send(value, axis, step):
    return lax.ppermute(value, axis, [(i, i ^ step) for i in range(lax.axis_size(axis))])


def pick(blocks, index):
    return lax.dynamic_index_in_dim(blocks, index, 0, keepdims=False)


def tie(*values):
    return lax.optimization_barrier(values)


def after(value, *others):
    return lax.optimization_barrier((value,) + others)[0]


def my_place():
    return jnp.stack([lax.axis_index(n) for n in ("y", "x", "c")]).astype(jnp.int32)


class Split:
    def __init__(self, shard, by_rows=False, columns=None):
        self.shard_rows, self.columns = shard[0], columns or shard[1]
        self.by_rows = by_rows
        self.rows = self.shard_rows // 4 if by_rows else self.shard_rows // 2
        self.wide = self.columns if by_rows else self.columns // 2

def exchange(blocks, axis):
    return lax.all_to_all(blocks, axis, split_axis=0, concat_axis=0, tiled=True)


def pieces_kernel(depth, rows, place_ref, qkv_ref, out_ref, up_ref, down_ref, *refs):
    *vector_refs, first_ref, second_ref, third_ref = refs
    x, c = place_ref[1], place_ref[2]
    at = pl.ds(pl.multiple_of(x * rows, rows), rows)

    def put(ref, lane, value):
        for z in range(depth):
            ref[z, : value.shape[0], lane : lane + value.shape[1]] = value
        return lane + value.shape[1]

    def columns(ref, start, count):
        return ref[at, pl.ds(pl.multiple_of(start, LANES), count)]

    width = out_ref.shape[1]
    part = width // 2
    lane = 0
    for t in range(3):
        lane = put(first_ref, lane, columns(qkv_ref, t * width + c * part, part))
    lane = put(first_ref, lane, columns(out_ref, c * part, part))
    packed = jnp.concatenate([ref[...] for ref in vector_refs], axis=0)
    padding = jnp.zeros((rows - packed.shape[0], LANES), packed.dtype)
    put(first_ref, lane, jnp.concatenate([packed, padding], axis=0))
    half = up_ref.shape[1] // 2
    put(second_ref, 0, columns(up_ref, c * half, half))
    blocks = down_ref.shape[0] // 4 // rows
    lane = 0
    for block in range(blocks):
        start = ((2 * c + x) * blocks + block) * rows
        lane = put(third_ref, lane, down_ref[pl.ds(pl.multiple_of(start, rows), rows), :])


def pieces(qkv, out, up, down, vectors):
    depth, rows = lax.axis_size("z"), qkv.shape[0] // 2
    vectors = [v.reshape(-1, LANES) for v in vectors]
    width = out.shape[1]
    wide = (2 * width + LANES, up.shape[1] // 2, down.shape[0] // 4 // rows * width)
    vmem = pl.BlockSpec(memory_space=pltpu.VMEM)
    return pl.pallas_call(
        functools.partial(pieces_kernel, depth, rows),
        in_specs=[pl.BlockSpec(memory_space=pltpu.SMEM)] + [vmem] * (4 + len(vectors)),
        out_specs=[vmem] * 3,
        out_shape=[jax.ShapeDtypeStruct((depth, rows, n), BF16) for n in wide],
        cost_estimate=cost(3),
    )(my_place(), qkv, out, up, down, *vectors)


def corner(from_x, from_y):
    half = from_x.shape[0] // 2
    return swap(from_x[:half], "y"), swap(from_y[half:], "x")


def core_swap(*pieces):
    return tuple(swap(v, "c") for v in pieces)


def my_place():
    return jnp.stack([lax.axis_index(n) for n in ("y", "x", "c")]).astype(jnp.int32)


def part_refs(x, near, far, rows, refs, at):
    own_ref, to_x_ref, to_y_ref, corner_ref = refs
    low, high = near[:rows], near[rows:]
    own_ref[at] = jnp.where(x == 0, low, high)
    to_x_ref[at] = jnp.where(x == 0, high, low)
    low, high = far[:rows], far[rows:]
    to_y_ref[at] = jnp.where(x == 0, low, high)
    corner_ref[at] = jnp.where(x == 0, high, low)


def grad_columns_kernel(ends, cut, place_ref, *refs):
    y, x = place_ref[0], place_ref[1]
    out_refs, turned_ref = refs[-5:-1], refs[-1]
    j = pl.program_id(0)

    def one(first, a_ref, a_sib_ref, g_ref, g_sib_ref):
        @pl.when(j == first)
        def _():
            turned_ref[0] = a_ref[...].T
            turned_ref[1] = a_sib_ref[...].T

        total = contract(turned_ref[0], g_ref[...], 1, 0) + contract(turned_ref[1], g_sib_ref[...], 1, 0)
        total = total.reshape(-1, 2, cut.shard_rows, total.shape[1])
        for z in range(total.shape[0]):
            near = jnp.where(y == 0, total[z, 0], total[z, 1]).astype(BF16)
            far = jnp.where(y == 0, total[z, 1], total[z, 0]).astype(BF16)
            part_refs(x, near, far, cut.rows, out_refs, z)

    if len(ends) == 1:
        one(0, *refs[:4])
        return
    for i, end in enumerate(ends):
        first = 0 if i == 0 else ends[i - 1]
        pl.when((j >= first) & (j < end))(functools.partial(one, first, *refs[4 * i : 4 * i + 4]))


def grad_rows_kernel(cut, place_ref, a0_ref, a1_ref, a0_sib_ref, a1_sib_ref, g_ref, g_sib_ref, *out_refs):
    y, x = place_ref[0], place_ref[1]
    by_y = [
        contract(ref[...], g_ref[...], 0, 0)
        + contract(sib_ref[...], g_sib_ref[...], 0, 0)
        for ref, sib_ref in ((a0_ref, a0_sib_ref), (a1_ref, a1_sib_ref))
    ]
    near = jnp.where(y == 0, by_y[0], by_y[1]).astype(BF16)
    far = jnp.where(y == 0, by_y[1], by_y[0]).astype(BF16)
    part_refs(x, near, far, cut.rows, out_refs, 0)


def grad_parts(jobs, cut, depth, step=512):
    tokens = jobs[0][0].shape[0]
    specs, operands, ends = [], [], []
    if cut.by_rows:
        ((a, a_sib, g, g_sib, _, _),) = jobs
        half = 2 * cut.rows
        every = pl.BlockSpec((tokens, cut.wide), lambda j, place: (0, 0))
        specs = [
            pl.BlockSpec((tokens, half), lambda j, place: (0, 4 * j + place[2])),
            pl.BlockSpec((tokens, half), lambda j, place: (0, 4 * j + 2 + place[2])),
            pl.BlockSpec((tokens, half), lambda j, place: (0, 4 * j + place[2])),
            pl.BlockSpec((tokens, half), lambda j, place: (0, 4 * j + 2 + place[2])),
            every,
            every,
        ]
        operands, kernel, grid, wide = [a, a, a_sib, a_sib, g, g_sib], functools.partial(grad_rows_kernel, cut), depth, cut.wide
        out_spec = lambda n: pl.BlockSpec((1, n, wide), lambda j, place: (j, 0, 0))
    else:
        grid = 0
        for a, a_sib, g, g_sib, start, steps in jobs:
            in_half = g.shape[1] // 2 // step
            every = pl.BlockSpec((tokens, a.shape[1]), lambda j, place: (0, 0))
            at = lambda j, first=grid, steps=steps: jnp.clip(j - first, 0, steps - 1)
            specs += [
                every,
                every,
            ] + [
                pl.BlockSpec(
                    (tokens, step), lambda j, place, at=at, n=in_half, s=start: (0, place[2] * n + s + at(j))
                )
            ] * 2
            operands += [a, a_sib, g, g_sib]
            grid += steps
            ends.append(grid)
        kernel, wide = functools.partial(grad_columns_kernel, ends, cut), grid * step
        out_spec = lambda n: pl.BlockSpec((depth, n, step), lambda j, place: (0, 0, j))
    total = 8 * depth * cut.rows * wide
    return pl.pallas_call(
        kernel,
        grid_spec=pltpu.PrefetchScalarGridSpec(
            num_scalar_prefetch=1,
            grid=(grid,),
            in_specs=specs,
            out_specs=[out_spec(cut.rows)] * 4,
            scratch_shapes=[] if cut.by_rows else [pltpu.VMEM((2, jobs[0][0].shape[1], tokens), BF16)],
        ),
        out_shape=[jax.ShapeDtypeStruct((depth, cut.rows, wide), BF16)] * 4,
        compiler_params=pltpu.CompilerParams(vmem_limit_bytes=52 << 20),
        cost_estimate=cost(total * 2.2e-6),
    )(my_place(), *operands)


def add(one, other):
    return (one.astype(F32) + other.astype(F32)).astype(BF16)


def grad_z(parts, from_x, from_y):
    return exchange(sum(v.astype(F32) for v in (parts[0], from_x, from_y)).astype(BF16), "z")


def grad_x(blocks):
    mine = jnp.sum(blocks.astype(F32), axis=0).astype(BF16)
    return mine, swap(mine, "x")


def grad_core(mine, from_x):
    return mine, from_x, swap(mine, "c"), swap(from_x, "c")


def shard_kernel(plan, place_ref, *refs):
    x, c = place_ref[1], place_ref[2]
    parts, out_refs = refs[: -len(plan)], refs[-len(plan) :]
    for (by_rows, sources), out_ref in zip(plan, out_refs):
        column = 0
        for core in range(2):
            for number, start, count, at in sources:
                four = parts[4 * number : 4 * number + 4]
                rows = four[0].shape[0]
                for half in range(2):
                    both = [
                        jnp.where(c == core, four[i][:, start : start + count], four[2 + i][:, start : start + count])
                        for i in range(2)
                    ]
                    value = jnp.where(x == half, both[0], both[1]).astype(F32)
                    if by_rows:
                        row = (2 * core + half) * rows
                        out_ref[row : row + rows, :] = value
                    else:
                        out_ref[half * rows : (half + 1) * rows, at[core] : at[core] + count] = value


def shards_of(gradients, plan):
    parts = [v for gradient in gradients for v in gradient]
    vmem = pl.BlockSpec(memory_space=pltpu.VMEM)
    return pl.pallas_call(
        functools.partial(shard_kernel, [(by_rows, sources) for by_rows, _, sources in plan]),
        in_specs=[pl.BlockSpec(memory_space=pltpu.SMEM)] + [vmem] * len(parts),
        out_specs=[vmem] * len(plan),
        out_shape=[jax.ShapeDtypeStruct(shape, F32) for _, shape, _ in plan],
        cost_estimate=cost(2),
    )(my_place(), *parts)


def pack_kernel(sums_a_ref, joint_ref, sums_b_ref, up_ref, down_ref, out_ref):
    shards = out_ref.shape[0]
    width = down_ref.shape[1]
    part = width // GROUPS

    def put(at, count, source):
        for i in range(shards):
            out_ref[i : i + 1, at : at + count] = source(i, count)
        return at + count

    def plain(ref, row):
        return lambda i, n: ref[row : row + 1, i * n : (i + 1) * n]

    def query_value(i, n):
        value, at = divmod(i * n, width)
        group, at = divmod(at, part)
        start = (3 * group + 2 * value) * part + at
        return joint_ref[0:1, start : start + n]

    n = width // shards
    at = put(0, n, plain(sums_a_ref, 0))
    at = put(at, n, plain(sums_a_ref, 1))
    at = put(at, 2 * n, query_value)
    at = put(at, n, plain(sums_b_ref, 2))
    at = put(at, n, plain(sums_b_ref, 0))
    at = put(at, n, plain(sums_b_ref, 1))
    at = put(at, up_ref.shape[1] // shards, plain(up_ref, 0))
    put(at, n, plain(down_ref, 0))


def pack(shards, sums_a, joint_sums, sums_b, up_sums, down_sums):
    vmem = pl.BlockSpec(memory_space=pltpu.VMEM)
    columns = (9 - 1) * down_sums.shape[1] + up_sums.shape[1]
    return pl.pallas_call(
        pack_kernel,
        in_specs=[vmem] * 5,
        out_specs=vmem,
        out_shape=jax.ShapeDtypeStruct((shards, columns // shards), F32),
        cost_estimate=cost(1),
    )(sums_a, joint_sums, sums_b, up_sums, down_sums)


def in_order(index, mine, theirs, axis):
    first, second = jnp.where(index == 0, mine, theirs), jnp.where(index == 0, theirs, mine)
    return jnp.concatenate([first, second], axis=axis)


def order_vectors(own_y, other_y):
    y = lax.axis_index("y")
    rows = [jnp.where(y == 0, own_y, other_y), jnp.where(y == 0, other_y, own_y)]
    return jnp.stack(rows, axis=1).reshape(2 * own_y.shape[0], -1)


def over_pairs(packed):
    y = lax.axis_index("y")
    packed = packed + swap(packed, "c")
    packed = packed + swap(packed, "x")
    packed = packed.reshape(lax.axis_size("z"), 2, -1)
    row = lambda yy: lax.dynamic_index_in_dim(packed, yy, 1, keepdims=False)
    return row(y) + swap(row(1 - y), "y")


def over_line(packed):
    z = lax.axis_index("z")
    return pick(packed, z) + sum(send(pick(packed, z ^ k), "z", k) for k in range(1, lax.axis_size("z")))


def scatter_plain(a, g):
    grad = lax.psum_scatter(contract(a, g, 0, 0).astype(BF16), FSDP, scatter_dimension=0, tiled=True)
    return lax.psum(grad, SEQ).astype(F32)


def shards(
    tokens,
    lengths,
    attn_gain,
    attn_shift,
    attn_weight,
    attn_bias,
    out_weight,
    out_bias,
    mlp_gain,
    mlp_shift,
    up_weight,
    up_bias,
    down_weight,
    down_bias,
    cotangent,
):
    width = tokens.shape[2]
    members = lax.axis_size(SEQ)
    staged = lax.axis_size("z") <= 8 and attn_weight.shape[0] % 128 == 0
    images = tokens.shape[0] // members
    slots = tokens.shape[1] * members
    rows = images * slots

    small = (attn_gain, attn_shift, attn_bias, out_bias, mlp_gain, mlp_shift, up_bias, down_bias)
    sizes = [v.shape[0] for v in small]
    cuts = [sum(sizes[:i]) for i in range(len(sizes))]
    packed = jnp.concatenate(small)

    few = tokens.shape[1]
    here = lax.axis_index(SEQ)
    lens = lax.dynamic_slice_in_dim(lengths, here * images, images, 0)
    slot = jnp.arange(slots, dtype=jnp.int32)
    slot = (slot // few ^ here) * few + slot % few
    valid = slot[None, :] < lens[:, None]
    key_bias = jnp.where(valid, 0.0, -1000000000.0)[:, :, None]
    valid = valid.reshape(rows, 1)

    def by_image(value):
        value = value.reshape(members, images, few, width)
        return [send(pick(value, here ^ k), SEQ, k) if k else pick(value, here) for k in range(members)]

    def by_slot(value):
        value = value.reshape(images, members, few, width)
        return [send(value[:, k], SEQ, k) if k else value[:, 0] for k in range(members)]

    def in_images(blocks):
        return jnp.stack(blocks, axis=1).reshape(rows, width)

    def in_slots(blocks):
        blocks = jnp.stack(blocks)
        return jnp.concatenate([pick(blocks, here ^ k) for k in range(members)], axis=0)

    def unpack(vectors):
        vectors = vectors.astype(F32)
        return [vectors[:, c : c + n].reshape(1, -1) for c, n in zip(cuts, sizes)]

    if staged:
        cut_qkv, cut_out, cut_up = (Split(w.shape) for w in (attn_weight, out_weight, up_weight))
        cut_down = Split(down_weight.shape, by_rows=True)
        cut_group = Split(attn_weight.shape, columns=3 * width // GROUPS)
        place = my_place()
        first, second, third = pieces(attn_weight, out_weight, up_weight, down_weight, small)
        tokens, cot, z1, second, third = tie(
            by_image(tokens), by_image(cotangent), exchange(first, "z"), second, third
        )
        tokens, cot = in_images(tokens), in_images(cot)
        x1, y1 = swap(z1, "x"), swap(z1, "y")
        z2 = exchange(second, "z")
        x1, y1, z1, third = tie(x1, y1, z1, third)
        vec_z, vec_y = (v[:, : sum(sizes) // LANES, -LANES:].reshape(v.shape[0], -1) for v in (z1, y1))
        vectors = unpack(order_vectors(vec_z, vec_y))
        d1, c1, z2, vectors, third = tie(corner(x1, y1), core_swap(z1, x1, y1), z2, vectors, third)
        gain_a, shift_a, bias_qv, bias_out, gain_b, shift_b, bias_up, bias_down = vectors
        arrays = (z1, x1, y1, *d1, *c1, *core_swap(*d1))
        qkv_full = Weight(arrays, blocks=3 * width // STEP)
        out_full = Weight(arrays, base=cut_qkv.wide, blocks=width // STEP)
        x2, y2, z3 = swap(z2, "x"), swap(z2, "y"), exchange(third, "z")
        normed_a, joint = project(place, tokens, gain_a, shift_a, qkv_full, bias_qv)
        joint, x2, y2, z2, normed_a = tie(joint, x2, y2, z2, normed_a)
        joint = joint.reshape(images, slots, 3 * width)
        d2, c2 = corner(x2, y2), core_swap(z2, x2, y2)
        context, lse = attention(key_bias, joint)
        context, d2, c2, z3 = tie(context.reshape(rows, width), d2, c2, z3)
        x3, y3 = swap(z3, "x"), swap(z3, "y")
        up_full = Weight((z2, x2, y2, *d2, *c2, *core_swap(*d2)), blocks=cut_up.columns // STEP)
        middle, normed_b, hidden, slope = expand(
            place, tokens, context, out_full, bias_out, gain_b, shift_b, up_full, bias_up
        )
        hidden, slope, x3, y3, z3, normed_sib = tie(hidden, slope, x3, y3, z3, swap(normed_a, "c"))
    else:
        vectors = unpack(lax.all_gather(packed, FSDP, axis=0))
        gain_a, shift_a, bias_qv, bias_out, gain_b, shift_b, bias_up, bias_down = vectors
        place = jnp.zeros((3,), jnp.int32)
        qkv_full, out_full, up_full, down_full = (
            Weight([lax.all_gather(w, FSDP, axis=0, tiled=True)], by_rows=w is down_weight)
            for w in (grouped(attn_weight), out_weight, up_weight, down_weight)
        )
        tokens = in_images(by_image(tokens))
        cot = in_images(by_image(cotangent))
        normed_a, joint = project(place, tokens, gain_a, shift_a, qkv_full, bias_qv)
        joint = joint.reshape(images, slots, 3 * width)
        context, lse = attention(key_bias, joint)
        context = context.reshape(rows, width)
        middle, normed_b, hidden, slope = expand(
            place, tokens, context, out_full, bias_out, gain_b, shift_b, up_full, bias_up
        )

    grad_out = jnp.where(valid, cot, jnp.zeros_like(cot))
    g_bias_down = jnp.sum(grad_out.astype(F32), axis=0, keepdims=True)
    valid_wide = valid.astype(F32)

    def back_attention(grad_context, group):
        saved = (lse, context.reshape(images, slots, width), grad_context)
        grad = attention(key_bias, joint, saved, group)
        return grad.reshape(rows, 3 * width // GROUPS)

    shard_count = lax.axis_size(FSDP)
    depth = lax.axis_size("z")
    if staged:
        d3, c3 = corner(x3, y3), core_swap(z3, x3, y3)
        down_parts = grad_parts([(hidden, swap(hidden, "c"), grad_out, swap(grad_out, "c"), 0, 0)], cut_down, depth)
        down_parts, slope, d3, c3, hidden = tie(down_parts, slope, d3, c3, hidden)
        down_full = Weight((z3, x3, y3, *d3, *c3, *core_swap(*d3)), by_rows=True)
        down_e = swap(down_parts[3], "y")
        grad_pre, bias_up_sums, grad_middle, grad_branch, grad_context, sums_b = back(
            place, grad_out, down_full, slope, up_full, middle, gain_b, out_full
        )
        grad_pre, down_e, grad_context, grad_branch, context_sib, normed_sib_b = tie(
            grad_pre, down_e, grad_context, grad_branch, swap(context, "c"), swap(normed_b, "c")
        )
        grad_context = grad_context.reshape(images, slots, width)
        pre_sib, branch_sib = swap(grad_pre, "c"), swap(grad_branch, "c")
        down_x, down_y = swap(add(down_parts[1], down_e), "x"), swap(down_parts[2], "y")
        joint_0 = back_attention(grad_context, 0)
        joint_0, grad_context, pre_sib, branch_sib = tie(joint_0, grad_context, pre_sib, branch_sib)
        half = cut_up.wide // STEP // 2
        up_job = (normed_b, normed_sib_b, grad_pre, pre_sib)
        a_parts = grad_parts([up_job + (0, half)], cut_up, depth)
        joint_0_sib = swap(joint_0, "c")
        a_parts, grad_context = tie(a_parts, grad_context)
        a_e = swap(a_parts[3], "y")
        out_job = (context, context_sib, grad_branch, branch_sib, 0, cut_out.wide // STEP)
        b_parts = grad_parts([up_job + (half, half), out_job], cut_up, depth)
        b_parts, grad_context, a_e, down_x, down_y = tie(b_parts, grad_context, a_e, down_x, down_y)
        a_x, a_y = swap(add(a_parts[1], a_e), "x"), swap(a_parts[2], "y")
        b_e = swap(b_parts[3], "y")
        down_b = grad_z(down_parts, down_x, down_y)
        qkv_job = lambda joint, sib: [(normed_a, normed_sib, joint, sib, 0, 1)]
        parts_0 = grad_parts(qkv_job(joint_0, joint_0_sib), cut_group, depth, cut_group.wide)
        parts_0, grad_context = tie(parts_0, grad_context)
        e_0 = swap(parts_0[3], "x")
        joint_1 = back_attention(grad_context, 1)
        joint_1, e_0, a_x, a_y, b_e, down_b, hidden = tie(joint_1, e_0, a_x, a_y, b_e, down_b, hidden)
        b_x, b_y = swap(add(b_parts[1], b_e), "x"), swap(b_parts[2], "y")
        a_z = grad_z(a_parts, a_x, a_y)
        x_0, y_0 = swap(parts_0[1], "x"), swap(add(parts_0[2], e_0), "y")
        parts_1 = grad_parts(qkv_job(joint_1, swap(joint_1, "c")), cut_group, depth, cut_group.wide)
        parts_1, joint_1 = tie(parts_1, joint_1)
        e_1 = swap(parts_1[3], "y")
        input_grad, joint_sums, sums_a = back_input(place, joint_0, joint_1, qkv_full, tokens, gain_a, grad_middle)
        input_grad, e_1, x_0, y_0, b_x, b_y, a_z, hidden = tie(input_grad, e_1, x_0, y_0, b_x, b_y, a_z, hidden)
        x_1, y_1 = swap(add(parts_1[1], e_1), "x"), swap(parts_1[2], "y")
        b_z = grad_z(b_parts, b_x, b_y)
        result = finish(place, hidden, down_full, middle, bias_down, valid_wide)
    else:
        grad_pre, bias_up_sums, grad_middle, grad_branch, grad_context, sums_b = back(
            place,
            grad_out, down_full, slope, up_full, middle, gain_b, out_full
        )
        grad_context = grad_context.reshape(images, slots, width)
        joint_0, joint_1 = (back_attention(grad_context, g) for g in range(GROUPS))
        input_grad, joint_sums, sums_a = back_input(place, joint_0, joint_1, qkv_full, tokens, gain_a, grad_middle)
        grad_joint = jnp.concatenate([joint_0, joint_1], axis=1)
        layer_out = by_slot(finish(place, hidden, down_full, middle, bias_down, valid_wide))

    if staged:
        packed = pack(shard_count, sums_a, joint_sums, sums_b, bias_up_sums, g_bias_down)
    else:
        group = 3 * width // GROUPS
        joint_sums = ungrouped([joint_sums[:, g * group : (g + 1) * group] for g in range(GROUPS)])
        g_bias_qv = jnp.concatenate([joint_sums[:, :width], joint_sums[:, 2 * width :]], axis=1)
        small_grads = (sums_a[0], sums_a[1], g_bias_qv, sums_b[2], sums_b[0], sums_b[1], bias_up_sums, g_bias_down)
        packed = jnp.concatenate([v.reshape(shard_count, -1) for v in small_grads], axis=1)
    if staged:
        x_1, y_1, b_z, result, input_grad, packed, a_g, down_g = tie(
            x_1, y_1, b_z, result, by_slot(input_grad), packed, grad_x(a_z), grad_x(down_b)
        )
        qkv_b = grad_z(
            tuple(jnp.concatenate([p, q], axis=2) for p, q in zip(parts_0[:1], parts_1[:1])),
            jnp.concatenate([x_0, x_1], axis=2),
            jnp.concatenate([y_0, y_1], axis=2),
        )
        qkv_b, a_g, b_g, down_g, layer_out, packed = tie(
            qkv_b, grad_core(*a_g), grad_core(*grad_x(b_z)), grad_core(*down_g), by_slot(result), over_pairs(packed)
        )
        packed = over_line(packed)
        half, n_out, n_qkv = cut_up.wide // 2, cut_out.wide, cut_group.wide
        up_plan = [(0, 0, half, (0, 2 * half)), (1, 0, half, (half, 3 * half))]
        g_up, g_out, g_down = shards_of(
            (a_g, b_g, down_g),
            [
                (False, up_weight.shape, up_plan),
                (False, out_weight.shape, [(1, half, n_out, (0, n_out))]),
                (True, down_weight.shape, [(2, 0, width, None)]),
            ],
        )
        part = width // GROUPS
        qkv_plan = []
        for g in range(GROUPS):
            for low in range(0, n_qkv, LANES):
                places = [divmod(c * n_qkv + low, part) for c in range(2)]
                places = [t * width + g * part + at for t, at in places]
                qkv_plan.append((0, g * n_qkv + low, LANES, places))
        (g_qkv,) = shards_of([grad_core(*grad_x(qkv_b))], [(False, attn_weight.shape, qkv_plan)])
    else:
        input_grad = by_slot(input_grad)
        packed = lax.psum_scatter(packed, FSDP, scatter_dimension=0)
        packed = lax.psum(packed, SEQ)
        g_qkv, g_out, g_up, g_down = (
            scatter_plain(a, g)
            for a, g in ((normed_a, grad_joint), (context, grad_branch), (normed_b, grad_pre), (hidden, grad_out))
        )
        g_qkv = ungrouped([g_qkv[:, : 3 * width // GROUPS], g_qkv[:, 3 * width // GROUPS :]])
    layer_out, input_grad = in_slots(layer_out), in_slots(input_grad)
    (g_gain_a, g_shift_a, g_bias_qv, g_bias_out, g_gain_b, g_shift_b, g_bias_up, g_bias_down) = (
        packed[c : c + n] for c, n in zip(cuts, sizes)
    )
    return (
        layer_out,
        input_grad,
        g_gain_a,
        g_shift_a,
        g_qkv,
        g_bias_qv,
        g_out,
        g_bias_out,
        g_gain_b,
        g_shift_b,
        g_up,
        g_bias_up,
        g_down,
        g_bias_down,
    )


def solution(mesh):
    shard_count, members = mesh.devices.shape
    fine = Mesh(mesh.devices.reshape(shard_count // 2, 2, members // 2, 2), FSDP + SEQ)
    rows, vector, matrix = P(FSDP, SEQ, None), P(FSDP), P(FSDP, None)
    weights = (vector, vector, matrix, vector, matrix, vector, vector, vector, matrix, vector, matrix, vector)
    return jax.shard_map(
        shards,
        mesh=fine,
        in_specs=(rows, vector) + weights + (rows,),
        out_specs=(rows, rows) + weights,
        check_vma=False,
    )
```

```python
import functools

import jax
import jax.numpy as jnp
from jax import lax
from jax.experimental import pallas as pl
from jax.experimental.pallas import tpu as pltpu
from jax.sharding import Mesh
from jax.sharding import PartitionSpec as P

HEAD_DIM = 64
LANES = 128
GROUPS = 2
TILES = 2
EPSILON = 1e-06
BF16 = jnp.bfloat16
F32 = jnp.float32
FSDP, SEQ = ("z", "y"), ("x", "c")


def cost(microseconds, nbytes=0):
    return pl.CostEstimate(flops=int(microseconds * 1.1e9), bytes_accessed=nbytes, transcendentals=0)


def norm_back(grad_norm, gain, normal, inv_std):
    scaled = grad_norm * gain
    return inv_std * (
        scaled
        - jnp.mean(scaled, axis=-1, keepdims=True)
        - normal * jnp.mean(scaled * normal, axis=-1, keepdims=True)
    )


def contract(a, b, ca, cb):
    return lax.dot_general(a, b, (((ca,), (cb,)), ((), ())), preferred_element_type=F32)


def lanes_of(shape):
    lane = lax.broadcasted_iota(jnp.int32, shape, 1)
    return lane // HEAD_DIM, lane % HEAD_DIM


def spread_over(places, place, columns, rest=0.0):
    out = jnp.full(place.shape, rest, F32)
    for i in places:
        out = jnp.where(place == i, columns[i], out)
    return out


def parts_of(value, count):
    parts = []
    for _ in range(count):
        parts.append(value.astype(BF16).astype(F32))
        value = value - parts[-1]
    return parts


SCALE = HEAD_DIM ** (-0.5)


def attend_kernel(bias_ref, q_ref, k_ref, v_ref, out_ref, lse_ref):
    bias = bias_ref[0]
    for tile in range(q_ref.shape[2] // LANES):
        at = slice(tile * LANES, (tile + 1) * LANES)
        q, k, v = (ref[0, :, at].astype(F32) for ref in (q_ref, k_ref, v_ref))
        head_of, place = lanes_of(q.shape)
        context, lse = jnp.zeros(q.shape, F32), jnp.zeros(q.shape, F32)
        for head in range(LANES // HEAD_DIM):
            own = head_of == head
            left = jnp.where(own, q * SCALE, spread_over((0,), place, (1.0,))).astype(BF16)
            right = jnp.where(own, k, spread_over((0,), place, (bias,))).astype(BF16)
            scores = contract(left, right, 1, 1)
            top = jnp.max(scores, axis=-1, keepdims=True)
            exps = jnp.exp(scores - top).astype(BF16)
            both = contract(exps, jnp.where(own, v, 1.0).astype(BF16), 1, 0)
            other = (1 - head) * HEAD_DIM
            total = both[:, other : other + 1]
            context = jnp.where(own, both * (1.0 / total), context)
            lse = jnp.where(own, lse, top + jnp.log(total))
        out_ref[0, :, at] = context.astype(BF16)
        lse_ref[0, :, at] = lse


def attend_back_kernel(bias_ref, q_ref, k_ref, v_ref, lse_ref, context_ref, g_ref, out_ref):
    bias = bias_ref[0]
    tiles = q_ref.shape[2] // LANES
    width = out_ref.shape[2] // 3
    for tile in range(tiles):
        at = slice(tile * LANES, (tile + 1) * LANES)
        q_low, k_low, g_low = q_ref[0, :, at], k_ref[0, :, at], g_ref[0, :, at]
        q, k, v, g, context = (ref[0, :, at].astype(F32) for ref in (q_ref, k_ref, v_ref, g_ref, context_ref))
        head_of, place = lanes_of(q.shape)
        dq, dk, dv = (jnp.zeros(q.shape, F32) for _ in range(3))
        lse_parts = [-part for part in parts_of(lse_ref[0, :, at], 3)] + [1.0]
        product = g * context
        for head in range(LANES // HEAD_DIM):
            own = head_of == head
            left = jnp.where(own, q * SCALE, spread_over(range(4), place, lse_parts)).astype(BF16)
            right = jnp.where(own, k, spread_over(range(4), place, (1.0, 1.0, 1.0, bias))).astype(BF16)
            probs = jnp.exp(contract(left, right, 1, 1))
            inner = jnp.sum(jnp.where(own, product, 0.0), axis=-1, keepdims=True)
            inner_parts = [-part for part in parts_of(inner, 2)]
            left = jnp.where(own, g, spread_over(range(2), place, inner_parts)).astype(BF16)
            right = jnp.where(own, v, spread_over(range(2), place, (1.0, 1.0))).astype(BF16)
            grad_scores = (probs * contract(left, right, 1, 1)).astype(BF16)
            dq = jnp.where(own, contract(grad_scores, k_low, 1, 0), dq)
            dk = jnp.where(own, contract(grad_scores, q_low, 0, 0), dk)
            dv = jnp.where(own, contract(probs.astype(BF16), g_low, 0, 0), dv)
        for block, value in enumerate((dq * SCALE, dk * SCALE, dv)):
            start = block * width + (pl.program_id(1) * tiles + tile) * LANES
            out_ref[0, :, pl.ds(pl.multiple_of(start, LANES), LANES)] = value.astype(BF16)


def attention(key_bias, joint, saved=(), group=0):
    images, slots, width = joint.shape[0], joint.shape[1], joint.shape[2] // 3
    lanes = TILES * LANES
    in_group = width // lanes // GROUPS
    back = len(saved) > 0
    pairs = in_group if back else in_group * GROUPS
    block = (1, slots, lanes)

    def spec(part):
        def index(i, h):
            h = h + group * in_group
            return i, 0, (h // in_group * 3 + part) * in_group + h % in_group

        return pl.BlockSpec(block, index)

    plain = pl.BlockSpec(block, lambda i, h: (i, 0, h + group * in_group))
    bias = pl.BlockSpec((1, slots, 1), lambda i, h: (i, 0, 0))
    whole = pl.BlockSpec((1, slots, 3 * pairs * lanes), lambda i, h: (i, 0, 0))
    shape = lambda columns, kind: jax.ShapeDtypeStruct((images, slots, columns), kind)
    return pl.pallas_call(
        attend_back_kernel if back else attend_kernel,
        grid=(images, pairs),
        in_specs=[bias] + [spec(part) for part in range(3)] + [plain] * len(saved),
        out_specs=whole if back else [plain, plain],
        out_shape=shape(3 * pairs * lanes, BF16) if back else [shape(width, BF16), shape(width, F32)],
        cost_estimate=cost((1.3 if back else 0.8) * images * pairs * TILES),
    )(key_bias, joint, joint, joint, *saved)


STEP = 1024


def stats(values):
    center = values - jnp.mean(values, axis=-1, keepdims=True)
    inv_std = lax.rsqrt(jnp.mean(center * center, axis=-1, keepdims=True) + EPSILON)
    return center * inv_std, inv_std


def column_sums(values):
    return jnp.sum(values, axis=0, keepdims=True)


def block_spec(shape, index=lambda j: 0, at=1):
    def position(j, place):
        value = index(j, place) if index.__code__.co_argcount == 2 else index(j)
        return (0, value) if at else (value, 0)

    return pl.BlockSpec(shape, position)


def whole_spec(array):
    return block_spec(array.shape)


def columns_spec(rows, index=lambda j: j, step=STEP):
    return block_spec((rows, step), index)


class Weight:
    def __init__(self, arrays, by_rows=False, base=0, blocks=None, step=STEP):
        self.arrays, self.by_rows, self.base, self.blocks, self.step = tuple(arrays), by_rows, base, blocks, step

    def specs(self):
        return [pl.BlockSpec(memory_space=pl.ANY)] * len(self.arrays)

    def copies(self, refs, place_ref, j, block, buf, sem):
        copy = lambda source, target: pltpu.make_async_copy(source, target, sem)
        if len(refs) == 1:
            at = pl.ds(pl.multiple_of(block * self.step, self.step), self.step)
            return [(None, [copy(refs[0].at[at] if self.by_rows else refs[0].at[:, at], buf)])]
        y, x, c = place_ref[0], place_ref[1], place_ref[2]
        depth, rows = refs[0].shape[0], refs[0].shape[1]

        def piece(owner, i, z):
            five = refs[5 * owner : 5 * owner + 5]
            if i < 3:
                return five[i].at[z]
            return five[3].at[z] if z < depth // 2 else five[4].at[z - depth // 2]

        found = []
        if not self.by_rows:
            half = self.blocks // 2
            lanes = pl.ds(pl.multiple_of(self.base + block % half * self.step, LANES), self.step)
            for owner in range(2):
                some = []
                for i in range(4):
                    for z in range(depth):
                        row = (2 * z + (y ^ (i // 2))) * 2 * rows + (x ^ (i % 2)) * rows
                        target = buf.at[pl.ds(pl.multiple_of(row, rows), rows)]
                        some.append(copy(piece(owner, i, z).at[:, lanes], target))
                found.append(((block // half == c) == (owner == 0), some))
            return found
        width = buf.shape[1]
        segments = refs[0].shape[2] // width
        for z in range(depth):
            some = []
            for owner in range(2):
                for i in range(4):
                    for k in range(segments):
                        row = (((y ^ (i // 2)) * 2 + (c ^ owner)) * 2 + (x ^ (i % 2))) * segments * rows + k * rows
                        source = piece(owner, i, z).at[:, pl.ds(k * width, width)]
                        some.append(copy(source, buf.at[pl.ds(pl.multiple_of(row, rows), rows)]))
            found.append((j == z, some))
        return found

    def start(self, *where):
        for condition, some in self.copies(*where):
            go = lambda some=some: [one.start() for one in some] and None
            go() if condition is None else pl.when(condition)(go)

    def wait(self, *where):
        for condition, some in self.copies(*where):
            go = lambda some=some: [one.wait() for one in some] and None
            go() if condition is None else pl.when(condition)(go)


def stream(weight, refs, place_ref, buf, sems):
    j = pl.program_id(0)

    def where(step):
        slot = step % 2
        return refs, place_ref, step, step, buf.at[slot], sems.at[slot]

    @pl.when(j == 0)
    def _():
        weight.start(*where(j))

    @pl.when(j + 1 < pl.num_programs(0))
    def _():
        weight.start(*where(j + 1))

    weight.wait(*where(j))
    return buf[j % 2]


def split_refs(refs, weights):
    groups = []
    for weight in weights:
        groups.append(refs[: len(weight.arrays)])
        refs = refs[len(weight.arrays) :]
    return groups, refs


def stepped(kernel, steps, place, weights, in_specs, operands, out_specs, out_shape, scratch, microseconds):
    specs = [spec for weight in weights for spec in weight.specs()]
    arrays = [v for weight in weights for v in weight.arrays]
    return pl.pallas_call(
        functools.partial(kernel, weights),
        grid_spec=pltpu.PrefetchScalarGridSpec(
            num_scalar_prefetch=1,
            grid=(steps,),
            in_specs=specs + in_specs,
            out_specs=out_specs,
            scratch_shapes=scratch,
        ),
        out_shape=out_shape,
        compiler_params=pltpu.CompilerParams(vmem_limit_bytes=56 << 20),
        cost_estimate=cost(microseconds),
    )(place, *arrays, *operands)


def streamed(rows, columns):
    return [pltpu.VMEM((2, rows, columns), BF16), pltpu.SemaphoreType.DMA((2,))]


def project_kernel(weights, place_ref, *refs):
    (weight_refs,), refs = split_refs(refs, weights)
    tokens_ref, gain_ref, shift_ref, query_ref, value_ref, normed_ref, joint_ref, buf, sems = refs

    @pl.when(pl.program_id(0) == 0)
    def _():
        normal, _ = stats(tokens_ref[...].astype(F32))
        normed_ref[...] = (normal * gain_ref[...] + shift_ref[...]).astype(BF16)

    weight = stream(weights[0], weight_refs, place_ref, buf, sems)
    bias = jnp.concatenate([query_ref[...], jnp.zeros_like(query_ref[...]), value_ref[...]], axis=1)
    joint_ref[...] = (contract(normed_ref[...], weight, 1, 0) + bias).astype(BF16)


def project(place, tokens, gain, shift, weight, bias_qv):
    rows, width = tokens.shape
    part = width // GROUPS
    return stepped(
        project_kernel,
        GROUPS,
        place,
        [weight],
        [whole_spec(tokens), whole_spec(gain), whole_spec(shift)]
        + [columns_spec(1, index, part) for index in (lambda j: j, lambda j: GROUPS + j)],
        (tokens, gain, shift, bias_qv, bias_qv),
        [whole_spec(tokens), columns_spec(rows, step=3 * part)],
        [jax.ShapeDtypeStruct((rows, width), BF16), jax.ShapeDtypeStruct((rows, 3 * width), BF16)],
        streamed(width, 3 * part),
        10,
    )


def out_blocks(weight, refs, place_ref, buf, sem):
    for block in range(buf.shape[0]):
        yield weight, (refs, place_ref, 0, block, buf.at[block], sem)


def expand_kernel(weights, place_ref, *refs):
    (up_refs, out_w_refs), refs = split_refs(refs, weights)
    tokens_ref, context_ref, bias_out_ref, gain_ref, shift_ref, bias_ref, *refs = refs
    middle_ref, normed_ref, hidden_ref, slope_ref, buf, sems, out_buf, out_sem = refs

    @pl.when(pl.program_id(0) == 0)
    def _():
        blocks = list(out_blocks(weights[1], out_w_refs, place_ref, out_buf, out_sem))
        for weight, where in blocks:
            weight.start(*where)
        for weight, where in blocks:
            weight.wait(*where)
        context = context_ref[...]
        branch = jnp.concatenate([contract(context, out_buf[b], 1, 0) for b in range(out_buf.shape[0])], axis=1)
        middle = tokens_ref[...].astype(F32) + (branch + bias_out_ref[...])
        middle_ref[...] = middle
        normal, _ = stats(middle)
        normed_ref[...] = (normal * gain_ref[...] + shift_ref[...]).astype(BF16)

    weight = stream(weights[0], up_refs, place_ref, buf, sems)
    pre = contract(normed_ref[...], weight, 1, 0) + bias_ref[...]
    cumul = 0.5 * (1.0 + lax.erf(pre * 0.7071067811865476))
    hidden_ref[...] = (pre * cumul).astype(BF16)
    slope = cumul + pre * (jnp.exp(-0.5 * pre * pre) * 0.3989422804014327)
    slope_ref[...] = slope.astype(BF16)


def expand(place, tokens, context, out_weight, bias_out, gain, shift, up, bias_up):
    rows, width = tokens.shape
    hidden = bias_up.shape[1]
    return stepped(
        expand_kernel,
        hidden // STEP,
        place,
        [up, out_weight],
        [whole_spec(v) for v in (tokens, context, bias_out, gain, shift)] + [columns_spec(1)],
        (tokens, context, bias_out, gain, shift, bias_up),
        [whole_spec(tokens)] * 2 + [columns_spec(rows)] * 2,
        [jax.ShapeDtypeStruct((rows, width), F32), jax.ShapeDtypeStruct((rows, width), BF16)]
        + [jax.ShapeDtypeStruct((rows, hidden), BF16)] * 2,
        streamed(width, STEP) + [pltpu.VMEM((width // out_weight.step, width, out_weight.step), BF16), pltpu.SemaphoreType.DMA],
        20,
    )


def accumulate(total_ref, part, first=None):
    j = pl.program_id(0)

    @pl.when(j == 0)
    def _():
        total_ref[...] = part if first is None else first() + part

    @pl.when(j > 0)
    def _():
        total_ref[...] += part


def finish_kernel(weights, place_ref, *refs):
    (down_refs,), refs = split_refs(refs, weights)
    hidden_ref, middle_ref, bias_ref, valid_ref, result_ref, total_ref, buf, sems = refs
    weight = stream(weights[0], down_refs, place_ref, buf, sems)
    part = contract(hidden_ref[...], weight, 1, 0)
    accumulate(total_ref, part, lambda: middle_ref[...] + bias_ref[...])

    @pl.when(pl.program_id(0) == pl.num_programs(0) - 1)
    def _():
        result_ref[...] = jnp.where(valid_ref[...] > 0.5, total_ref[...], 0.0).astype(BF16)


def finish(place, hidden, down, middle, bias_down, valid):
    rows, width = middle.shape
    return stepped(
        finish_kernel,
        hidden.shape[1] // STEP,
        place,
        [down],
        [columns_spec(rows)] + [whole_spec(v) for v in (middle, bias_down, valid)],
        (hidden, middle, bias_down, valid),
        whole_spec(middle),
        jax.ShapeDtypeStruct((rows, width), BF16),
        [pltpu.VMEM((rows, width), F32)] + streamed(STEP, width),
        11,
    )


def back_kernel(weights, place_ref, *refs):
    (down_refs, up_refs, out_w_refs), refs = split_refs(refs, weights)
    grad_ref, slope_ref, middle_ref, gain_ref, *refs = refs
    pre_ref, bias_up_ref, grad_middle_ref, branch_ref, context_ref, sums_ref, total_ref, *refs = refs
    down_buf, down_sems, up_buf, up_sems, out_buf, out_sem = refs
    j = pl.program_id(0)
    blocks = lambda: out_blocks(weights[2], out_w_refs, place_ref, out_buf, out_sem)

    @pl.when(j == 0)
    def _():
        for weight, where in blocks():
            weight.start(*where)

    down = stream(weights[0], down_refs, place_ref, down_buf, down_sems)
    up = stream(weights[1], up_refs, place_ref, up_buf, up_sems)
    pre = (contract(grad_ref[...], down, 1, 1) * slope_ref[...].astype(F32)).astype(BF16)
    pre_ref[...] = pre
    bias_up_ref[...] = column_sums(pre.astype(F32))
    accumulate(total_ref, contract(pre, up, 1, 1))

    @pl.when(j == pl.num_programs(0) - 1)
    def _():
        for weight, where in blocks():
            weight.wait(*where)
        normal, inv_std = stats(middle_ref[...])
        total = total_ref[...]
        grad_middle = grad_ref[...].astype(F32) + norm_back(total, gain_ref[...], normal, inv_std)
        grad_middle_ref[...] = grad_middle
        branch = grad_middle.astype(BF16)
        branch_ref[...] = branch
        context_ref[...] = sum(
            contract(branch[:, b * out_buf.shape[2] : (b + 1) * out_buf.shape[2]], out_buf[b], 1, 1)
            for b in range(out_buf.shape[0])
        ).astype(BF16)
        sums_ref[0:1] = column_sums(total * normal)
        sums_ref[1:2] = column_sums(total)
        sums_ref[2:3] = column_sums(branch.astype(F32))


def back(place, grad_out, down, slope, up, middle, gain, out_weight):
    rows, width = middle.shape
    hidden = slope.shape[1]
    return stepped(
        back_kernel,
        hidden // STEP,
        place,
        [down, up, out_weight],
        [whole_spec(grad_out), columns_spec(rows), whole_spec(middle), whole_spec(gain)],
        (grad_out, slope, middle, gain),
        [columns_spec(rows), columns_spec(1)]
        + [whole_spec(middle)] * 3
        + [block_spec((8, width))],
        [
            jax.ShapeDtypeStruct((rows, hidden), BF16),
            jax.ShapeDtypeStruct((1, hidden), F32),
            jax.ShapeDtypeStruct((rows, width), F32),
            jax.ShapeDtypeStruct((rows, width), BF16),
            jax.ShapeDtypeStruct((rows, width), BF16),
            jax.ShapeDtypeStruct((8, width), F32),
        ],
        [pltpu.VMEM((rows, width), F32)]
        + streamed(STEP, width)
        + streamed(width, STEP)
        + [pltpu.VMEM((width // out_weight.step, width, out_weight.step), BF16), pltpu.SemaphoreType.DMA],
        23,
    )


def input_kernel(weights, place_ref, *refs):
    (weight_refs,), refs = split_refs(refs, weights)
    joint_0_ref, joint_1_ref, tokens_ref, gain_ref, grad_middle_ref, *refs = refs
    input_ref, bias_ref, sums_ref, total_ref, buf, sems = refs
    j = pl.program_id(0)
    first = jnp.broadcast_to(j == 0, joint_0_ref.shape)
    joint = jnp.where(first, joint_0_ref[...], joint_1_ref[...])
    bias_ref[...] = column_sums(joint.astype(F32))
    weight = stream(weights[0], weight_refs, place_ref, buf, sems)
    accumulate(total_ref, contract(joint, weight, 1, 1))

    @pl.when(j == pl.num_programs(0) - 1)
    def _():
        normal, inv_std = stats(tokens_ref[...].astype(F32))
        total = total_ref[...]
        grad = grad_middle_ref[...] + norm_back(total, gain_ref[...], normal, inv_std)
        input_ref[...] = grad.astype(BF16)
        sums_ref[0:1] = column_sums(total * normal)
        sums_ref[1:2] = column_sums(total)


def back_input(place, joint_0, joint_1, weight, tokens, gain, grad_middle):
    rows, width = tokens.shape
    group = 3 * width // GROUPS
    return stepped(
        input_kernel,
        GROUPS,
        place,
        [weight],
        [whole_spec(v) for v in (joint_0, joint_1, tokens, gain, grad_middle)],
        (joint_0, joint_1, tokens, gain, grad_middle),
        [whole_spec(tokens), columns_spec(1, step=group), block_spec((8, width))],
        [
            jax.ShapeDtypeStruct((rows, width), BF16),
            jax.ShapeDtypeStruct((1, 3 * width), F32),
            jax.ShapeDtypeStruct((8, width), F32),
        ],
        [pltpu.VMEM((rows, width), F32)] + streamed(width, group),
        13,
    )


def grouped(value):
    width = value.shape[-1] // 3
    part = width // GROUPS
    return jnp.concatenate(
        [value[..., t * width + g * part :][..., :part] for g in range(GROUPS) for t in range(3)], axis=-1
    )


def ungrouped(values):
    part = values[0].shape[-1] // 3
    return jnp.concatenate(
        [v[..., t * part : (t + 1) * part] for t in range(3) for v in values], axis=-1
    )


def swap(value, axis):
    return lax.ppermute(value, axis, [(0, 1), (1, 0)])


def send(value, axis, step):
    return lax.ppermute(value, axis, [(i, i ^ step) for i in range(lax.axis_size(axis))])


def pick(blocks, index):
    return lax.dynamic_index_in_dim(blocks, index, 0, keepdims=False)


def tie(*values):
    return lax.optimization_barrier(values)


def after(value, *others):
    return lax.optimization_barrier((value,) + others)[0]


def my_place():
    return jnp.stack([lax.axis_index(n) for n in ("y", "x", "c")]).astype(jnp.int32)


class Split:
    def __init__(self, shard, by_rows=False, columns=None):
        self.shard_rows, self.columns = shard[0], columns or shard[1]
        self.by_rows = by_rows
        self.rows = self.shard_rows // 4 if by_rows else self.shard_rows // 2
        self.wide = self.columns if by_rows else self.columns // 2

def exchange(blocks, axis):
    return lax.all_to_all(blocks, axis, split_axis=0, concat_axis=0, tiled=True)


def pieces_kernel(depth, rows, place_ref, qkv_ref, out_ref, up_ref, down_ref, *refs):
    *vector_refs, first_ref, second_ref, third_ref = refs
    x, c = place_ref[1], place_ref[2]
    at = pl.ds(pl.multiple_of(x * rows, rows), rows)

    def put(ref, lane, value):
        for z in range(depth):
            ref[z, : value.shape[0], lane : lane + value.shape[1]] = value
        return lane + value.shape[1]

    def columns(ref, start, count):
        return ref[at, pl.ds(pl.multiple_of(start, LANES), count)]

    width = out_ref.shape[1]
    part = width // 2
    lane = 0
    for t in range(3):
        lane = put(first_ref, lane, columns(qkv_ref, t * width + c * part, part))
    lane = put(first_ref, lane, columns(out_ref, c * part, part))
    packed = jnp.concatenate([ref[...] for ref in vector_refs], axis=0)
    padding = jnp.zeros((rows - packed.shape[0], LANES), packed.dtype)
    put(first_ref, lane, jnp.concatenate([packed, padding], axis=0))
    half = up_ref.shape[1] // 2
    put(second_ref, 0, columns(up_ref, c * half, half))
    blocks = down_ref.shape[0] // 4 // rows
    lane = 0
    for block in range(blocks):
        start = ((2 * c + x) * blocks + block) * rows
        lane = put(third_ref, lane, down_ref[pl.ds(pl.multiple_of(start, rows), rows), :])


def pieces(qkv, out, up, down, vectors):
    depth, rows = lax.axis_size("z"), qkv.shape[0] // 2
    vectors = [v.reshape(-1, LANES) for v in vectors]
    width = out.shape[1]
    wide = (2 * width + LANES, up.shape[1] // 2, down.shape[0] // 4 // rows * width)
    vmem = pl.BlockSpec(memory_space=pltpu.VMEM)
    return pl.pallas_call(
        functools.partial(pieces_kernel, depth, rows),
        in_specs=[pl.BlockSpec(memory_space=pltpu.SMEM)] + [vmem] * (4 + len(vectors)),
        out_specs=[vmem] * 3,
        out_shape=[jax.ShapeDtypeStruct((depth, rows, n), BF16) for n in wide],
        cost_estimate=cost(3),
    )(my_place(), qkv, out, up, down, *vectors)


def corner(from_x, from_y):
    half = from_x.shape[0] // 2
    return swap(from_x[:half], "y"), swap(from_y[half:], "x")


def core_swap(*pieces):
    return tuple(swap(v, "c") for v in pieces)


def my_place():
    return jnp.stack([lax.axis_index(n) for n in ("y", "x", "c")]).astype(jnp.int32)


def part_refs(x, near, far, rows, refs, at):
    own_ref, to_x_ref, to_y_ref, corner_ref = refs
    low, high = near[:rows], near[rows:]
    own_ref[at] = jnp.where(x == 0, low, high)
    to_x_ref[at] = jnp.where(x == 0, high, low)
    low, high = far[:rows], far[rows:]
    to_y_ref[at] = jnp.where(x == 0, low, high)
    corner_ref[at] = jnp.where(x == 0, high, low)


def grad_columns_kernel(ends, cut, place_ref, *refs):
    y, x = place_ref[0], place_ref[1]
    out_refs, turned_ref = refs[-5:-1], refs[-1]
    j = pl.program_id(0)

    def one(first, a_ref, a_sib_ref, g_ref, g_sib_ref):
        @pl.when(j == first)
        def _():
            turned_ref[0] = a_ref[...].T
            turned_ref[1] = a_sib_ref[...].T

        total = contract(turned_ref[0], g_ref[...], 1, 0) + contract(turned_ref[1], g_sib_ref[...], 1, 0)
        total = total.reshape(-1, 2, cut.shard_rows, total.shape[1])
        for z in range(total.shape[0]):
            near = jnp.where(y == 0, total[z, 0], total[z, 1]).astype(BF16)
            far = jnp.where(y == 0, total[z, 1], total[z, 0]).astype(BF16)
            part_refs(x, near, far, cut.rows, out_refs, z)

    if len(ends) == 1:
        one(0, *refs[:4])
        return
    for i, end in enumerate(ends):
        first = 0 if i == 0 else ends[i - 1]
        pl.when((j >= first) & (j < end))(functools.partial(one, first, *refs[4 * i : 4 * i + 4]))


def grad_rows_kernel(cut, place_ref, a0_ref, a1_ref, a0_sib_ref, a1_sib_ref, g_ref, g_sib_ref, *out_refs):
    y, x = place_ref[0], place_ref[1]
    by_y = [
        contract(ref[...], g_ref[...], 0, 0)
        + contract(sib_ref[...], g_sib_ref[...], 0, 0)
        for ref, sib_ref in ((a0_ref, a0_sib_ref), (a1_ref, a1_sib_ref))
    ]
    near = jnp.where(y == 0, by_y[0], by_y[1]).astype(BF16)
    far = jnp.where(y == 0, by_y[1], by_y[0]).astype(BF16)
    part_refs(x, near, far, cut.rows, out_refs, 0)


def grad_parts(jobs, cut, depth, step=512):
    tokens = jobs[0][0].shape[0]
    specs, operands, ends = [], [], []
    if cut.by_rows:
        ((a, a_sib, g, g_sib, _, _),) = jobs
        half = 2 * cut.rows
        every = pl.BlockSpec((tokens, cut.wide), lambda j, place: (0, 0))
        specs = [
            pl.BlockSpec((tokens, half), lambda j, place: (0, 4 * j + place[2])),
            pl.BlockSpec((tokens, half), lambda j, place: (0, 4 * j + 2 + place[2])),
            pl.BlockSpec((tokens, half), lambda j, place: (0, 4 * j + place[2])),
            pl.BlockSpec((tokens, half), lambda j, place: (0, 4 * j + 2 + place[2])),
            every,
            every,
        ]
        operands, kernel, grid, wide = [a, a, a_sib, a_sib, g, g_sib], functools.partial(grad_rows_kernel, cut), depth, cut.wide
        out_spec = lambda n: pl.BlockSpec((1, n, wide), lambda j, place: (j, 0, 0))
    else:
        grid = 0
        for a, a_sib, g, g_sib, start, steps in jobs:
            in_half = g.shape[1] // 2 // step
            every = pl.BlockSpec((tokens, a.shape[1]), lambda j, place: (0, 0))
            at = lambda j, first=grid, steps=steps: jnp.clip(j - first, 0, steps - 1)
            specs += [
                every,
                every,
            ] + [
                pl.BlockSpec(
                    (tokens, step), lambda j, place, at=at, n=in_half, s=start: (0, place[2] * n + s + at(j))
                )
            ] * 2
            operands += [a, a_sib, g, g_sib]
            grid += steps
            ends.append(grid)
        kernel, wide = functools.partial(grad_columns_kernel, ends, cut), grid * step
        out_spec = lambda n: pl.BlockSpec((depth, n, step), lambda j, place: (0, 0, j))
    total = 8 * depth * cut.rows * wide
    return pl.pallas_call(
        kernel,
        grid_spec=pltpu.PrefetchScalarGridSpec(
            num_scalar_prefetch=1,
            grid=(grid,),
            in_specs=specs,
            out_specs=[out_spec(cut.rows)] * 4,
            scratch_shapes=[] if cut.by_rows else [pltpu.VMEM((2, jobs[0][0].shape[1], tokens), BF16)],
        ),
        out_shape=[jax.ShapeDtypeStruct((depth, cut.rows, wide), BF16)] * 4,
        compiler_params=pltpu.CompilerParams(vmem_limit_bytes=52 << 20),
        cost_estimate=cost(total * 2.2e-6),
    )(my_place(), *operands)


def add(one, other):
    return (one.astype(F32) + other.astype(F32)).astype(BF16)


def grad_z(parts, from_x, from_y):
    return exchange(sum(v.astype(F32) for v in (parts[0], from_x, from_y)).astype(BF16), "z")


def grad_x(blocks):
    mine = jnp.sum(blocks.astype(F32), axis=0).astype(BF16)
    return mine, swap(mine, "x")


def grad_core(mine, from_x):
    return mine, from_x, swap(mine, "c"), swap(from_x, "c")


def shard_kernel(plan, place_ref, *refs):
    x, c = place_ref[1], place_ref[2]
    parts, out_refs = refs[: -len(plan)], refs[-len(plan) :]
    for (by_rows, sources), out_ref in zip(plan, out_refs):
        column = 0
        for core in range(2):
            for number, start, count, at in sources:
                four = parts[4 * number : 4 * number + 4]
                rows = four[0].shape[0]
                for half in range(2):
                    both = [
                        jnp.where(c == core, four[i][:, start : start + count], four[2 + i][:, start : start + count])
                        for i in range(2)
                    ]
                    value = jnp.where(x == half, both[0], both[1]).astype(F32)
                    if by_rows:
                        row = (2 * core + half) * rows
                        out_ref[row : row + rows, :] = value
                    else:
                        out_ref[half * rows : (half + 1) * rows, at[core] : at[core] + count] = value


def shards_of(gradients, plan):
    parts = [v for gradient in gradients for v in gradient]
    vmem = pl.BlockSpec(memory_space=pltpu.VMEM)
    return pl.pallas_call(
        functools.partial(shard_kernel, [(by_rows, sources) for by_rows, _, sources in plan]),
        in_specs=[pl.BlockSpec(memory_space=pltpu.SMEM)] + [vmem] * len(parts),
        out_specs=[vmem] * len(plan),
        out_shape=[jax.ShapeDtypeStruct(shape, F32) for _, shape, _ in plan],
        cost_estimate=cost(2),
    )(my_place(), *parts)


def pack_kernel(sums_a_ref, joint_ref, sums_b_ref, up_ref, down_ref, out_ref):
    shards = out_ref.shape[0]
    width = down_ref.shape[1]
    part = width // GROUPS

    def put(at, count, source):
        for i in range(shards):
            out_ref[i : i + 1, at : at + count] = source(i, count)
        return at + count

    def plain(ref, row):
        return lambda i, n: ref[row : row + 1, i * n : (i + 1) * n]

    def query_value(i, n):
        value, at = divmod(i * n, width)
        group, at = divmod(at, part)
        start = (3 * group + 2 * value) * part + at
        return joint_ref[0:1, start : start + n]

    n = width // shards
    at = put(0, n, plain(sums_a_ref, 0))
    at = put(at, n, plain(sums_a_ref, 1))
    at = put(at, 2 * n, query_value)
    at = put(at, n, plain(sums_b_ref, 2))
    at = put(at, n, plain(sums_b_ref, 0))
    at = put(at, n, plain(sums_b_ref, 1))
    at = put(at, up_ref.shape[1] // shards, plain(up_ref, 0))
    put(at, n, plain(down_ref, 0))


def pack(shards, sums_a, joint_sums, sums_b, up_sums, down_sums):
    vmem = pl.BlockSpec(memory_space=pltpu.VMEM)
    columns = (9 - 1) * down_sums.shape[1] + up_sums.shape[1]
    return pl.pallas_call(
        pack_kernel,
        in_specs=[vmem] * 5,
        out_specs=vmem,
        out_shape=jax.ShapeDtypeStruct((shards, columns // shards), F32),
        cost_estimate=cost(1),
    )(sums_a, joint_sums, sums_b, up_sums, down_sums)


def in_order(index, mine, theirs, axis):
    first, second = jnp.where(index == 0, mine, theirs), jnp.where(index == 0, theirs, mine)
    return jnp.concatenate([first, second], axis=axis)


def order_vectors(own_y, other_y):
    y = lax.axis_index("y")
    rows = [jnp.where(y == 0, own_y, other_y), jnp.where(y == 0, other_y, own_y)]
    return jnp.stack(rows, axis=1).reshape(2 * own_y.shape[0], -1)


def over_rows(packed):
    y = lax.axis_index("y")
    packed = packed.reshape(lax.axis_size("z"), 2, -1)
    row = lambda yy: lax.dynamic_index_in_dim(packed, yy, 1, keepdims=False)
    return row(y) + swap(row(1 - y), "y")


def over_line(packed):
    z = lax.axis_index("z")
    return pick(packed, z) + sum(send(pick(packed, z ^ k), "z", k) for k in range(1, lax.axis_size("z")))


def scatter_plain(a, g):
    grad = lax.psum_scatter(contract(a, g, 0, 0).astype(BF16), FSDP, scatter_dimension=0, tiled=True)
    return lax.psum(grad, SEQ).astype(F32)


def shards(
    tokens,
    lengths,
    attn_gain,
    attn_shift,
    attn_weight,
    attn_bias,
    out_weight,
    out_bias,
    mlp_gain,
    mlp_shift,
    up_weight,
    up_bias,
    down_weight,
    down_bias,
    cotangent,
):
    width = tokens.shape[2]
    members = lax.axis_size(SEQ)
    staged = lax.axis_size("z") <= 8 and attn_weight.shape[0] % 128 == 0
    images = tokens.shape[0] // members
    slots = tokens.shape[1] * members
    rows = images * slots

    small = (attn_gain, attn_shift, attn_bias, out_bias, mlp_gain, mlp_shift, up_bias, down_bias)
    sizes = [v.shape[0] for v in small]
    cuts = [sum(sizes[:i]) for i in range(len(sizes))]
    packed = jnp.concatenate(small)

    few = tokens.shape[1]
    here = lax.axis_index(SEQ)
    lens = lax.dynamic_slice_in_dim(lengths, here * images, images, 0)
    slot = jnp.arange(slots, dtype=jnp.int32)
    slot = (slot // few ^ here) * few + slot % few
    valid = slot[None, :] < lens[:, None]
    key_bias = jnp.where(valid, 0.0, -1000000000.0)[:, :, None]
    valid = valid.reshape(rows, 1)

    def by_image(value, which=range(members)):
        value = value.reshape(members, images, few, width)
        return [send(pick(value, here ^ k), SEQ, k) if k else pick(value, here) for k in which]

    def by_slot(*values):
        value = jnp.concatenate([v.reshape(images, members, few, width) for v in values])
        return [send(value[:, k], SEQ, k) if k else value[:, 0] for k in range(members)]

    def in_images(blocks):
        return jnp.stack(blocks, axis=1).reshape(rows, width)

    def in_slots(blocks):
        blocks = jnp.stack(blocks)
        kinds = blocks.shape[1] // images
        blocks = jnp.concatenate([pick(blocks, here ^ k).reshape(kinds, images, few, width) for k in range(members)], axis=1)
        return [blocks[i] for i in range(kinds)]

    def unpack(vectors):
        vectors = vectors.astype(F32)
        return [vectors[:, c : c + n].reshape(1, -1) for c, n in zip(cuts, sizes)]

    if staged:
        cut_qkv, cut_out, cut_up = (Split(w.shape) for w in (attn_weight, out_weight, up_weight))
        cut_down = Split(down_weight.shape, by_rows=True)
        cut_group = Split(attn_weight.shape, columns=3 * width // GROUPS)
        place = my_place()
        first, second, third = pieces(attn_weight, out_weight, up_weight, down_weight, small)
        cot = by_image(cotangent, range(members - 1))
        tokens, cot, cotangent, z1, second, third = tie(
            by_image(tokens), cot, cotangent, exchange(first, "z"), second, third
        )
        tokens = in_images(tokens)
        x1, y1 = swap(z1, "x"), swap(z1, "y")
        z2 = exchange(second, "z")
        x1, y1, z1, third = tie(x1, y1, z1, third)
        vec_z, vec_y = (v[:, : sum(sizes) // LANES, -LANES:].reshape(v.shape[0], -1) for v in (z1, y1))
        vectors = unpack(order_vectors(vec_z, vec_y))
        d1, c1, z2, vectors, third = tie(corner(x1, y1), core_swap(z1, x1, y1), z2, vectors, third)
        gain_a, shift_a, bias_qv, bias_out, gain_b, shift_b, bias_up, bias_down = vectors
        arrays = (z1, x1, y1, *d1, *c1, *core_swap(*d1))
        qkv_full = Weight(arrays, blocks=GROUPS, step=3 * width // GROUPS)
        out_full = Weight(arrays, base=cut_qkv.wide, blocks=2, step=cut_out.wide)
        x2, y2 = swap(z2, "x"), swap(z2, "y")
        normed_a, joint = project(place, tokens, gain_a, shift_a, qkv_full, bias_qv)
        joint, third = tie(joint, third)
        z3 = exchange(third, "z")
        joint, x2, y2, z2, normed_a, cotangent = tie(joint, x2, y2, z2, normed_a, cotangent)
        joint = joint.reshape(images, slots, 3 * width)
        d2, c2 = corner(x2, y2), core_swap(z2, x2, y2)
        context, lse = attention(key_bias, joint)
        context, d2, c2, z3, cot = tie(
            context.reshape(rows, width), d2, c2, z3, cot + by_image(cotangent, [members - 1])
        )
        cot = in_images(cot)
        x3, y3 = swap(z3, "x"), swap(z3, "y")
        up_full = Weight((z2, x2, y2, *d2, *c2, *core_swap(*d2)), blocks=cut_up.columns // STEP)
        middle, normed_b, hidden, slope = expand(
            place, tokens, context, out_full, bias_out, gain_b, shift_b, up_full, bias_up
        )
        grad_out = jnp.where(valid, cot, jnp.zeros_like(cot))
        hidden, slope, x3, y3, z3, normed_sib, out_sib = tie(
            hidden, slope, x3, y3, z3, swap(normed_a, "c"), swap(grad_out, "c")
        )
    else:
        vectors = unpack(lax.all_gather(packed, FSDP, axis=0))
        gain_a, shift_a, bias_qv, bias_out, gain_b, shift_b, bias_up, bias_down = vectors
        place = jnp.zeros((3,), jnp.int32)
        qkv_full, out_full, up_full, down_full = (
            Weight([lax.all_gather(w, FSDP, axis=0, tiled=True)], by_rows=w is down_weight)
            for w in (grouped(attn_weight), out_weight, up_weight, down_weight)
        )
        qkv_full.step, out_full.step = 3 * width // GROUPS, width // 2
        tokens = in_images(by_image(tokens))
        cot = in_images(by_image(cotangent))
        grad_out = jnp.where(valid, cot, jnp.zeros_like(cot))
        normed_a, joint = project(place, tokens, gain_a, shift_a, qkv_full, bias_qv)
        joint = joint.reshape(images, slots, 3 * width)
        context, lse = attention(key_bias, joint)
        context = context.reshape(rows, width)
        middle, normed_b, hidden, slope = expand(
            place, tokens, context, out_full, bias_out, gain_b, shift_b, up_full, bias_up
        )

    g_bias_down = jnp.sum(grad_out.astype(F32), axis=0, keepdims=True)
    valid_wide = valid.astype(F32)

    def back_attention(grad_context, group):
        saved = (lse, context.reshape(images, slots, width), grad_context)
        grad = attention(key_bias, joint, saved, group)
        return grad.reshape(rows, 3 * width // GROUPS)

    shard_count = lax.axis_size(FSDP)
    depth = lax.axis_size("z")
    if staged:
        d3, c3 = corner(x3, y3), core_swap(z3, x3, y3)
        down_parts = grad_parts([(hidden, swap(hidden, "c"), grad_out, out_sib, 0, 0)], cut_down, depth)
        down_parts, slope, d3, c3, hidden = tie(down_parts, slope, d3, c3, hidden)
        down_full = Weight((z3, x3, y3, *d3, *c3, *core_swap(*d3)), by_rows=True)
        down_e = swap(down_parts[3], "y")
        grad_pre, bias_up_sums, grad_middle, grad_branch, grad_context, sums_b = back(
            place, grad_out, down_full, slope, up_full, middle, gain_b, out_full
        )
        grad_pre, down_e, grad_context, grad_branch, context_sib, normed_sib_b = tie(
            grad_pre, down_e, grad_context, grad_branch, swap(context, "c"), swap(normed_b, "c")
        )
        grad_context = grad_context.reshape(images, slots, width)
        pre_sib, branch_sib = swap(grad_pre, "c"), swap(grad_branch, "c")
        down_x, down_y = swap(add(down_parts[1], down_e), "x"), swap(down_parts[2], "y")
        joint_0 = back_attention(grad_context, 0)
        joint_0, grad_context, pre_sib, branch_sib = tie(joint_0, grad_context, pre_sib, branch_sib)
        half = cut_up.wide // 512 // 2
        up_job = (normed_b, normed_sib_b, grad_pre, pre_sib)
        a_parts = grad_parts([up_job + (0, half)], cut_up, depth)
        joint_0_sib = swap(joint_0, "c")
        a_parts, grad_context = tie(a_parts, grad_context)
        a_e = swap(a_parts[3], "y")
        out_job = (context, context_sib, grad_branch, branch_sib, 0, cut_out.wide // 512)
        b_parts = grad_parts([up_job + (half, half), out_job], cut_up, depth)
        b_parts, grad_context, a_e, down_x, down_y = tie(b_parts, grad_context, a_e, down_x, down_y)
        a_x, a_y = swap(add(a_parts[1], a_e), "x"), swap(a_parts[2], "y")
        b_e = swap(b_parts[3], "y")
        down_b = grad_z(down_parts, down_x, down_y)
        qkv_job = lambda joint, sib: [(normed_a, normed_sib, joint, sib, 0, 1)]
        parts_0 = grad_parts(qkv_job(joint_0, joint_0_sib), cut_group, depth, cut_group.wide)
        parts_0, grad_context = tie(parts_0, grad_context)
        e_0 = swap(parts_0[3], "x")
        joint_1 = back_attention(grad_context, 1)
        joint_1, e_0, a_x, a_y, b_e, down_b, hidden = tie(joint_1, e_0, a_x, a_y, b_e, down_b, hidden)
        b_x, b_y = swap(add(b_parts[1], b_e), "x"), swap(b_parts[2], "y")
        a_z = grad_z(a_parts, a_x, a_y)
        x_0, y_0 = swap(parts_0[1], "x"), swap(add(parts_0[2], e_0), "y")
        parts_1 = grad_parts(qkv_job(joint_1, swap(joint_1, "c")), cut_group, depth, cut_group.wide)
        parts_1, joint_1 = tie(parts_1, joint_1)
        e_1 = swap(parts_1[3], "y")
        input_grad, joint_sums, sums_a = back_input(place, joint_0, joint_1, qkv_full, tokens, gain_a, grad_middle)
        packed = pack(shard_count, sums_a, joint_sums, sums_b, bias_up_sums, g_bias_down)
        input_grad, e_1, x_0, y_0, b_x, b_y, a_z, hidden, down_b, packed = tie(
            input_grad, e_1, x_0, y_0, b_x, b_y, a_z, hidden, down_b, packed
        )
        x_1, y_1 = swap(add(parts_1[1], e_1), "x"), swap(parts_1[2], "y")
        b_z = grad_z(b_parts, b_x, b_y)
        result = finish(place, hidden, down_full, middle, bias_down, valid_wide)
    else:
        grad_pre, bias_up_sums, grad_middle, grad_branch, grad_context, sums_b = back(
            place,
            grad_out, down_full, slope, up_full, middle, gain_b, out_full
        )
        grad_context = grad_context.reshape(images, slots, width)
        joint_0, joint_1 = (back_attention(grad_context, g) for g in range(GROUPS))
        input_grad, joint_sums, sums_a = back_input(place, joint_0, joint_1, qkv_full, tokens, gain_a, grad_middle)
        grad_joint = jnp.concatenate([joint_0, joint_1], axis=1)
        result = finish(place, hidden, down_full, middle, bias_down, valid_wide)

    if not staged:
        group = 3 * width // GROUPS
        joint_sums = ungrouped([joint_sums[:, g * group : (g + 1) * group] for g in range(GROUPS)])
        g_bias_qv = jnp.concatenate([joint_sums[:, :width], joint_sums[:, 2 * width :]], axis=1)
        small_grads = (sums_a[0], sums_a[1], g_bias_qv, sums_b[2], sums_b[0], sums_b[1], bias_up_sums, g_bias_down)
        packed = jnp.concatenate([v.reshape(shard_count, -1) for v in small_grads], axis=1)
    if staged:
        packed = packed + swap(packed, "c")
        packed = packed + swap(packed, "x")
        x_1, y_1, b_z, result, input_grad, packed, a_g, down_g = tie(
            x_1, y_1, b_z, result, input_grad, packed, grad_x(a_z), grad_x(down_b)
        )
        qkv_b = grad_z(
            tuple(jnp.concatenate([p, q], axis=2) for p, q in zip(parts_0[:1], parts_1[:1])),
            jnp.concatenate([x_0, x_1], axis=2),
            jnp.concatenate([y_0, y_1], axis=2),
        )
        outs = by_slot(input_grad, result)
        early, late = outs[:-1], outs[-1]
        qkv_b, b_g, packed, a_g, down_g, early = tie(qkv_b, grad_x(b_z), over_rows(packed), a_g, down_g, early)
        b_g, a_g, down_g = (grad_core(*v) for v in (b_g, a_g, down_g))
        mine, from_x = grad_x(qkv_b)
        half, n_out, n_qkv = cut_up.wide // 2, cut_out.wide, cut_group.wide
        up_plan = [(0, 0, half, (0, 2 * half)), (1, 0, half, (half, 3 * half))]
        g_up, g_out, g_down = shards_of(
            (a_g, b_g, down_g),
            [
                (False, up_weight.shape, up_plan),
                (False, out_weight.shape, [(1, half, n_out, (0, n_out))]),
                (True, down_weight.shape, [(2, 0, width, None)]),
            ],
        )
        g_up, g_out, g_down, packed, late, from_x = tie(g_up, g_out, g_down, packed, late, from_x)
        outs = early + [late]
        qkv_g = grad_core(mine, from_x)
        packed = over_line(packed)
        part = width // GROUPS
        qkv_plan = []
        for g in range(GROUPS):
            for low in range(0, n_qkv, LANES):
                places = [divmod(c * n_qkv + low, part) for c in range(2)]
                places = [t * width + g * part + at for t, at in places]
                qkv_plan.append((0, g * n_qkv + low, LANES, places))
        (g_qkv,) = shards_of([qkv_g], [(False, attn_weight.shape, qkv_plan)])
    else:
        outs = by_slot(input_grad, result)
        packed = lax.psum_scatter(packed, FSDP, scatter_dimension=0)
        packed = lax.psum(packed, SEQ)
        g_qkv, g_out, g_up, g_down = (
            scatter_plain(a, g)
            for a, g in ((normed_a, grad_joint), (context, grad_branch), (normed_b, grad_pre), (hidden, grad_out))
        )
        g_qkv = ungrouped([g_qkv[:, : 3 * width // GROUPS], g_qkv[:, 3 * width // GROUPS :]])
    input_grad, layer_out = in_slots(outs)
    (g_gain_a, g_shift_a, g_bias_qv, g_bias_out, g_gain_b, g_shift_b, g_bias_up, g_bias_down) = (
        packed[c : c + n] for c, n in zip(cuts, sizes)
    )
    return (
        layer_out,
        input_grad,
        g_gain_a,
        g_shift_a,
        g_qkv,
        g_bias_qv,
        g_out,
        g_bias_out,
        g_gain_b,
        g_shift_b,
        g_up,
        g_bias_up,
        g_down,
        g_bias_down,
    )


def solution(mesh):
    shard_count, members = mesh.devices.shape
    fine = Mesh(mesh.devices.reshape(shard_count // 2, 2, members // 2, 2), FSDP + SEQ)
    rows, vector, matrix = P(FSDP, SEQ, None), P(FSDP), P(FSDP, None)
    weights = (vector, vector, matrix, vector, matrix, vector, vector, vector, matrix, vector, matrix, vector)
    return jax.shard_map(
        shards,
        mesh=fine,
        in_specs=(rows, vector) + weights + (rows,),
        out_specs=(rows, rows) + weights,
        check_vma=False,
    )
```

```python
import functools

import jax
import jax.numpy as jnp
from jax import lax
from jax.experimental import pallas as pl
from jax.experimental.pallas import tpu as pltpu
from jax.sharding import Mesh
from jax.sharding import PartitionSpec as P

HEAD_DIM = 64
LANES = 128
GROUPS = 2
TILES = 2
EPSILON = 1e-06
BF16 = jnp.bfloat16
F32 = jnp.float32
FSDP, SEQ = ("z", "y"), ("x", "c")


def cost(microseconds, nbytes=0):
    return pl.CostEstimate(flops=int(microseconds * 1.1e9), bytes_accessed=nbytes, transcendentals=0)


def norm_back(grad_norm, gain, normal, inv_std):
    scaled = grad_norm * gain
    return inv_std * (
        scaled
        - jnp.mean(scaled, axis=-1, keepdims=True)
        - normal * jnp.mean(scaled * normal, axis=-1, keepdims=True)
    )


def contract(a, b, ca, cb):
    return lax.dot_general(a, b, (((ca,), (cb,)), ((), ())), preferred_element_type=F32)


def lanes_of(shape):
    lane = lax.broadcasted_iota(jnp.int32, shape, 1)
    return lane // HEAD_DIM, lane % HEAD_DIM


def spread_over(places, place, columns, rest=0.0):
    out = jnp.full(place.shape, rest, F32)
    for i in places:
        out = jnp.where(place == i, columns[i], out)
    return out


def parts_of(value, count):
    parts = []
    for _ in range(count):
        parts.append(value.astype(BF16).astype(F32))
        value = value - parts[-1]
    return parts


SCALE = HEAD_DIM ** (-0.5)


def attend_kernel(bias_ref, q_ref, k_ref, v_ref, out_ref, lse_ref):
    bias = bias_ref[0]
    for tile in range(q_ref.shape[2] // LANES):
        at = slice(tile * LANES, (tile + 1) * LANES)
        q, k, v = (ref[0, :, at].astype(F32) for ref in (q_ref, k_ref, v_ref))
        head_of, place = lanes_of(q.shape)
        context, lse = jnp.zeros(q.shape, F32), jnp.zeros(q.shape, F32)
        for head in range(LANES // HEAD_DIM):
            own = head_of == head
            left = jnp.where(own, q * SCALE, spread_over((0,), place, (1.0,))).astype(BF16)
            right = jnp.where(own, k, spread_over((0,), place, (bias,))).astype(BF16)
            scores = contract(left, right, 1, 1)
            top = jnp.max(scores, axis=-1, keepdims=True)
            exps = jnp.exp(scores - top).astype(BF16)
            both = contract(exps, jnp.where(own, v, 1.0).astype(BF16), 1, 0)
            other = (1 - head) * HEAD_DIM
            total = both[:, other : other + 1]
            context = jnp.where(own, both * (1.0 / total), context)
            lse = jnp.where(own, lse, top + jnp.log(total))
        out_ref[0, :, at] = context.astype(BF16)
        lse_ref[0, :, at] = lse


def attend_back_kernel(bias_ref, q_ref, k_ref, v_ref, lse_ref, context_ref, g_ref, out_ref):
    bias = bias_ref[0]
    tiles = q_ref.shape[2] // LANES
    width = out_ref.shape[2] // 3
    for tile in range(tiles):
        at = slice(tile * LANES, (tile + 1) * LANES)
        q_low, k_low, g_low = q_ref[0, :, at], k_ref[0, :, at], g_ref[0, :, at]
        q, k, v, g, context = (ref[0, :, at].astype(F32) for ref in (q_ref, k_ref, v_ref, g_ref, context_ref))
        head_of, place = lanes_of(q.shape)
        dq, dk, dv = (jnp.zeros(q.shape, F32) for _ in range(3))
        lse_parts = [-part for part in parts_of(lse_ref[0, :, at], 3)] + [1.0]
        product = g * context
        for head in range(LANES // HEAD_DIM):
            own = head_of == head
            left = jnp.where(own, q * SCALE, spread_over(range(4), place, lse_parts)).astype(BF16)
            right = jnp.where(own, k, spread_over(range(4), place, (1.0, 1.0, 1.0, bias))).astype(BF16)
            probs = jnp.exp(contract(left, right, 1, 1))
            inner = jnp.sum(jnp.where(own, product, 0.0), axis=-1, keepdims=True)
            inner_parts = [-part for part in parts_of(inner, 2)]
            left = jnp.where(own, g, spread_over(range(2), place, inner_parts)).astype(BF16)
            right = jnp.where(own, v, spread_over(range(2), place, (1.0, 1.0))).astype(BF16)
            grad_scores = (probs * contract(left, right, 1, 1)).astype(BF16)
            dq = jnp.where(own, contract(grad_scores, k_low, 1, 0), dq)
            dk = jnp.where(own, contract(grad_scores, q_low, 0, 0), dk)
            dv = jnp.where(own, contract(probs.astype(BF16), g_low, 0, 0), dv)
        for block, value in enumerate((dq * SCALE, dk * SCALE, dv)):
            start = block * width + (pl.program_id(1) * tiles + tile) * LANES
            out_ref[0, :, pl.ds(pl.multiple_of(start, LANES), LANES)] = value.astype(BF16)


def attention(key_bias, joint, saved=(), group=0):
    images, slots, width = joint.shape[0], joint.shape[1], joint.shape[2] // 3
    lanes = TILES * LANES
    in_group = width // lanes // GROUPS
    back = len(saved) > 0
    pairs = in_group if back else in_group * GROUPS
    block = (1, slots, lanes)

    def spec(part):
        def index(i, h):
            h = h + group * in_group
            return i, 0, (h // in_group * 3 + part) * in_group + h % in_group

        return pl.BlockSpec(block, index)

    plain = pl.BlockSpec(block, lambda i, h: (i, 0, h + group * in_group))
    bias = pl.BlockSpec((1, slots, 1), lambda i, h: (i, 0, 0))
    whole = pl.BlockSpec((1, slots, 3 * pairs * lanes), lambda i, h: (i, 0, 0))
    shape = lambda columns, kind: jax.ShapeDtypeStruct((images, slots, columns), kind)
    return pl.pallas_call(
        attend_back_kernel if back else attend_kernel,
        grid=(images, pairs),
        in_specs=[bias] + [spec(part) for part in range(3)] + [plain] * len(saved),
        out_specs=whole if back else [plain, plain],
        out_shape=shape(3 * pairs * lanes, BF16) if back else [shape(width, BF16), shape(width, F32)],
        cost_estimate=cost((1.3 if back else 0.8) * images * pairs * TILES),
    )(key_bias, joint, joint, joint, *saved)


STEP = 1024


def stats(values):
    center = values - jnp.mean(values, axis=-1, keepdims=True)
    inv_std = lax.rsqrt(jnp.mean(center * center, axis=-1, keepdims=True) + EPSILON)
    return center * inv_std, inv_std


def column_sums(values):
    return jnp.sum(values, axis=0, keepdims=True)


def block_spec(shape, index=lambda j: 0, at=1):
    def position(j, place):
        value = index(j, place) if index.__code__.co_argcount == 2 else index(j)
        return (0, value) if at else (value, 0)

    return pl.BlockSpec(shape, position)


def whole_spec(array):
    return block_spec(array.shape)


def columns_spec(rows, index=lambda j: j, step=STEP):
    return block_spec((rows, step), index)


class Weight:
    def __init__(self, arrays, by_rows=False, base=0, blocks=None, step=STEP):
        self.arrays, self.by_rows, self.base, self.blocks, self.step = tuple(arrays), by_rows, base, blocks, step

    def specs(self):
        return [pl.BlockSpec(memory_space=pl.ANY)] * len(self.arrays)

    def copies(self, refs, place_ref, j, block, buf, sem):
        copy = lambda source, target: pltpu.make_async_copy(source, target, sem)
        if len(refs) == 1:
            at = pl.ds(pl.multiple_of(block * self.step, self.step), self.step)
            return [(None, [copy(refs[0].at[at] if self.by_rows else refs[0].at[:, at], buf)])]
        y, x, c = place_ref[0], place_ref[1], place_ref[2]
        depth, rows = refs[0].shape[0], refs[0].shape[1]

        def piece(owner, i, z):
            five = refs[5 * owner : 5 * owner + 5]
            if i < 3:
                return five[i].at[z]
            return five[3].at[z] if z < depth // 2 else five[4].at[z - depth // 2]

        found = []
        if not self.by_rows:
            half = self.blocks // 2
            lanes = pl.ds(pl.multiple_of(self.base + block % half * self.step, LANES), self.step)
            for owner in range(2):
                some = []
                for i in range(4):
                    for z in range(depth):
                        row = (2 * z + (y ^ (i // 2))) * 2 * rows + (x ^ (i % 2)) * rows
                        target = buf.at[pl.ds(pl.multiple_of(row, rows), rows)]
                        some.append(copy(piece(owner, i, z).at[:, lanes], target))
                found.append(((block // half == c) == (owner == 0), some))
            return found
        width = buf.shape[1]
        segments = refs[0].shape[2] // width
        for z in range(depth):
            some = []
            for owner in range(2):
                for i in range(4):
                    for k in range(segments):
                        row = (((y ^ (i // 2)) * 2 + (c ^ owner)) * 2 + (x ^ (i % 2))) * segments * rows + k * rows
                        source = piece(owner, i, z).at[:, pl.ds(k * width, width)]
                        some.append(copy(source, buf.at[pl.ds(pl.multiple_of(row, rows), rows)]))
            found.append((j == z, some))
        return found

    def start(self, *where):
        for condition, some in self.copies(*where):
            go = lambda some=some: [one.start() for one in some] and None
            go() if condition is None else pl.when(condition)(go)

    def wait(self, *where):
        for condition, some in self.copies(*where):
            go = lambda some=some: [one.wait() for one in some] and None
            go() if condition is None else pl.when(condition)(go)


def stream(weight, refs, place_ref, buf, sems):
    j = pl.program_id(0)

    def where(step):
        slot = step % 2
        return refs, place_ref, step, step, buf.at[slot], sems.at[slot]

    @pl.when(j == 0)
    def _():
        weight.start(*where(j))

    @pl.when(j + 1 < pl.num_programs(0))
    def _():
        weight.start(*where(j + 1))

    weight.wait(*where(j))
    return buf[j % 2]


def split_refs(refs, weights):
    groups = []
    for weight in weights:
        groups.append(refs[: len(weight.arrays)])
        refs = refs[len(weight.arrays) :]
    return groups, refs


def stepped(kernel, steps, place, weights, in_specs, operands, out_specs, out_shape, scratch, microseconds):
    specs = [spec for weight in weights for spec in weight.specs()]
    arrays = [v for weight in weights for v in weight.arrays]
    return pl.pallas_call(
        functools.partial(kernel, weights),
        grid_spec=pltpu.PrefetchScalarGridSpec(
            num_scalar_prefetch=1,
            grid=(steps,),
            in_specs=specs + in_specs,
            out_specs=out_specs,
            scratch_shapes=scratch,
        ),
        out_shape=out_shape,
        compiler_params=pltpu.CompilerParams(vmem_limit_bytes=56 << 20),
        cost_estimate=cost(microseconds),
    )(place, *arrays, *operands)


def streamed(rows, columns):
    return [pltpu.VMEM((2, rows, columns), BF16), pltpu.SemaphoreType.DMA((2,))]


def project_kernel(weights, place_ref, *refs):
    (weight_refs,), refs = split_refs(refs, weights)
    tokens_ref, gain_ref, shift_ref, query_ref, value_ref, normed_ref, joint_ref, buf, sems = refs

    @pl.when(pl.program_id(0) == 0)
    def _():
        normal, _ = stats(tokens_ref[...].astype(F32))
        normed_ref[...] = (normal * gain_ref[...] + shift_ref[...]).astype(BF16)

    weight = stream(weights[0], weight_refs, place_ref, buf, sems)
    bias = jnp.concatenate([query_ref[...], jnp.zeros_like(query_ref[...]), value_ref[...]], axis=1)
    joint_ref[...] = (contract(normed_ref[...], weight, 1, 0) + bias).astype(BF16)


def project(place, tokens, gain, shift, weight, bias_qv):
    rows, width = tokens.shape
    part = width // GROUPS
    return stepped(
        project_kernel,
        GROUPS,
        place,
        [weight],
        [whole_spec(tokens), whole_spec(gain), whole_spec(shift)]
        + [columns_spec(1, index, part) for index in (lambda j: j, lambda j: GROUPS + j)],
        (tokens, gain, shift, bias_qv, bias_qv),
        [whole_spec(tokens), columns_spec(rows, step=3 * part)],
        [jax.ShapeDtypeStruct((rows, width), BF16), jax.ShapeDtypeStruct((rows, 3 * width), BF16)],
        streamed(width, 3 * part),
        10,
    )


def out_blocks(weight, refs, place_ref, buf, sem):
    for block in range(buf.shape[0]):
        yield weight, (refs, place_ref, 0, block, buf.at[block], sem)


def expand_kernel(weights, place_ref, *refs):
    (up_refs, out_w_refs), refs = split_refs(refs, weights)
    tokens_ref, context_ref, bias_out_ref, gain_ref, shift_ref, bias_ref, *refs = refs
    middle_ref, normed_ref, hidden_ref, slope_ref, other_ref, buf, sems, out_buf, out_sem = refs

    @pl.when(pl.program_id(0) == 0)
    def _():
        blocks = list(out_blocks(weights[1], out_w_refs, place_ref, out_buf, out_sem))
        for weight, where in blocks:
            weight.start(*where)
        for weight, where in blocks:
            weight.wait(*where)
        context = context_ref[...]
        branch = jnp.concatenate([contract(context, out_buf[b], 1, 0) for b in range(out_buf.shape[0])], axis=1)
        middle = tokens_ref[...].astype(F32) + (branch + bias_out_ref[...])
        middle_ref[...] = middle
        normal, _ = stats(middle)
        normed_ref[...] = (normal * gain_ref[...] + shift_ref[...]).astype(BF16)

    weight = stream(weights[0], up_refs, place_ref, buf, sems)
    pre = contract(normed_ref[...], weight, 1, 0) + bias_ref[...]
    cumul = 0.5 * (1.0 + lax.erf(pre * 0.7071067811865476))
    hidden = (pre * cumul).astype(BF16)
    hidden_ref[...] = hidden
    half = 2 * LANES
    for i in range(other_ref.shape[1] // half):
        low, high = (hidden[:, (2 * i + k) * half : (2 * i + k + 1) * half] for k in range(2))
        other_ref[:, i * half : (i + 1) * half] = jnp.where(place_ref[2] == 0, high, low)
    slope = cumul + pre * (jnp.exp(-0.5 * pre * pre) * 0.3989422804014327)
    slope_ref[...] = slope.astype(BF16)


def expand(place, tokens, context, out_weight, bias_out, gain, shift, up, bias_up):
    rows, width = tokens.shape
    hidden = bias_up.shape[1]
    return stepped(
        expand_kernel,
        hidden // STEP,
        place,
        [up, out_weight],
        [whole_spec(v) for v in (tokens, context, bias_out, gain, shift)] + [columns_spec(1)],
        (tokens, context, bias_out, gain, shift, bias_up),
        [whole_spec(tokens)] * 2 + [columns_spec(rows)] * 2 + [columns_spec(rows, step=STEP // 2)],
        [jax.ShapeDtypeStruct((rows, width), F32), jax.ShapeDtypeStruct((rows, width), BF16)]
        + [jax.ShapeDtypeStruct((rows, n), BF16) for n in (hidden, hidden, hidden // 2)],
        streamed(width, STEP) + [pltpu.VMEM((width // out_weight.step, width, out_weight.step), BF16), pltpu.SemaphoreType.DMA],
        20,
    )


def accumulate(total_ref, part, first=None):
    j = pl.program_id(0)

    @pl.when(j == 0)
    def _():
        total_ref[...] = part if first is None else first() + part

    @pl.when(j > 0)
    def _():
        total_ref[...] += part


def finish_kernel(weights, place_ref, *refs):
    (down_refs,), refs = split_refs(refs, weights)
    hidden_ref, middle_ref, bias_ref, valid_ref, result_ref, total_ref, buf, sems = refs
    weight = stream(weights[0], down_refs, place_ref, buf, sems)
    part = contract(hidden_ref[...], weight, 1, 0)
    accumulate(total_ref, part, lambda: middle_ref[...] + bias_ref[...])

    @pl.when(pl.program_id(0) == pl.num_programs(0) - 1)
    def _():
        result_ref[...] = jnp.where(valid_ref[...] > 0.5, total_ref[...], 0.0).astype(BF16)


def finish(place, hidden, down, middle, bias_down, valid):
    rows, width = middle.shape
    return stepped(
        finish_kernel,
        hidden.shape[1] // STEP,
        place,
        [down],
        [columns_spec(rows)] + [whole_spec(v) for v in (middle, bias_down, valid)],
        (hidden, middle, bias_down, valid),
        whole_spec(middle),
        jax.ShapeDtypeStruct((rows, width), BF16),
        [pltpu.VMEM((rows, width), F32)] + streamed(STEP, width),
        11,
    )


def back_kernel(weights, place_ref, *refs):
    (down_refs, up_refs, out_w_refs), refs = split_refs(refs, weights)
    grad_ref, slope_ref, middle_ref, gain_ref, *refs = refs
    pre_ref, bias_up_ref, grad_middle_ref, branch_ref, context_ref, sums_ref, total_ref, *refs = refs
    down_buf, down_sems, up_buf, up_sems, out_buf, out_sem = refs
    j = pl.program_id(0)
    blocks = lambda: out_blocks(weights[2], out_w_refs, place_ref, out_buf, out_sem)

    @pl.when(j == 0)
    def _():
        for weight, where in blocks():
            weight.start(*where)

    down = stream(weights[0], down_refs, place_ref, down_buf, down_sems)
    up = stream(weights[1], up_refs, place_ref, up_buf, up_sems)
    pre = (contract(grad_ref[...], down, 1, 1) * slope_ref[...].astype(F32)).astype(BF16)
    pre_ref[...] = pre
    bias_up_ref[...] = column_sums(pre.astype(F32))
    accumulate(total_ref, contract(pre, up, 1, 1))

    @pl.when(j == pl.num_programs(0) - 1)
    def _():
        for weight, where in blocks():
            weight.wait(*where)
        normal, inv_std = stats(middle_ref[...])
        total = total_ref[...]
        grad_middle = grad_ref[...].astype(F32) + norm_back(total, gain_ref[...], normal, inv_std)
        grad_middle_ref[...] = grad_middle
        branch = grad_middle.astype(BF16)
        branch_ref[...] = branch
        context_ref[...] = sum(
            contract(branch[:, b * out_buf.shape[2] : (b + 1) * out_buf.shape[2]], out_buf[b], 1, 1)
            for b in range(out_buf.shape[0])
        ).astype(BF16)
        sums_ref[0:1] = column_sums(total * normal)
        sums_ref[1:2] = column_sums(total)
        sums_ref[2:3] = column_sums(branch.astype(F32))


def back(place, grad_out, down, slope, up, middle, gain, out_weight):
    rows, width = middle.shape
    hidden = slope.shape[1]
    return stepped(
        back_kernel,
        hidden // STEP,
        place,
        [down, up, out_weight],
        [whole_spec(grad_out), columns_spec(rows), whole_spec(middle), whole_spec(gain)],
        (grad_out, slope, middle, gain),
        [columns_spec(rows), columns_spec(1)]
        + [whole_spec(middle)] * 3
        + [block_spec((8, width))],
        [
            jax.ShapeDtypeStruct((rows, hidden), BF16),
            jax.ShapeDtypeStruct((1, hidden), F32),
            jax.ShapeDtypeStruct((rows, width), F32),
            jax.ShapeDtypeStruct((rows, width), BF16),
            jax.ShapeDtypeStruct((rows, width), BF16),
            jax.ShapeDtypeStruct((8, width), F32),
        ],
        [pltpu.VMEM((rows, width), F32)]
        + streamed(STEP, width)
        + streamed(width, STEP)
        + [pltpu.VMEM((width // out_weight.step, width, out_weight.step), BF16), pltpu.SemaphoreType.DMA],
        23,
    )


def input_kernel(weights, place_ref, *refs):
    (weight_refs,), refs = split_refs(refs, weights)
    joint_0_ref, joint_1_ref, tokens_ref, gain_ref, grad_middle_ref, *refs = refs
    input_ref, bias_ref, sums_ref, total_ref, buf, sems = refs
    j = pl.program_id(0)
    first = jnp.broadcast_to(j == 0, joint_0_ref.shape)
    joint = jnp.where(first, joint_0_ref[...], joint_1_ref[...])
    bias_ref[...] = column_sums(joint.astype(F32))
    weight = stream(weights[0], weight_refs, place_ref, buf, sems)
    accumulate(total_ref, contract(joint, weight, 1, 1))

    @pl.when(j == pl.num_programs(0) - 1)
    def _():
        normal, inv_std = stats(tokens_ref[...].astype(F32))
        total = total_ref[...]
        grad = grad_middle_ref[...] + norm_back(total, gain_ref[...], normal, inv_std)
        input_ref[...] = grad.astype(BF16)
        sums_ref[0:1] = column_sums(total * normal)
        sums_ref[1:2] = column_sums(total)


def back_input(place, joint_0, joint_1, weight, tokens, gain, grad_middle):
    rows, width = tokens.shape
    group = 3 * width // GROUPS
    return stepped(
        input_kernel,
        GROUPS,
        place,
        [weight],
        [whole_spec(v) for v in (joint_0, joint_1, tokens, gain, grad_middle)],
        (joint_0, joint_1, tokens, gain, grad_middle),
        [whole_spec(tokens), columns_spec(1, step=group), block_spec((8, width))],
        [
            jax.ShapeDtypeStruct((rows, width), BF16),
            jax.ShapeDtypeStruct((1, 3 * width), F32),
            jax.ShapeDtypeStruct((8, width), F32),
        ],
        [pltpu.VMEM((rows, width), F32)] + streamed(width, group),
        13,
    )


def grouped(value):
    width = value.shape[-1] // 3
    part = width // GROUPS
    return jnp.concatenate(
        [value[..., t * width + g * part :][..., :part] for g in range(GROUPS) for t in range(3)], axis=-1
    )


def ungrouped(values):
    part = values[0].shape[-1] // 3
    return jnp.concatenate(
        [v[..., t * part : (t + 1) * part] for t in range(3) for v in values], axis=-1
    )


def swap(value, axis):
    return lax.ppermute(value, axis, [(0, 1), (1, 0)])


def send(value, axis, step):
    return lax.ppermute(value, axis, [(i, i ^ step) for i in range(lax.axis_size(axis))])


def pick(blocks, index):
    return lax.dynamic_index_in_dim(blocks, index, 0, keepdims=False)


def tie(*values):
    return lax.optimization_barrier(values)


def after(value, *others):
    return lax.optimization_barrier((value,) + others)[0]


def my_place():
    return jnp.stack([lax.axis_index(n) for n in ("y", "x", "c")]).astype(jnp.int32)


class Split:
    def __init__(self, shard, by_rows=False, columns=None):
        self.shard_rows, self.columns = shard[0], columns or shard[1]
        self.by_rows = by_rows
        self.rows = self.shard_rows // 4 if by_rows else self.shard_rows // 2
        self.wide = self.columns if by_rows else self.columns // 2

def exchange(blocks, axis):
    return lax.all_to_all(blocks, axis, split_axis=0, concat_axis=0, tiled=True)


def pieces_kernel(depth, rows, place_ref, qkv_ref, out_ref, up_ref, down_ref, *refs):
    *vector_refs, first_ref, second_ref, third_ref = refs
    x, c = place_ref[1], place_ref[2]
    at = pl.ds(pl.multiple_of(x * rows, rows), rows)

    def put(ref, lane, value):
        for z in range(depth):
            ref[z, : value.shape[0], lane : lane + value.shape[1]] = value
        return lane + value.shape[1]

    def columns(ref, start, count):
        return ref[at, pl.ds(pl.multiple_of(start, LANES), count)]

    width = out_ref.shape[1]
    part = width // 2
    lane = 0
    for t in range(3):
        lane = put(first_ref, lane, columns(qkv_ref, t * width + c * part, part))
    lane = put(first_ref, lane, columns(out_ref, c * part, part))
    packed = jnp.concatenate([ref[...] for ref in vector_refs], axis=0)
    padding = jnp.zeros((rows - packed.shape[0], LANES), packed.dtype)
    put(first_ref, lane, jnp.concatenate([packed, padding], axis=0))
    half = up_ref.shape[1] // 2
    put(second_ref, 0, columns(up_ref, c * half, half))
    blocks = down_ref.shape[0] // 4 // rows
    lane = 0
    for block in range(blocks):
        start = ((2 * c + x) * blocks + block) * rows
        lane = put(third_ref, lane, down_ref[pl.ds(pl.multiple_of(start, rows), rows), :])


def pieces(qkv, out, up, down, vectors):
    depth, rows = lax.axis_size("z"), qkv.shape[0] // 2
    vectors = [v.reshape(-1, LANES) for v in vectors]
    width = out.shape[1]
    wide = (2 * width + LANES, up.shape[1] // 2, down.shape[0] // 4 // rows * width)
    vmem = pl.BlockSpec(memory_space=pltpu.VMEM)
    return pl.pallas_call(
        functools.partial(pieces_kernel, depth, rows),
        in_specs=[pl.BlockSpec(memory_space=pltpu.SMEM)] + [vmem] * (4 + len(vectors)),
        out_specs=[vmem] * 3,
        out_shape=[jax.ShapeDtypeStruct((depth, rows, n), BF16) for n in wide],
        cost_estimate=cost(3),
    )(my_place(), qkv, out, up, down, *vectors)


def corner(from_x, from_y):
    half = from_x.shape[0] // 2
    return swap(from_x[:half], "y"), swap(from_y[half:], "x")


def core_swap(*pieces):
    return tuple(swap(v, "c") for v in pieces)


def my_place():
    return jnp.stack([lax.axis_index(n) for n in ("y", "x", "c")]).astype(jnp.int32)


def part_refs(x, near, far, rows, refs, at):
    own_ref, to_x_ref, to_y_ref, corner_ref = refs
    low, high = near[:rows], near[rows:]
    own_ref[at] = jnp.where(x == 0, low, high)
    to_x_ref[at] = jnp.where(x == 0, high, low)
    low, high = far[:rows], far[rows:]
    to_y_ref[at] = jnp.where(x == 0, low, high)
    corner_ref[at] = jnp.where(x == 0, high, low)


def grad_columns_kernel(ends, cut, place_ref, *refs):
    y, x = place_ref[0], place_ref[1]
    out_refs, turned_ref = refs[-5:-1], refs[-1]
    j = pl.program_id(0)

    def one(first, a_ref, a_sib_ref, g_ref, g_sib_ref):
        @pl.when(j == first)
        def _():
            turned_ref[0] = a_ref[...].T
            turned_ref[1] = a_sib_ref[...].T

        total = contract(turned_ref[0], g_ref[...], 1, 0) + contract(turned_ref[1], g_sib_ref[...], 1, 0)
        total = total.reshape(-1, 2, cut.shard_rows, total.shape[1])
        for z in range(total.shape[0]):
            near = jnp.where(y == 0, total[z, 0], total[z, 1]).astype(BF16)
            far = jnp.where(y == 0, total[z, 1], total[z, 0]).astype(BF16)
            part_refs(x, near, far, cut.rows, out_refs, z)

    if len(ends) == 1:
        one(0, *refs[:4])
        return
    for i, end in enumerate(ends):
        first = 0 if i == 0 else ends[i - 1]
        pl.when((j >= first) & (j < end))(functools.partial(one, first, *refs[4 * i : 4 * i + 4]))


def grad_rows_kernel(cut, place_ref, a0_ref, a1_ref, a0_sib_ref, a1_sib_ref, g_ref, g_sib_ref, *out_refs):
    y, x = place_ref[0], place_ref[1]
    by_y = [
        contract(ref[...], g_ref[...], 0, 0)
        + contract(sib_ref[...], g_sib_ref[...], 0, 0)
        for ref, sib_ref in ((a0_ref, a0_sib_ref), (a1_ref, a1_sib_ref))
    ]
    near = jnp.where(y == 0, by_y[0], by_y[1]).astype(BF16)
    far = jnp.where(y == 0, by_y[1], by_y[0]).astype(BF16)
    part_refs(x, near, far, cut.rows, out_refs, 0)


def grad_parts(jobs, cut, depth, step=512):
    tokens = jobs[0][0].shape[0]
    specs, operands, ends = [], [], []
    if cut.by_rows:
        ((a, a_sib, g, g_sib, _, _),) = jobs
        half = 2 * cut.rows
        every = pl.BlockSpec((tokens, cut.wide), lambda j, place: (0, 0))
        specs = [
            pl.BlockSpec((tokens, half), lambda j, place: (0, 4 * j + place[2])),
            pl.BlockSpec((tokens, half), lambda j, place: (0, 4 * j + 2 + place[2])),
            pl.BlockSpec((tokens, half), lambda j, place: (0, 2 * j)),
            pl.BlockSpec((tokens, half), lambda j, place: (0, 2 * j + 1)),
            every,
            every,
        ]
        operands, kernel, grid, wide = [a, a, a_sib, a_sib, g, g_sib], functools.partial(grad_rows_kernel, cut), depth, cut.wide
        out_spec = lambda n: pl.BlockSpec((1, n, wide), lambda j, place: (j, 0, 0))
    else:
        grid = 0
        for a, a_sib, g, g_sib, start, steps in jobs:
            in_half = g.shape[1] // 2 // step
            every = pl.BlockSpec((tokens, a.shape[1]), lambda j, place: (0, 0))
            at = lambda j, first=grid, steps=steps: jnp.clip(j - first, 0, steps - 1)
            specs += [
                every,
                every,
            ] + [
                pl.BlockSpec(
                    (tokens, step), lambda j, place, at=at, n=in_half, s=start: (0, place[2] * n + s + at(j))
                )
            ] * 2
            operands += [a, a_sib, g, g_sib]
            grid += steps
            ends.append(grid)
        kernel, wide = functools.partial(grad_columns_kernel, ends, cut), grid * step
        out_spec = lambda n: pl.BlockSpec((depth, n, step), lambda j, place: (0, 0, j))
    total = 8 * depth * cut.rows * wide
    return pl.pallas_call(
        kernel,
        grid_spec=pltpu.PrefetchScalarGridSpec(
            num_scalar_prefetch=1,
            grid=(grid,),
            in_specs=specs,
            out_specs=[out_spec(cut.rows)] * 4,
            scratch_shapes=[] if cut.by_rows else [pltpu.VMEM((2, jobs[0][0].shape[1], tokens), BF16)],
        ),
        out_shape=[jax.ShapeDtypeStruct((depth, cut.rows, wide), BF16)] * 4,
        compiler_params=pltpu.CompilerParams(vmem_limit_bytes=52 << 20),
        cost_estimate=cost(total * 2.2e-6),
    )(my_place(), *operands)


def add(one, other):
    return (one.astype(F32) + other.astype(F32)).astype(BF16)


def grad_z(parts, from_x, from_y):
    return exchange(sum(v.astype(F32) for v in (parts[0], from_x, from_y)).astype(BF16), "z")


def grad_x(blocks):
    mine = jnp.sum(blocks.astype(F32), axis=0).astype(BF16)
    return mine, swap(mine, "x")


def grad_core(mine, from_x):
    return mine, from_x, swap(mine, "c"), swap(from_x, "c")


def shard_kernel(plan, place_ref, *refs):
    x, c = place_ref[1], place_ref[2]
    parts, out_refs = refs[: -len(plan)], refs[-len(plan) :]
    for (by_rows, sources), out_ref in zip(plan, out_refs):
        column = 0
        for core in range(2):
            for number, start, count, at in sources:
                four = parts[4 * number : 4 * number + 4]
                rows = four[0].shape[0]
                for half in range(2):
                    both = [
                        jnp.where(c == core, four[i][:, start : start + count], four[2 + i][:, start : start + count])
                        for i in range(2)
                    ]
                    value = jnp.where(x == half, both[0], both[1]).astype(F32)
                    if by_rows:
                        row = (2 * core + half) * rows
                        out_ref[row : row + rows, :] = value
                    else:
                        out_ref[half * rows : (half + 1) * rows, at[core] : at[core] + count] = value


def shards_of(gradients, plan):
    parts = [v for gradient in gradients for v in gradient]
    vmem = pl.BlockSpec(memory_space=pltpu.VMEM)
    return pl.pallas_call(
        functools.partial(shard_kernel, [(by_rows, sources) for by_rows, _, sources in plan]),
        in_specs=[pl.BlockSpec(memory_space=pltpu.SMEM)] + [vmem] * len(parts),
        out_specs=[vmem] * len(plan),
        out_shape=[jax.ShapeDtypeStruct(shape, F32) for _, shape, _ in plan],
        cost_estimate=cost(2),
    )(my_place(), *parts)


def pack_kernel(sums_a_ref, joint_ref, sums_b_ref, up_ref, down_ref, out_ref):
    shards = out_ref.shape[0]
    width = down_ref.shape[1]
    part = width // GROUPS

    def put(at, count, source):
        for i in range(shards):
            out_ref[i : i + 1, at : at + count] = source(i, count)
        return at + count

    def plain(ref, row):
        return lambda i, n: ref[row : row + 1, i * n : (i + 1) * n]

    def query_value(i, n):
        value, at = divmod(i * n, width)
        group, at = divmod(at, part)
        start = (3 * group + 2 * value) * part + at
        return joint_ref[0:1, start : start + n]

    n = width // shards
    at = put(0, n, plain(sums_a_ref, 0))
    at = put(at, n, plain(sums_a_ref, 1))
    at = put(at, 2 * n, query_value)
    at = put(at, n, plain(sums_b_ref, 2))
    at = put(at, n, plain(sums_b_ref, 0))
    at = put(at, n, plain(sums_b_ref, 1))
    at = put(at, up_ref.shape[1] // shards, plain(up_ref, 0))
    put(at, n, plain(down_ref, 0))


def pack(shards, sums_a, joint_sums, sums_b, up_sums, down_sums):
    vmem = pl.BlockSpec(memory_space=pltpu.VMEM)
    columns = (9 - 1) * down_sums.shape[1] + up_sums.shape[1]
    return pl.pallas_call(
        pack_kernel,
        in_specs=[vmem] * 5,
        out_specs=vmem,
        out_shape=jax.ShapeDtypeStruct((shards, columns // shards), F32),
        cost_estimate=cost(1),
    )(sums_a, joint_sums, sums_b, up_sums, down_sums)


def in_order(index, mine, theirs, axis):
    first, second = jnp.where(index == 0, mine, theirs), jnp.where(index == 0, theirs, mine)
    return jnp.concatenate([first, second], axis=axis)


def order_vectors(own_y, other_y):
    y = lax.axis_index("y")
    rows = [jnp.where(y == 0, own_y, other_y), jnp.where(y == 0, other_y, own_y)]
    return jnp.stack(rows, axis=1).reshape(2 * own_y.shape[0], -1)


def over_rows(packed):
    y = lax.axis_index("y")
    packed = packed.reshape(lax.axis_size("z"), 2, -1)
    row = lambda yy: lax.dynamic_index_in_dim(packed, yy, 1, keepdims=False)
    return row(y) + swap(row(1 - y), "y")


def over_line(packed):
    z = lax.axis_index("z")
    return pick(packed, z) + sum(send(pick(packed, z ^ k), "z", k) for k in range(1, lax.axis_size("z")))


def scatter_plain(a, g):
    grad = lax.psum_scatter(contract(a, g, 0, 0).astype(BF16), FSDP, scatter_dimension=0, tiled=True)
    return lax.psum(grad, SEQ).astype(F32)


def shards(
    tokens,
    lengths,
    attn_gain,
    attn_shift,
    attn_weight,
    attn_bias,
    out_weight,
    out_bias,
    mlp_gain,
    mlp_shift,
    up_weight,
    up_bias,
    down_weight,
    down_bias,
    cotangent,
):
    width = tokens.shape[2]
    members = lax.axis_size(SEQ)
    staged = lax.axis_size("z") <= 8 and attn_weight.shape[0] % 128 == 0
    images = tokens.shape[0] // members
    slots = tokens.shape[1] * members
    rows = images * slots

    small = (attn_gain, attn_shift, attn_bias, out_bias, mlp_gain, mlp_shift, up_bias, down_bias)
    sizes = [v.shape[0] for v in small]
    cuts = [sum(sizes[:i]) for i in range(len(sizes))]
    packed = jnp.concatenate(small)

    few = tokens.shape[1]
    here = lax.axis_index(SEQ)
    lens = lax.dynamic_slice_in_dim(lengths, here * images, images, 0)
    slot = jnp.arange(slots, dtype=jnp.int32)
    slot = (slot // few ^ here) * few + slot % few
    valid = slot[None, :] < lens[:, None]
    key_bias = jnp.where(valid, 0.0, -1000000000.0)[:, :, None]
    valid = valid.reshape(rows, 1)

    def by_image(value, which=range(members)):
        value = value.reshape(members, images, few, width)
        return [send(pick(value, here ^ k), SEQ, k) if k else pick(value, here) for k in which]

    def by_slot(*values):
        value = jnp.concatenate([v.reshape(images, members, few, width) for v in values])
        return [send(value[:, k], SEQ, k) if k else value[:, 0] for k in range(members)]

    def in_images(blocks):
        return jnp.stack(blocks, axis=1).reshape(rows, width)

    def in_slots(blocks):
        blocks = jnp.stack(blocks)
        kinds = blocks.shape[1] // images
        blocks = jnp.concatenate([pick(blocks, here ^ k).reshape(kinds, images, few, width) for k in range(members)], axis=1)
        return [blocks[i] for i in range(kinds)]

    def unpack(vectors):
        vectors = vectors.astype(F32)
        return [vectors[:, c : c + n].reshape(1, -1) for c, n in zip(cuts, sizes)]

    if staged:
        cut_qkv, cut_out, cut_up = (Split(w.shape) for w in (attn_weight, out_weight, up_weight))
        cut_down = Split(down_weight.shape, by_rows=True)
        cut_group = Split(attn_weight.shape, columns=3 * width // GROUPS)
        place = my_place()
        first, second, third = pieces(attn_weight, out_weight, up_weight, down_weight, small)
        cot = by_image(cotangent, range(members - 1))
        tokens, cot, cotangent, z1, second, third = tie(
            by_image(tokens), cot, cotangent, exchange(first, "z"), second, third
        )
        tokens = in_images(tokens)
        x1, y1 = swap(z1, "x"), swap(z1, "y")
        z2 = exchange(second, "z")
        x1, y1, z1, third = tie(x1, y1, z1, third)
        vec_z, vec_y = (v[:, : sum(sizes) // LANES, -LANES:].reshape(v.shape[0], -1) for v in (z1, y1))
        vectors = unpack(order_vectors(vec_z, vec_y))
        d1, c1, z2, vectors, third, tokens = tie(
            corner(x1, y1), core_swap(z1, x1, y1), z2, vectors, third, tokens
        )
        gain_a, shift_a, bias_qv, bias_out, gain_b, shift_b, bias_up, bias_down = vectors
        arrays = (z1, x1, y1, *d1, *c1, *core_swap(*d1))
        qkv_full = Weight(arrays, blocks=GROUPS, step=3 * width // GROUPS)
        out_full = Weight(arrays, base=cut_qkv.wide, blocks=2, step=cut_out.wide)
        x2, y2 = swap(z2, "x"), swap(z2, "y")
        normed_a, joint = project(place, tokens, gain_a, shift_a, qkv_full, bias_qv)
        joint, third = tie(joint, third)
        z3 = exchange(third, "z")
        joint, x2, y2, c_z2, normed_a, cotangent = tie(joint, x2, y2, swap(z2, "c"), normed_a, cotangent)
        joint = joint.reshape(images, slots, 3 * width)
        d2, c2 = corner(x2, y2), (c_z2, *core_swap(x2, y2))
        context, lse = attention(key_bias, joint)
        context, d2, c2, z3, cot = tie(
            context.reshape(rows, width), d2, c2, z3, cot + by_image(cotangent, [members - 1])
        )
        cot = in_images(cot)
        x3, y3 = swap(z3, "x"), swap(z3, "y")
        up_full = Weight((z2, x2, y2, *d2, *c2, *core_swap(*d2)), blocks=cut_up.columns // STEP)
        middle, normed_b, hidden, slope, hidden_other = expand(
            place, tokens, context, out_full, bias_out, gain_b, shift_b, up_full, bias_up
        )
        grad_out = jnp.where(valid, cot, jnp.zeros_like(cot))
        hidden, hidden_other, slope, x3, y3, c_z3, grad_out, out_sib = tie(
            hidden, hidden_other, slope, x3, y3, swap(z3, "c"), grad_out, swap(grad_out, "c")
        )
    else:
        vectors = unpack(lax.all_gather(packed, FSDP, axis=0))
        gain_a, shift_a, bias_qv, bias_out, gain_b, shift_b, bias_up, bias_down = vectors
        place = jnp.zeros((3,), jnp.int32)
        qkv_full, out_full, up_full, down_full = (
            Weight([lax.all_gather(w, FSDP, axis=0, tiled=True)], by_rows=w is down_weight)
            for w in (grouped(attn_weight), out_weight, up_weight, down_weight)
        )
        qkv_full.step, out_full.step = 3 * width // GROUPS, width // 2
        tokens = in_images(by_image(tokens))
        cot = in_images(by_image(cotangent))
        grad_out = jnp.where(valid, cot, jnp.zeros_like(cot))
        normed_a, joint = project(place, tokens, gain_a, shift_a, qkv_full, bias_qv)
        joint = joint.reshape(images, slots, 3 * width)
        context, lse = attention(key_bias, joint)
        context = context.reshape(rows, width)
        middle, normed_b, hidden, slope, hidden_other = expand(
            place, tokens, context, out_full, bias_out, gain_b, shift_b, up_full, bias_up
        )

    g_bias_down = jnp.sum(grad_out.astype(F32), axis=0, keepdims=True)
    valid_wide = valid.astype(F32)

    def back_attention(grad_context, group):
        saved = (lse, context.reshape(images, slots, width), grad_context)
        grad = attention(key_bias, joint, saved, group)
        return grad.reshape(rows, 3 * width // GROUPS)

    shard_count = lax.axis_size(FSDP)
    depth = lax.axis_size("z")
    if staged:
        d3, c3 = corner(x3, y3), (c_z3, *core_swap(x3, y3))
        down_parts = grad_parts([(hidden, swap(hidden_other, "c"), grad_out, out_sib, 0, 0)], cut_down, depth)
        down_parts, slope, d3, c3, hidden, g_bias_down, valid_wide = tie(
            down_parts, slope, d3, c3, hidden, g_bias_down, valid_wide
        )
        down_full = Weight((z3, x3, y3, *d3, *c3, *core_swap(*d3)), by_rows=True)
        down_e = swap(down_parts[3], "y")
        grad_pre, bias_up_sums, grad_middle, grad_branch, grad_context, sums_b = back(
            place, grad_out, down_full, slope, up_full, middle, gain_b, out_full
        )
        grad_pre, down_e, grad_context, grad_branch, context_sib, normed_sib_b, normed_sib = tie(
            grad_pre, down_e, grad_context, grad_branch, swap(context, "c"), swap(normed_b, "c"), swap(normed_a, "c")
        )
        grad_context = grad_context.reshape(images, slots, width)
        pre_sib, branch_sib = swap(grad_pre, "c"), swap(grad_branch, "c")
        down_x, down_y = swap(add(down_parts[1], down_e), "x"), swap(down_parts[2], "y")
        joint_0 = back_attention(grad_context, 0)
        joint_0, grad_context, pre_sib, branch_sib = tie(joint_0, grad_context, pre_sib, branch_sib)
        half = cut_up.wide // 512 // 2
        up_job = (normed_b, normed_sib_b, grad_pre, pre_sib)
        a_parts = grad_parts([up_job + (0, half)], cut_up, depth)
        joint_0_sib = swap(joint_0, "c")
        a_parts, grad_context = tie(a_parts, grad_context)
        a_e = swap(a_parts[3], "y")
        out_job = (context, context_sib, grad_branch, branch_sib, 0, cut_out.wide // 512)
        b_parts = grad_parts([up_job + (half, half), out_job], cut_up, depth)
        b_parts, grad_context, a_e, down_x, down_y = tie(b_parts, grad_context, a_e, down_x, down_y)
        a_x, a_y = swap(add(a_parts[1], a_e), "x"), swap(a_parts[2], "y")
        b_e = swap(b_parts[3], "y")
        down_b = grad_z(down_parts, down_x, down_y)
        qkv_job = lambda joint, sib: [(normed_a, normed_sib, joint, sib, 0, 1)]
        parts_0 = grad_parts(qkv_job(joint_0, joint_0_sib), cut_group, depth, cut_group.wide)
        parts_0, grad_context = tie(parts_0, grad_context)
        e_0 = swap(parts_0[3], "x")
        joint_1 = back_attention(grad_context, 1)
        joint_1, e_0, a_x, a_y, b_e, down_b, hidden = tie(joint_1, e_0, a_x, a_y, b_e, down_b, hidden)
        b_x, b_y = swap(add(b_parts[1], b_e), "x"), swap(b_parts[2], "y")
        a_z = grad_z(a_parts, a_x, a_y)
        x_0, y_0 = swap(parts_0[1], "x"), swap(add(parts_0[2], e_0), "y")
        parts_1 = grad_parts(qkv_job(joint_1, swap(joint_1, "c")), cut_group, depth, cut_group.wide)
        parts_1, joint_1 = tie(parts_1, joint_1)
        e_1 = swap(parts_1[3], "y")
        input_grad, joint_sums, sums_a = back_input(place, joint_0, joint_1, qkv_full, tokens, gain_a, grad_middle)
        packed = pack(shard_count, sums_a, joint_sums, sums_b, bias_up_sums, g_bias_down)
        input_grad, e_1, x_0, y_0, b_x, b_y, a_z, hidden, down_b, packed = tie(
            input_grad, e_1, x_0, y_0, b_x, b_y, a_z, hidden, down_b, packed
        )
        x_1, y_1 = swap(add(parts_1[1], e_1), "x"), swap(parts_1[2], "y")
        b_z = grad_z(b_parts, b_x, b_y)
        result = finish(place, hidden, down_full, middle, bias_down, valid_wide)
    else:
        grad_pre, bias_up_sums, grad_middle, grad_branch, grad_context, sums_b = back(
            place,
            grad_out, down_full, slope, up_full, middle, gain_b, out_full
        )
        grad_context = grad_context.reshape(images, slots, width)
        joint_0, joint_1 = (back_attention(grad_context, g) for g in range(GROUPS))
        input_grad, joint_sums, sums_a = back_input(place, joint_0, joint_1, qkv_full, tokens, gain_a, grad_middle)
        grad_joint = jnp.concatenate([joint_0, joint_1], axis=1)
        result = finish(place, hidden, down_full, middle, bias_down, valid_wide)

    if not staged:
        group = 3 * width // GROUPS
        joint_sums = ungrouped([joint_sums[:, g * group : (g + 1) * group] for g in range(GROUPS)])
        g_bias_qv = jnp.concatenate([joint_sums[:, :width], joint_sums[:, 2 * width :]], axis=1)
        small_grads = (sums_a[0], sums_a[1], g_bias_qv, sums_b[2], sums_b[0], sums_b[1], bias_up_sums, g_bias_down)
        packed = jnp.concatenate([v.reshape(shard_count, -1) for v in small_grads], axis=1)
    if staged:
        packed = packed + swap(packed, "c")
        packed = packed + swap(packed, "x")
        x_1, y_1, b_z, result, input_grad, packed, a_g, down_g = tie(
            x_1, y_1, b_z, result, input_grad, packed, grad_x(a_z), grad_x(down_b)
        )
        qkv_b = grad_z(
            tuple(jnp.concatenate([p, q], axis=2) for p, q in zip(parts_0[:1], parts_1[:1])),
            jnp.concatenate([x_0, x_1], axis=2),
            jnp.concatenate([y_0, y_1], axis=2),
        )
        outs = by_slot(input_grad, result)
        early, late = outs[:-1], outs[-1]
        qkv_b, b_g, packed, a_g, down_g, early = tie(qkv_b, grad_x(b_z), over_rows(packed), a_g, down_g, early)
        b_g, a_g, down_g = (grad_core(*v) for v in (b_g, a_g, down_g))
        mine, from_x = grad_x(qkv_b)
        half, n_out, n_qkv = cut_up.wide // 2, cut_out.wide, cut_group.wide
        up_plan = [(0, 0, half, (0, 2 * half)), (1, 0, half, (half, 3 * half))]
        g_up, g_out, g_down = shards_of(
            (a_g, b_g, down_g),
            [
                (False, up_weight.shape, up_plan),
                (False, out_weight.shape, [(1, half, n_out, (0, n_out))]),
                (True, down_weight.shape, [(2, 0, width, None)]),
            ],
        )
        g_up, g_out, g_down, packed, late, from_x = tie(g_up, g_out, g_down, packed, late, from_x)
        outs = early + [late]
        qkv_g = grad_core(mine, from_x)
        packed = over_line(packed)
        part = width // GROUPS
        qkv_plan = []
        for g in range(GROUPS):
            for low in range(0, n_qkv, LANES):
                places = [divmod(c * n_qkv + low, part) for c in range(2)]
                places = [t * width + g * part + at for t, at in places]
                qkv_plan.append((0, g * n_qkv + low, LANES, places))
        (g_qkv,) = shards_of([qkv_g], [(False, attn_weight.shape, qkv_plan)])
    else:
        outs = by_slot(input_grad, result)
        packed = lax.psum_scatter(packed, FSDP, scatter_dimension=0)
        packed = lax.psum(packed, SEQ)
        g_qkv, g_out, g_up, g_down = (
            scatter_plain(a, g)
            for a, g in ((normed_a, grad_joint), (context, grad_branch), (normed_b, grad_pre), (hidden, grad_out))
        )
        g_qkv = ungrouped([g_qkv[:, : 3 * width // GROUPS], g_qkv[:, 3 * width // GROUPS :]])
    input_grad, layer_out = in_slots(outs)
    (g_gain_a, g_shift_a, g_bias_qv, g_bias_out, g_gain_b, g_shift_b, g_bias_up, g_bias_down) = (
        packed[c : c + n] for c, n in zip(cuts, sizes)
    )
    return (
        layer_out,
        input_grad,
        g_gain_a,
        g_shift_a,
        g_qkv,
        g_bias_qv,
        g_out,
        g_bias_out,
        g_gain_b,
        g_shift_b,
        g_up,
        g_bias_up,
        g_down,
        g_bias_down,
    )


def solution(mesh):
    shard_count, members = mesh.devices.shape
    fine = Mesh(mesh.devices.reshape(shard_count // 2, 2, members // 2, 2), FSDP + SEQ)
    rows, vector, matrix = P(FSDP, SEQ, None), P(FSDP), P(FSDP, None)
    weights = (vector, vector, matrix, vector, matrix, vector, vector, vector, matrix, vector, matrix, vector)
    return jax.shard_map(
        shards,
        mesh=fine,
        in_specs=(rows, vector) + weights + (rows,),
        out_specs=(rows, rows) + weights,
        check_vma=False,
    )
```

```python
import functools

import jax
import jax.numpy as jnp
from jax import lax
from jax.experimental import pallas as pl
from jax.experimental.pallas import tpu as pltpu
from jax.sharding import Mesh
from jax.sharding import PartitionSpec as P

HEAD_DIM = 64
LANES = 128
GROUPS = 2
TILES = 4
EPSILON = 1e-06
BF16 = jnp.bfloat16
F32 = jnp.float32
FSDP, SEQ = ("z", "y"), ("x", "c")


def cost(microseconds, nbytes=0):
    return pl.CostEstimate(flops=int(microseconds * 1.1e9), bytes_accessed=nbytes, transcendentals=0)


def norm_back(grad_norm, gain, normal, inv_std):
    scaled = grad_norm * gain
    return inv_std * (
        scaled
        - jnp.mean(scaled, axis=-1, keepdims=True)
        - normal * jnp.mean(scaled * normal, axis=-1, keepdims=True)
    )


def contract(a, b, ca, cb):
    return lax.dot_general(a, b, (((ca,), (cb,)), ((), ())), preferred_element_type=F32)


def lanes_of(shape):
    lane = lax.broadcasted_iota(jnp.int32, shape, 1)
    return lane // HEAD_DIM, lane % HEAD_DIM


def spread_over(places, place, columns, rest=0.0):
    out = jnp.full(place.shape, rest, F32)
    for i in places:
        out = jnp.where(place == i, columns[i], out)
    return out


def parts_of(value, count):
    parts = []
    for _ in range(count):
        parts.append(value.astype(BF16).astype(F32))
        value = value - parts[-1]
    return parts


SCALE = HEAD_DIM ** (-0.5)


def attend_kernel(bias_ref, q_ref, k_ref, v_ref, out_ref, lse_ref):
    bias = bias_ref[0]
    for tile in range(q_ref.shape[2] // LANES):
        at = slice(tile * LANES, (tile + 1) * LANES)
        q, k, v = (ref[0, :, at].astype(F32) for ref in (q_ref, k_ref, v_ref))
        head_of, place = lanes_of(q.shape)
        context, lse = jnp.zeros(q.shape, F32), jnp.zeros(q.shape, F32)
        for head in range(LANES // HEAD_DIM):
            own = head_of == head
            left = jnp.where(own, q * SCALE, spread_over((0,), place, (1.0,))).astype(BF16)
            right = jnp.where(own, k, spread_over((0,), place, (bias,))).astype(BF16)
            scores = contract(left, right, 1, 1)
            top = jnp.max(scores, axis=-1, keepdims=True)
            exps = jnp.exp(scores - top).astype(BF16)
            both = contract(exps, jnp.where(own, v, 1.0).astype(BF16), 1, 0)
            other = (1 - head) * HEAD_DIM
            total = both[:, other : other + 1]
            context = jnp.where(own, both * (1.0 / total), context)
            lse = jnp.where(own, lse, top + jnp.log(total))
        out_ref[0, :, at] = context.astype(BF16)
        lse_ref[0, :, at] = lse


def attend_back_kernel(bias_ref, q_ref, k_ref, v_ref, lse_ref, context_ref, g_ref, out_ref):
    bias = bias_ref[0]
    tiles = q_ref.shape[2] // LANES
    width = out_ref.shape[2] // 3
    for tile in range(tiles):
        at = slice(tile * LANES, (tile + 1) * LANES)
        q_low, k_low, g_low = q_ref[0, :, at], k_ref[0, :, at], g_ref[0, :, at]
        q, k, v, g, context = (ref[0, :, at].astype(F32) for ref in (q_ref, k_ref, v_ref, g_ref, context_ref))
        head_of, place = lanes_of(q.shape)
        dq, dk, dv = (jnp.zeros(q.shape, F32) for _ in range(3))
        lse_parts = [-part for part in parts_of(lse_ref[0, :, at], 3)] + [1.0]
        product = g * context
        for head in range(LANES // HEAD_DIM):
            own = head_of == head
            left = jnp.where(own, q * SCALE, spread_over(range(4), place, lse_parts)).astype(BF16)
            right = jnp.where(own, k, spread_over(range(4), place, (1.0, 1.0, 1.0, bias))).astype(BF16)
            probs = jnp.exp(contract(left, right, 1, 1))
            inner = jnp.sum(jnp.where(own, product, 0.0), axis=-1, keepdims=True)
            inner_parts = [-part for part in parts_of(inner, 2)]
            left = jnp.where(own, g, spread_over(range(2), place, inner_parts)).astype(BF16)
            right = jnp.where(own, v, spread_over(range(2), place, (1.0, 1.0))).astype(BF16)
            grad_scores = (probs * contract(left, right, 1, 1)).astype(BF16)
            dq = jnp.where(own, contract(grad_scores, k_low, 1, 0), dq)
            dk = jnp.where(own, contract(grad_scores, q_low, 0, 0), dk)
            dv = jnp.where(own, contract(probs.astype(BF16), g_low, 0, 0), dv)
        for block, value in enumerate((dq * SCALE, dk * SCALE, dv)):
            start = block * width + (pl.program_id(1) * tiles + tile) * LANES
            out_ref[0, :, pl.ds(pl.multiple_of(start, LANES), LANES)] = value.astype(BF16)


def attention(key_bias, joint, saved=(), group=0):
    images, slots, width = joint.shape[0], joint.shape[1], joint.shape[2] // 3
    lanes = TILES * LANES
    in_group = width // lanes // GROUPS
    back = len(saved) > 0
    pairs = in_group if back else in_group * GROUPS
    block = (1, slots, lanes)

    def spec(part):
        def index(i, h):
            h = h + group * in_group
            return i, 0, (h // in_group * 3 + part) * in_group + h % in_group

        return pl.BlockSpec(block, index)

    plain = pl.BlockSpec(block, lambda i, h: (i, 0, h + group * in_group))
    bias = pl.BlockSpec((1, slots, 1), lambda i, h: (i, 0, 0))
    whole = pl.BlockSpec((1, slots, 3 * pairs * lanes), lambda i, h: (i, 0, 0))
    shape = lambda columns, kind: jax.ShapeDtypeStruct((images, slots, columns), kind)
    return pl.pallas_call(
        attend_back_kernel if back else attend_kernel,
        grid=(images, pairs),
        in_specs=[bias] + [spec(part) for part in range(3)] + [plain] * len(saved),
        out_specs=whole if back else [plain, plain],
        out_shape=shape(3 * pairs * lanes, BF16) if back else [shape(width, BF16), shape(width, F32)],
        cost_estimate=cost((1.3 if back else 0.8) * images * pairs * TILES),
    )(key_bias, joint, joint, joint, *saved)


STEP = 1024


def stats(values):
    center = values - jnp.mean(values, axis=-1, keepdims=True)
    inv_std = lax.rsqrt(jnp.mean(center * center, axis=-1, keepdims=True) + EPSILON)
    return center * inv_std, inv_std


def column_sums(values):
    return jnp.sum(values, axis=0, keepdims=True)


def block_spec(shape, index=lambda j: 0, at=1):
    def position(j, place):
        value = index(j, place) if index.__code__.co_argcount == 2 else index(j)
        return (0, value) if at else (value, 0)

    return pl.BlockSpec(shape, position)


def whole_spec(array):
    return block_spec(array.shape)


def columns_spec(rows, index=lambda j: j, step=STEP):
    return block_spec((rows, step), index)


class Weight:
    def __init__(self, arrays, by_rows=False, base=0, blocks=None, step=STEP):
        self.arrays, self.by_rows, self.base, self.blocks, self.step = tuple(arrays), by_rows, base, blocks, step

    def specs(self):
        return [pl.BlockSpec(memory_space=pl.ANY)] * len(self.arrays)

    def copies(self, refs, place_ref, j, block, buf, sem):
        copy = lambda source, target: pltpu.make_async_copy(source, target, sem)
        if len(refs) == 1:
            at = pl.ds(pl.multiple_of(block * self.step, self.step), self.step)
            return [(None, [copy(refs[0].at[at] if self.by_rows else refs[0].at[:, at], buf)])]
        y, x, c = place_ref[0], place_ref[1], place_ref[2]
        depth, rows = refs[0].shape[0], refs[0].shape[1]

        def piece(owner, i, z):
            five = refs[5 * owner : 5 * owner + 5]
            if i < 3:
                return five[i].at[z]
            return five[3].at[z] if z < depth // 2 else five[4].at[z - depth // 2]

        found = []
        if not self.by_rows:
            half = self.blocks // 2
            lanes = pl.ds(pl.multiple_of(self.base + block % half * self.step, LANES), self.step)
            for owner in range(2):
                some = []
                for i in range(4):
                    for z in range(depth):
                        row = (2 * z + (y ^ (i // 2))) * 2 * rows + (x ^ (i % 2)) * rows
                        target = buf.at[pl.ds(pl.multiple_of(row, rows), rows)]
                        some.append(copy(piece(owner, i, z).at[:, lanes], target))
                found.append(((block // half == c) == (owner == 0), some))
            return found
        width = buf.shape[1]
        segments = refs[0].shape[2] // width
        for z in range(depth):
            some = []
            for owner in range(2):
                for i in range(4):
                    for k in range(segments):
                        row = (((y ^ (i // 2)) * 2 + (c ^ owner)) * 2 + (x ^ (i % 2))) * segments * rows + k * rows
                        source = piece(owner, i, z).at[:, pl.ds(k * width, width)]
                        some.append(copy(source, buf.at[pl.ds(pl.multiple_of(row, rows), rows)]))
            found.append((j == z, some))
        return found

    def start(self, *where):
        for condition, some in self.copies(*where):
            go = lambda some=some: [one.start() for one in some] and None
            go() if condition is None else pl.when(condition)(go)

    def wait(self, *where):
        for condition, some in self.copies(*where):
            go = lambda some=some: [one.wait() for one in some] and None
            go() if condition is None else pl.when(condition)(go)


def stream(weight, refs, place_ref, buf, sems):
    j = pl.program_id(0)

    def where(step):
        slot = step % 2
        return refs, place_ref, step, step, buf.at[slot], sems.at[slot]

    @pl.when(j == 0)
    def _():
        weight.start(*where(j))

    @pl.when(j + 1 < pl.num_programs(0))
    def _():
        weight.start(*where(j + 1))

    weight.wait(*where(j))
    return buf[j % 2]


def split_refs(refs, weights):
    groups = []
    for weight in weights:
        groups.append(refs[: len(weight.arrays)])
        refs = refs[len(weight.arrays) :]
    return groups, refs


def stepped(kernel, steps, place, weights, in_specs, operands, out_specs, out_shape, scratch, microseconds):
    specs = [spec for weight in weights for spec in weight.specs()]
    arrays = [v for weight in weights for v in weight.arrays]
    return pl.pallas_call(
        functools.partial(kernel, weights),
        grid_spec=pltpu.PrefetchScalarGridSpec(
            num_scalar_prefetch=1,
            grid=(steps,),
            in_specs=specs + in_specs,
            out_specs=out_specs,
            scratch_shapes=scratch,
        ),
        out_shape=out_shape,
        compiler_params=pltpu.CompilerParams(vmem_limit_bytes=56 << 20),
        cost_estimate=cost(microseconds),
    )(place, *arrays, *operands)


def streamed(rows, columns):
    return [pltpu.VMEM((2, rows, columns), BF16), pltpu.SemaphoreType.DMA((2,))]


def project_kernel(weights, place_ref, *refs):
    (weight_refs,), refs = split_refs(refs, weights)
    tokens_ref, gain_ref, shift_ref, query_ref, value_ref, normed_ref, joint_ref, buf, sems = refs

    @pl.when(pl.program_id(0) == 0)
    def _():
        normal, _ = stats(tokens_ref[...].astype(F32))
        normed_ref[...] = (normal * gain_ref[...] + shift_ref[...]).astype(BF16)

    weight = stream(weights[0], weight_refs, place_ref, buf, sems)
    bias = jnp.concatenate([query_ref[...], jnp.zeros_like(query_ref[...]), value_ref[...]], axis=1)
    joint_ref[...] = (contract(normed_ref[...], weight, 1, 0) + bias).astype(BF16)


def project(place, tokens, gain, shift, weight, bias_qv):
    rows, width = tokens.shape
    part = width // GROUPS
    return stepped(
        project_kernel,
        GROUPS,
        place,
        [weight],
        [whole_spec(tokens), whole_spec(gain), whole_spec(shift)]
        + [columns_spec(1, index, part) for index in (lambda j: j, lambda j: GROUPS + j)],
        (tokens, gain, shift, bias_qv, bias_qv),
        [whole_spec(tokens), columns_spec(rows, step=3 * part)],
        [jax.ShapeDtypeStruct((rows, width), BF16), jax.ShapeDtypeStruct((rows, 3 * width), BF16)],
        streamed(width, 3 * part),
        10,
    )


def out_blocks(weight, refs, place_ref, buf, sem):
    for block in range(buf.shape[0]):
        yield weight, (refs, place_ref, 0, block, buf.at[block], sem)


def expand_kernel(weights, place_ref, *refs):
    (up_refs, out_w_refs), refs = split_refs(refs, weights)
    tokens_ref, context_ref, bias_out_ref, gain_ref, shift_ref, bias_ref, *refs = refs
    middle_ref, normed_ref, hidden_ref, slope_ref, other_ref, buf, sems, out_buf, out_sem = refs

    @pl.when(pl.program_id(0) == 0)
    def _():
        blocks = list(out_blocks(weights[1], out_w_refs, place_ref, out_buf, out_sem))
        for weight, where in blocks:
            weight.start(*where)
        for weight, where in blocks:
            weight.wait(*where)
        context = context_ref[...]
        branch = jnp.concatenate([contract(context, out_buf[b], 1, 0) for b in range(out_buf.shape[0])], axis=1)
        middle = tokens_ref[...].astype(F32) + (branch + bias_out_ref[...])
        middle_ref[...] = middle
        normal, _ = stats(middle)
        normed_ref[...] = (normal * gain_ref[...] + shift_ref[...]).astype(BF16)

    weight = stream(weights[0], up_refs, place_ref, buf, sems)
    pre = contract(normed_ref[...], weight, 1, 0) + bias_ref[...]
    cumul = 0.5 * (1.0 + lax.erf(pre * 0.7071067811865476))
    hidden = (pre * cumul).astype(BF16)
    hidden_ref[...] = hidden
    half = 2 * LANES
    for i in range(other_ref.shape[1] // half):
        low, high = (hidden[:, (2 * i + k) * half : (2 * i + k + 1) * half] for k in range(2))
        other_ref[:, i * half : (i + 1) * half] = jnp.where(place_ref[2] == 0, high, low)
    slope = cumul + pre * (jnp.exp(-0.5 * pre * pre) * 0.3989422804014327)
    slope_ref[...] = slope.astype(BF16)


def expand(place, tokens, context, out_weight, bias_out, gain, shift, up, bias_up):
    rows, width = tokens.shape
    hidden = bias_up.shape[1]
    return stepped(
        expand_kernel,
        hidden // STEP,
        place,
        [up, out_weight],
        [whole_spec(v) for v in (tokens, context, bias_out, gain, shift)] + [columns_spec(1)],
        (tokens, context, bias_out, gain, shift, bias_up),
        [whole_spec(tokens)] * 2 + [columns_spec(rows)] * 2 + [columns_spec(rows, step=STEP // 2)],
        [jax.ShapeDtypeStruct((rows, width), F32), jax.ShapeDtypeStruct((rows, width), BF16)]
        + [jax.ShapeDtypeStruct((rows, n), BF16) for n in (hidden, hidden, hidden // 2)],
        streamed(width, STEP) + [pltpu.VMEM((width // out_weight.step, width, out_weight.step), BF16), pltpu.SemaphoreType.DMA],
        20,
    )


def accumulate(total_ref, part, first=None):
    j = pl.program_id(0)

    @pl.when(j == 0)
    def _():
        total_ref[...] = part if first is None else first() + part

    @pl.when(j > 0)
    def _():
        total_ref[...] += part


def finish_kernel(weights, place_ref, *refs):
    (down_refs,), refs = split_refs(refs, weights)
    hidden_ref, middle_ref, bias_ref, valid_ref, result_ref, total_ref, buf, sems = refs
    weight = stream(weights[0], down_refs, place_ref, buf, sems)
    part = contract(hidden_ref[...], weight, 1, 0)
    accumulate(total_ref, part, lambda: middle_ref[...] + bias_ref[...])

    @pl.when(pl.program_id(0) == pl.num_programs(0) - 1)
    def _():
        result_ref[...] = jnp.where(valid_ref[...] > 0.5, total_ref[...], 0.0).astype(BF16)


def finish(place, hidden, down, middle, bias_down, valid):
    rows, width = middle.shape
    return stepped(
        finish_kernel,
        hidden.shape[1] // STEP,
        place,
        [down],
        [columns_spec(rows)] + [whole_spec(v) for v in (middle, bias_down, valid)],
        (hidden, middle, bias_down, valid),
        whole_spec(middle),
        jax.ShapeDtypeStruct((rows, width), BF16),
        [pltpu.VMEM((rows, width), F32)] + streamed(STEP, width),
        11,
    )


def back_kernel(weights, place_ref, *refs):
    (down_refs, up_refs, out_w_refs), refs = split_refs(refs, weights)
    grad_ref, slope_ref, middle_ref, gain_ref, *refs = refs
    pre_ref, bias_up_ref, grad_middle_ref, branch_ref, context_ref, sums_ref, total_ref, *refs = refs
    down_buf, down_sems, up_buf, up_sems, out_buf, out_sem = refs
    j = pl.program_id(0)
    blocks = lambda: out_blocks(weights[2], out_w_refs, place_ref, out_buf, out_sem)

    @pl.when(j == 0)
    def _():
        for weight, where in blocks():
            weight.start(*where)

    down = stream(weights[0], down_refs, place_ref, down_buf, down_sems)
    up = stream(weights[1], up_refs, place_ref, up_buf, up_sems)
    pre = (contract(grad_ref[...], down, 1, 1) * slope_ref[...].astype(F32)).astype(BF16)
    pre_ref[...] = pre
    bias_up_ref[...] = column_sums(pre.astype(F32))
    accumulate(total_ref, contract(pre, up, 1, 1))

    @pl.when(j == pl.num_programs(0) - 1)
    def _():
        for weight, where in blocks():
            weight.wait(*where)
        normal, inv_std = stats(middle_ref[...])
        total = total_ref[...]
        grad_middle = grad_ref[...].astype(F32) + norm_back(total, gain_ref[...], normal, inv_std)
        grad_middle_ref[...] = grad_middle
        branch = grad_middle.astype(BF16)
        branch_ref[...] = branch
        context_ref[...] = sum(
            contract(branch[:, b * out_buf.shape[2] : (b + 1) * out_buf.shape[2]], out_buf[b], 1, 1)
            for b in range(out_buf.shape[0])
        ).astype(BF16)
        sums_ref[0:1] = column_sums(total * normal)
        sums_ref[1:2] = column_sums(total)
        sums_ref[2:3] = column_sums(branch.astype(F32))


def back(place, grad_out, down, slope, up, middle, gain, out_weight):
    rows, width = middle.shape
    hidden = slope.shape[1]
    return stepped(
        back_kernel,
        hidden // STEP,
        place,
        [down, up, out_weight],
        [whole_spec(grad_out), columns_spec(rows), whole_spec(middle), whole_spec(gain)],
        (grad_out, slope, middle, gain),
        [columns_spec(rows), columns_spec(1)]
        + [whole_spec(middle)] * 3
        + [block_spec((8, width))],
        [
            jax.ShapeDtypeStruct((rows, hidden), BF16),
            jax.ShapeDtypeStruct((1, hidden), F32),
            jax.ShapeDtypeStruct((rows, width), F32),
            jax.ShapeDtypeStruct((rows, width), BF16),
            jax.ShapeDtypeStruct((rows, width), BF16),
            jax.ShapeDtypeStruct((8, width), F32),
        ],
        [pltpu.VMEM((rows, width), F32)]
        + streamed(STEP, width)
        + streamed(width, STEP)
        + [pltpu.VMEM((width // out_weight.step, width, out_weight.step), BF16), pltpu.SemaphoreType.DMA],
        23,
    )


def input_kernel(weights, place_ref, *refs):
    (weight_refs,), refs = split_refs(refs, weights)
    joint_0_ref, joint_1_ref, tokens_ref, gain_ref, grad_middle_ref, *refs = refs
    input_ref, bias_ref, sums_ref, total_ref, buf, sems = refs
    j = pl.program_id(0)
    first = jnp.broadcast_to(j == 0, joint_0_ref.shape)
    joint = jnp.where(first, joint_0_ref[...], joint_1_ref[...])
    bias_ref[...] = column_sums(joint.astype(F32))
    weight = stream(weights[0], weight_refs, place_ref, buf, sems)
    accumulate(total_ref, contract(joint, weight, 1, 1))

    @pl.when(j == pl.num_programs(0) - 1)
    def _():
        normal, inv_std = stats(tokens_ref[...].astype(F32))
        total = total_ref[...]
        grad = grad_middle_ref[...] + norm_back(total, gain_ref[...], normal, inv_std)
        input_ref[...] = grad.astype(BF16)
        sums_ref[0:1] = column_sums(total * normal)
        sums_ref[1:2] = column_sums(total)


def back_input(place, joint_0, joint_1, weight, tokens, gain, grad_middle):
    rows, width = tokens.shape
    group = 3 * width // GROUPS
    return stepped(
        input_kernel,
        GROUPS,
        place,
        [weight],
        [whole_spec(v) for v in (joint_0, joint_1, tokens, gain, grad_middle)],
        (joint_0, joint_1, tokens, gain, grad_middle),
        [whole_spec(tokens), columns_spec(1, step=group), block_spec((8, width))],
        [
            jax.ShapeDtypeStruct((rows, width), BF16),
            jax.ShapeDtypeStruct((1, 3 * width), F32),
            jax.ShapeDtypeStruct((8, width), F32),
        ],
        [pltpu.VMEM((rows, width), F32)] + streamed(width, group),
        13,
    )


def grouped(value):
    width = value.shape[-1] // 3
    part = width // GROUPS
    return jnp.concatenate(
        [value[..., t * width + g * part :][..., :part] for g in range(GROUPS) for t in range(3)], axis=-1
    )


def ungrouped(values):
    part = values[0].shape[-1] // 3
    return jnp.concatenate(
        [v[..., t * part : (t + 1) * part] for t in range(3) for v in values], axis=-1
    )


def swap(value, axis):
    return lax.ppermute(value, axis, [(0, 1), (1, 0)])


def send(value, axis, step):
    return lax.ppermute(value, axis, [(i, i ^ step) for i in range(lax.axis_size(axis))])


def pick(blocks, index):
    return lax.dynamic_index_in_dim(blocks, index, 0, keepdims=False)


def tie(*values):
    return lax.optimization_barrier(values)


def after(value, *others):
    return lax.optimization_barrier((value,) + others)[0]


def my_place():
    return jnp.stack([lax.axis_index(n) for n in ("y", "x", "c")]).astype(jnp.int32)


class Split:
    def __init__(self, shard, by_rows=False, columns=None):
        self.shard_rows, self.columns = shard[0], columns or shard[1]
        self.by_rows = by_rows
        self.rows = self.shard_rows // 4 if by_rows else self.shard_rows // 2
        self.wide = self.columns if by_rows else self.columns // 2

def exchange(blocks, axis):
    return lax.all_to_all(blocks, axis, split_axis=0, concat_axis=0, tiled=True)


def pieces_kernel(depth, rows, place_ref, qkv_ref, out_ref, up_ref, down_ref, *refs):
    *vector_refs, first_ref, second_ref, third_ref = refs
    x, c = place_ref[1], place_ref[2]
    at = pl.ds(pl.multiple_of(x * rows, rows), rows)

    def put(ref, lane, value):
        for z in range(depth):
            ref[z, : value.shape[0], lane : lane + value.shape[1]] = value
        return lane + value.shape[1]

    def columns(ref, start, count):
        return ref[at, pl.ds(pl.multiple_of(start, LANES), count)]

    width = out_ref.shape[1]
    part = width // 2
    lane = 0
    for t in range(3):
        lane = put(first_ref, lane, columns(qkv_ref, t * width + c * part, part))
    lane = put(first_ref, lane, columns(out_ref, c * part, part))
    packed = jnp.concatenate([ref[...] for ref in vector_refs], axis=0)
    padding = jnp.zeros((rows - packed.shape[0], LANES), packed.dtype)
    put(first_ref, lane, jnp.concatenate([packed, padding], axis=0))
    half = up_ref.shape[1] // 2
    put(second_ref, 0, columns(up_ref, c * half, half))
    blocks = down_ref.shape[0] // 4 // rows
    lane = 0
    for block in range(blocks):
        start = ((2 * c + x) * blocks + block) * rows
        lane = put(third_ref, lane, down_ref[pl.ds(pl.multiple_of(start, rows), rows), :])


def pieces(qkv, out, up, down, vectors):
    depth, rows = lax.axis_size("z"), qkv.shape[0] // 2
    vectors = [v.reshape(-1, LANES) for v in vectors]
    width = out.shape[1]
    wide = (2 * width + LANES, up.shape[1] // 2, down.shape[0] // 4 // rows * width)
    vmem = pl.BlockSpec(memory_space=pltpu.VMEM)
    return pl.pallas_call(
        functools.partial(pieces_kernel, depth, rows),
        in_specs=[pl.BlockSpec(memory_space=pltpu.SMEM)] + [vmem] * (4 + len(vectors)),
        out_specs=[vmem] * 3,
        out_shape=[jax.ShapeDtypeStruct((depth, rows, n), BF16) for n in wide],
        cost_estimate=cost(3),
    )(my_place(), qkv, out, up, down, *vectors)


def corner(from_x, from_y):
    half = from_x.shape[0] // 2
    return swap(from_x[:half], "y"), swap(from_y[half:], "x")


def core_swap(*pieces):
    return tuple(swap(v, "c") for v in pieces)


def my_place():
    return jnp.stack([lax.axis_index(n) for n in ("y", "x", "c")]).astype(jnp.int32)


def part_refs(x, near, far, rows, refs, at):
    own_ref, to_x_ref, to_y_ref, corner_ref = refs
    low, high = near[:rows], near[rows:]
    own_ref[at] = jnp.where(x == 0, low, high)
    to_x_ref[at] = jnp.where(x == 0, high, low)
    low, high = far[:rows], far[rows:]
    to_y_ref[at] = jnp.where(x == 0, low, high)
    corner_ref[at] = jnp.where(x == 0, high, low)


def grad_columns_kernel(ends, cut, place_ref, *refs):
    y, x = place_ref[0], place_ref[1]
    out_refs = refs[-4:]
    j = pl.program_id(0)

    def one(a_ref, a_sib_ref, g_ref, g_sib_ref):
        total = contract(a_ref[...], g_ref[...], 0, 0) + contract(a_sib_ref[...], g_sib_ref[...], 0, 0)
        total = total.reshape(-1, 2, cut.shard_rows, total.shape[1])
        for z in range(total.shape[0]):
            near = jnp.where(y == 0, total[z, 0], total[z, 1]).astype(BF16)
            far = jnp.where(y == 0, total[z, 1], total[z, 0]).astype(BF16)
            part_refs(x, near, far, cut.rows, out_refs, z)

    if len(ends) == 1:
        one(*refs[:4])
        return
    for i, end in enumerate(ends):
        first = 0 if i == 0 else ends[i - 1]
        pl.when((j >= first) & (j < end))(functools.partial(one, *refs[4 * i : 4 * i + 4]))


def grad_rows_kernel(cut, place_ref, a0_ref, a1_ref, a0_sib_ref, a1_sib_ref, g_ref, g_sib_ref, *out_refs):
    y, x = place_ref[0], place_ref[1]
    by_y = [
        contract(ref[...], g_ref[...], 0, 0)
        + contract(sib_ref[...], g_sib_ref[...], 0, 0)
        for ref, sib_ref in ((a0_ref, a0_sib_ref), (a1_ref, a1_sib_ref))
    ]
    near = jnp.where(y == 0, by_y[0], by_y[1]).astype(BF16)
    far = jnp.where(y == 0, by_y[1], by_y[0]).astype(BF16)
    part_refs(x, near, far, cut.rows, out_refs, 0)


def grad_parts(jobs, cut, depth, step=512):
    tokens = jobs[0][0].shape[0]
    specs, operands, ends = [], [], []
    if cut.by_rows:
        ((a, a_sib, g, g_sib, _, _),) = jobs
        half = 2 * cut.rows
        every = pl.BlockSpec((tokens, cut.wide), lambda j, place: (0, 0))
        specs = [
            pl.BlockSpec((tokens, half), lambda j, place: (0, 4 * j + place[2])),
            pl.BlockSpec((tokens, half), lambda j, place: (0, 4 * j + 2 + place[2])),
            pl.BlockSpec((tokens, half), lambda j, place: (0, 2 * j)),
            pl.BlockSpec((tokens, half), lambda j, place: (0, 2 * j + 1)),
            every,
            every,
        ]
        operands, kernel, grid, wide = [a, a, a_sib, a_sib, g, g_sib], functools.partial(grad_rows_kernel, cut), depth, cut.wide
        out_spec = lambda n: pl.BlockSpec((1, n, wide), lambda j, place: (j, 0, 0))
    else:
        grid = 0
        for a, a_sib, g, g_sib, start, steps in jobs:
            in_half = g.shape[1] // 2 // step
            every = pl.BlockSpec((tokens, a.shape[1]), lambda j, place: (0, 0))
            at = lambda j, first=grid, steps=steps: jnp.clip(j - first, 0, steps - 1)
            specs += [
                every,
                every,
            ] + [
                pl.BlockSpec(
                    (tokens, step), lambda j, place, at=at, n=in_half, s=start: (0, place[2] * n + s + at(j))
                )
            ] * 2
            operands += [a, a_sib, g, g_sib]
            grid += steps
            ends.append(grid)
        kernel, wide = functools.partial(grad_columns_kernel, ends, cut), grid * step
        out_spec = lambda n: pl.BlockSpec((depth, n, step), lambda j, place: (0, 0, j))
    total = 8 * depth * cut.rows * wide
    return pl.pallas_call(
        kernel,
        grid_spec=pltpu.PrefetchScalarGridSpec(
            num_scalar_prefetch=1,
            grid=(grid,),
            in_specs=specs,
            out_specs=[out_spec(cut.rows)] * 4,
        ),
        out_shape=[jax.ShapeDtypeStruct((depth, cut.rows, wide), BF16)] * 4,
        compiler_params=pltpu.CompilerParams(vmem_limit_bytes=52 << 20),
        cost_estimate=cost(total * 2.2e-6),
    )(my_place(), *operands)


def add(one, other):
    return (one.astype(F32) + other.astype(F32)).astype(BF16)


def grad_z(parts, from_x, from_y):
    return exchange(sum(v.astype(F32) for v in (parts[0], from_x, from_y)).astype(BF16), "z")


def grad_x(blocks):
    mine = jnp.sum(blocks.astype(F32), axis=0).astype(BF16)
    return mine, swap(mine, "x")


def grad_core(mine, from_x):
    return mine, from_x, swap(mine, "c"), swap(from_x, "c")


def shard_kernel(plan, place_ref, *refs):
    x, c = place_ref[1], place_ref[2]
    parts, out_refs = refs[: -len(plan)], refs[-len(plan) :]
    for (by_rows, sources), out_ref in zip(plan, out_refs):
        column = 0
        for core in range(2):
            for number, start, count, at in sources:
                four = parts[4 * number : 4 * number + 4]
                rows = four[0].shape[0]
                for half in range(2):
                    both = [
                        jnp.where(c == core, four[i][:, start : start + count], four[2 + i][:, start : start + count])
                        for i in range(2)
                    ]
                    value = jnp.where(x == half, both[0], both[1]).astype(F32)
                    if by_rows:
                        row = (2 * core + half) * rows
                        out_ref[row : row + rows, :] = value
                    else:
                        out_ref[half * rows : (half + 1) * rows, at[core] : at[core] + count] = value


def shards_of(gradients, plan):
    parts = [v for gradient in gradients for v in gradient]
    vmem = pl.BlockSpec(memory_space=pltpu.VMEM)
    return pl.pallas_call(
        functools.partial(shard_kernel, [(by_rows, sources) for by_rows, _, sources in plan]),
        in_specs=[pl.BlockSpec(memory_space=pltpu.SMEM)] + [vmem] * len(parts),
        out_specs=[vmem] * len(plan),
        out_shape=[jax.ShapeDtypeStruct(shape, F32) for _, shape, _ in plan],
        cost_estimate=cost(2),
    )(my_place(), *parts)


def pack_kernel(sums_a_ref, joint_ref, sums_b_ref, up_ref, down_ref, out_ref):
    shards = out_ref.shape[0]
    width = down_ref.shape[1]
    part = width // GROUPS

    def put(at, count, source):
        for i in range(shards):
            out_ref[i : i + 1, at : at + count] = source(i, count)
        return at + count

    def plain(ref, row):
        return lambda i, n: ref[row : row + 1, i * n : (i + 1) * n]

    def query_value(i, n):
        value, at = divmod(i * n, width)
        group, at = divmod(at, part)
        start = (3 * group + 2 * value) * part + at
        return joint_ref[0:1, start : start + n]

    n = width // shards
    at = put(0, n, plain(sums_a_ref, 0))
    at = put(at, n, plain(sums_a_ref, 1))
    at = put(at, 2 * n, query_value)
    at = put(at, n, plain(sums_b_ref, 2))
    at = put(at, n, plain(sums_b_ref, 0))
    at = put(at, n, plain(sums_b_ref, 1))
    at = put(at, up_ref.shape[1] // shards, plain(up_ref, 0))
    put(at, n, plain(down_ref, 0))


def pack(shards, sums_a, joint_sums, sums_b, up_sums, down_sums):
    vmem = pl.BlockSpec(memory_space=pltpu.VMEM)
    columns = (9 - 1) * down_sums.shape[1] + up_sums.shape[1]
    return pl.pallas_call(
        pack_kernel,
        in_specs=[vmem] * 5,
        out_specs=vmem,
        out_shape=jax.ShapeDtypeStruct((shards, columns // shards), F32),
        cost_estimate=cost(1),
    )(sums_a, joint_sums, sums_b, up_sums, down_sums)


def in_order(index, mine, theirs, axis):
    first, second = jnp.where(index == 0, mine, theirs), jnp.where(index == 0, theirs, mine)
    return jnp.concatenate([first, second], axis=axis)


def order_vectors(own_y, other_y):
    y = lax.axis_index("y")
    rows = [jnp.where(y == 0, own_y, other_y), jnp.where(y == 0, other_y, own_y)]
    return jnp.stack(rows, axis=1).reshape(2 * own_y.shape[0], -1)


def over_rows(packed):
    y = lax.axis_index("y")
    packed = packed.reshape(lax.axis_size("z"), 2, -1)
    row = lambda yy: lax.dynamic_index_in_dim(packed, yy, 1, keepdims=False)
    return row(y) + swap(row(1 - y), "y")


def over_line(packed):
    z = lax.axis_index("z")
    return pick(packed, z) + sum(send(pick(packed, z ^ k), "z", k) for k in range(1, lax.axis_size("z")))


def scatter_plain(a, g):
    grad = lax.psum_scatter(contract(a, g, 0, 0).astype(BF16), FSDP, scatter_dimension=0, tiled=True)
    return lax.psum(grad, SEQ).astype(F32)


def shards(
    tokens,
    lengths,
    attn_gain,
    attn_shift,
    attn_weight,
    attn_bias,
    out_weight,
    out_bias,
    mlp_gain,
    mlp_shift,
    up_weight,
    up_bias,
    down_weight,
    down_bias,
    cotangent,
):
    width = tokens.shape[2]
    members = lax.axis_size(SEQ)
    staged = lax.axis_size("z") <= 8 and attn_weight.shape[0] % 128 == 0
    images = tokens.shape[0] // members
    slots = tokens.shape[1] * members
    rows = images * slots

    small = (attn_gain, attn_shift, attn_bias, out_bias, mlp_gain, mlp_shift, up_bias, down_bias)
    sizes = [v.shape[0] for v in small]
    cuts = [sum(sizes[:i]) for i in range(len(sizes))]
    packed = jnp.concatenate(small)

    few = tokens.shape[1]
    here = lax.axis_index(SEQ)
    lens = lax.dynamic_slice_in_dim(lengths, here * images, images, 0)
    slot = jnp.arange(slots, dtype=jnp.int32)
    slot = (slot // few ^ here) * few + slot % few
    valid = slot[None, :] < lens[:, None]
    key_bias = jnp.where(valid, 0.0, -1000000000.0)[:, :, None]
    valid = valid.reshape(rows, 1)

    def by_image(value, which=range(members)):
        value = value.reshape(members, images, few, width)
        return [send(pick(value, here ^ k), SEQ, k) if k else pick(value, here) for k in which]

    def by_slot(*values):
        value = jnp.concatenate([v.reshape(images, members, few, width) for v in values])
        return [send(value[:, k], SEQ, k) if k else value[:, 0] for k in range(members)]

    def in_images(blocks):
        return jnp.stack(blocks, axis=1).reshape(rows, width)

    def in_slots(blocks):
        blocks = jnp.stack(blocks)
        kinds = blocks.shape[1] // images
        blocks = jnp.concatenate([pick(blocks, here ^ k).reshape(kinds, images, few, width) for k in range(members)], axis=1)
        return [blocks[i] for i in range(kinds)]

    def unpack(vectors):
        vectors = vectors.astype(F32)
        return [vectors[:, c : c + n].reshape(1, -1) for c, n in zip(cuts, sizes)]

    if staged:
        cut_qkv, cut_out, cut_up = (Split(w.shape) for w in (attn_weight, out_weight, up_weight))
        cut_down = Split(down_weight.shape, by_rows=True)
        cut_group = Split(attn_weight.shape, columns=3 * width // GROUPS)
        place = my_place()
        first, second, third = pieces(attn_weight, out_weight, up_weight, down_weight, small)
        cot = by_image(cotangent, range(members - 1))
        tokens, cot, cotangent, z1, second, third = tie(
            by_image(tokens), cot, cotangent, exchange(first, "z"), second, third
        )
        tokens = in_images(tokens)
        x1, y1 = swap(z1, "x"), swap(z1, "y")
        z2 = exchange(second, "z")
        x1, y1, z1, third = tie(x1, y1, z1, third)
        vec_z, vec_y = (v[:, : sum(sizes) // LANES, -LANES:].reshape(v.shape[0], -1) for v in (z1, y1))
        vectors = unpack(order_vectors(vec_z, vec_y))
        d1, c1, z2, vectors, third, tokens = tie(
            corner(x1, y1), core_swap(z1, x1, y1), z2, vectors, third, tokens
        )
        gain_a, shift_a, bias_qv, bias_out, gain_b, shift_b, bias_up, bias_down = vectors
        arrays = (z1, x1, y1, *d1, *c1, *core_swap(*d1))
        qkv_full = Weight(arrays, blocks=GROUPS, step=3 * width // GROUPS)
        out_full = Weight(arrays, base=cut_qkv.wide, blocks=2, step=cut_out.wide)
        x2, y2 = swap(z2, "x"), swap(z2, "y")
        normed_a, joint = project(place, tokens, gain_a, shift_a, qkv_full, bias_qv)
        joint, third = tie(joint, third)
        z3 = exchange(third, "z")
        joint, x2, y2, c_z2, normed_a, cotangent = tie(joint, x2, y2, swap(z2, "c"), normed_a, cotangent)
        joint = joint.reshape(images, slots, 3 * width)
        d2, c2 = corner(x2, y2), (c_z2, *core_swap(x2, y2))
        context, lse = attention(key_bias, joint)
        context, d2, c2, z3, cot = tie(
            context.reshape(rows, width), d2, c2, z3, cot + by_image(cotangent, [members - 1])
        )
        cot = in_images(cot)
        x3, y3 = swap(z3, "x"), swap(z3, "y")
        up_full = Weight((z2, x2, y2, *d2, *c2, *core_swap(*d2)), blocks=cut_up.columns // STEP)
        middle, normed_b, hidden, slope, hidden_other = expand(
            place, tokens, context, out_full, bias_out, gain_b, shift_b, up_full, bias_up
        )
        grad_out = jnp.where(valid, cot, jnp.zeros_like(cot))
        hidden, hidden_other, slope, x3, y3, c_z3, grad_out, out_sib = tie(
            hidden, hidden_other, slope, x3, y3, swap(z3, "c"), grad_out, swap(grad_out, "c")
        )
    else:
        vectors = unpack(lax.all_gather(packed, FSDP, axis=0))
        gain_a, shift_a, bias_qv, bias_out, gain_b, shift_b, bias_up, bias_down = vectors
        place = jnp.zeros((3,), jnp.int32)
        qkv_full, out_full, up_full, down_full = (
            Weight([lax.all_gather(w, FSDP, axis=0, tiled=True)], by_rows=w is down_weight)
            for w in (grouped(attn_weight), out_weight, up_weight, down_weight)
        )
        qkv_full.step, out_full.step = 3 * width // GROUPS, width // 2
        tokens = in_images(by_image(tokens))
        cot = in_images(by_image(cotangent))
        grad_out = jnp.where(valid, cot, jnp.zeros_like(cot))
        normed_a, joint = project(place, tokens, gain_a, shift_a, qkv_full, bias_qv)
        joint = joint.reshape(images, slots, 3 * width)
        context, lse = attention(key_bias, joint)
        context = context.reshape(rows, width)
        middle, normed_b, hidden, slope, hidden_other = expand(
            place, tokens, context, out_full, bias_out, gain_b, shift_b, up_full, bias_up
        )

    g_bias_down = jnp.sum(grad_out.astype(F32), axis=0, keepdims=True)
    valid_wide = valid.astype(F32)

    def back_attention(grad_context, group):
        saved = (lse, context.reshape(images, slots, width), grad_context)
        grad = attention(key_bias, joint, saved, group)
        return grad.reshape(rows, 3 * width // GROUPS)

    shard_count = lax.axis_size(FSDP)
    depth = lax.axis_size("z")
    if staged:
        d3, c3 = corner(x3, y3), (c_z3, *core_swap(x3, y3))
        down_parts = grad_parts([(hidden, swap(hidden_other, "c"), grad_out, out_sib, 0, 0)], cut_down, depth)
        down_parts, slope, d3, c3, hidden, g_bias_down, valid_wide = tie(
            down_parts, slope, d3, c3, hidden, g_bias_down, valid_wide
        )
        down_full = Weight((z3, x3, y3, *d3, *c3, *core_swap(*d3)), by_rows=True)
        down_e = swap(down_parts[3], "y")
        grad_pre, bias_up_sums, grad_middle, grad_branch, grad_context, sums_b = back(
            place, grad_out, down_full, slope, up_full, middle, gain_b, out_full
        )
        grad_pre, down_e, grad_context, grad_branch, context_sib, normed_sib_b, normed_sib = tie(
            grad_pre, down_e, grad_context, grad_branch, swap(context, "c"), swap(normed_b, "c"), swap(normed_a, "c")
        )
        grad_context = grad_context.reshape(images, slots, width)
        pre_sib, branch_sib = swap(grad_pre, "c"), swap(grad_branch, "c")
        down_x, down_y = swap(add(down_parts[1], down_e), "x"), swap(down_parts[2], "y")
        joint_0 = back_attention(grad_context, 0)
        joint_0, grad_context, pre_sib, branch_sib = tie(joint_0, grad_context, pre_sib, branch_sib)
        half = cut_up.wide // 512 // 2
        up_job = (normed_b, normed_sib_b, grad_pre, pre_sib)
        a_parts = grad_parts([up_job + (0, half)], cut_up, depth)
        joint_0_sib = swap(joint_0, "c")
        a_parts, grad_context = tie(a_parts, grad_context)
        a_e = swap(a_parts[3], "y")
        out_job = (context, context_sib, grad_branch, branch_sib, 0, cut_out.wide // 512)
        b_parts = grad_parts([up_job + (half, half), out_job], cut_up, depth)
        b_parts, grad_context, a_e, down_x, down_y = tie(b_parts, grad_context, a_e, down_x, down_y)
        a_x, a_y = swap(add(a_parts[1], a_e), "x"), swap(a_parts[2], "y")
        b_e = swap(b_parts[3], "y")
        down_b = grad_z(down_parts, down_x, down_y)
        qkv_job = lambda joint, sib: [(normed_a, normed_sib, joint, sib, 0, 1)]
        parts_0 = grad_parts(qkv_job(joint_0, joint_0_sib), cut_group, depth, cut_group.wide)
        parts_0, grad_context = tie(parts_0, grad_context)
        e_0 = swap(parts_0[3], "x")
        joint_1 = back_attention(grad_context, 1)
        joint_1, e_0, a_x, a_y, b_e, down_b, hidden = tie(joint_1, e_0, a_x, a_y, b_e, down_b, hidden)
        b_x, b_y = swap(add(b_parts[1], b_e), "x"), swap(b_parts[2], "y")
        a_z = grad_z(a_parts, a_x, a_y)
        x_0, y_0 = swap(parts_0[1], "x"), swap(add(parts_0[2], e_0), "y")
        parts_1 = grad_parts(qkv_job(joint_1, swap(joint_1, "c")), cut_group, depth, cut_group.wide)
        parts_1, joint_1 = tie(parts_1, joint_1)
        e_1 = swap(parts_1[3], "y")
        input_grad, joint_sums, sums_a = back_input(place, joint_0, joint_1, qkv_full, tokens, gain_a, grad_middle)
        packed = pack(shard_count, sums_a, joint_sums, sums_b, bias_up_sums, g_bias_down)
        input_grad, e_1, x_0, y_0, b_x, b_y, a_z, hidden, down_b, packed = tie(
            input_grad, e_1, x_0, y_0, b_x, b_y, a_z, hidden, down_b, packed
        )
        x_1, y_1 = swap(add(parts_1[1], e_1), "x"), swap(parts_1[2], "y")
        b_z = grad_z(b_parts, b_x, b_y)
        result = finish(place, hidden, down_full, middle, bias_down, valid_wide)
    else:
        grad_pre, bias_up_sums, grad_middle, grad_branch, grad_context, sums_b = back(
            place,
            grad_out, down_full, slope, up_full, middle, gain_b, out_full
        )
        grad_context = grad_context.reshape(images, slots, width)
        joint_0, joint_1 = (back_attention(grad_context, g) for g in range(GROUPS))
        input_grad, joint_sums, sums_a = back_input(place, joint_0, joint_1, qkv_full, tokens, gain_a, grad_middle)
        grad_joint = jnp.concatenate([joint_0, joint_1], axis=1)
        result = finish(place, hidden, down_full, middle, bias_down, valid_wide)

    if not staged:
        group = 3 * width // GROUPS
        joint_sums = ungrouped([joint_sums[:, g * group : (g + 1) * group] for g in range(GROUPS)])
        g_bias_qv = jnp.concatenate([joint_sums[:, :width], joint_sums[:, 2 * width :]], axis=1)
        small_grads = (sums_a[0], sums_a[1], g_bias_qv, sums_b[2], sums_b[0], sums_b[1], bias_up_sums, g_bias_down)
        packed = jnp.concatenate([v.reshape(shard_count, -1) for v in small_grads], axis=1)
    if staged:
        packed = packed + swap(packed, "c")
        packed = packed + swap(packed, "x")
        x_1, y_1, b_z, result, input_grad, packed, a_g, down_g = tie(
            x_1, y_1, b_z, result, input_grad, packed, grad_x(a_z), grad_x(down_b)
        )
        qkv_b = grad_z(
            tuple(jnp.concatenate([p, q], axis=2) for p, q in zip(parts_0[:1], parts_1[:1])),
            jnp.concatenate([x_0, x_1], axis=2),
            jnp.concatenate([y_0, y_1], axis=2),
        )
        outs = by_slot(input_grad, result)
        early, late = outs[:-1], outs[-1]
        qkv_b, b_g, packed, a_g, down_g, early = tie(qkv_b, grad_x(b_z), over_line(over_rows(packed)), a_g, down_g, early)
        b_g, a_g, down_g = (grad_core(*v) for v in (b_g, a_g, down_g))
        mine, from_x = grad_x(qkv_b)
        half, n_out, n_qkv = cut_up.wide // 2, cut_out.wide, cut_group.wide
        up_plan = [(0, 0, half, (0, 2 * half)), (1, 0, half, (half, 3 * half))]
        g_up, g_out, g_down = shards_of(
            (a_g, b_g, down_g),
            [
                (False, up_weight.shape, up_plan),
                (False, out_weight.shape, [(1, half, n_out, (0, n_out))]),
                (True, down_weight.shape, [(2, 0, width, None)]),
            ],
        )
        g_up, g_out, g_down, packed, late, from_x = tie(g_up, g_out, g_down, packed, late, from_x)
        outs = early + [late]
        qkv_g = grad_core(mine, from_x)
        part = width // GROUPS
        qkv_plan = []
        for g in range(GROUPS):
            for low in range(0, n_qkv, LANES):
                places = [divmod(c * n_qkv + low, part) for c in range(2)]
                places = [t * width + g * part + at for t, at in places]
                qkv_plan.append((0, g * n_qkv + low, LANES, places))
        (g_qkv,) = shards_of([qkv_g], [(False, attn_weight.shape, qkv_plan)])
    else:
        outs = by_slot(input_grad, result)
        packed = lax.psum_scatter(packed, FSDP, scatter_dimension=0)
        packed = lax.psum(packed, SEQ)
        g_qkv, g_out, g_up, g_down = (
            scatter_plain(a, g)
            for a, g in ((normed_a, grad_joint), (context, grad_branch), (normed_b, grad_pre), (hidden, grad_out))
        )
        g_qkv = ungrouped([g_qkv[:, : 3 * width // GROUPS], g_qkv[:, 3 * width // GROUPS :]])
    input_grad, layer_out = in_slots(outs)
    (g_gain_a, g_shift_a, g_bias_qv, g_bias_out, g_gain_b, g_shift_b, g_bias_up, g_bias_down) = (
        packed[c : c + n] for c, n in zip(cuts, sizes)
    )
    return (
        layer_out,
        input_grad,
        g_gain_a,
        g_shift_a,
        g_qkv,
        g_bias_qv,
        g_out,
        g_bias_out,
        g_gain_b,
        g_shift_b,
        g_up,
        g_bias_up,
        g_down,
        g_bias_down,
    )


def solution(mesh):
    shard_count, members = mesh.devices.shape
    fine = Mesh(mesh.devices.reshape(shard_count // 2, 2, members // 2, 2), FSDP + SEQ)
    rows, vector, matrix = P(FSDP, SEQ, None), P(FSDP), P(FSDP, None)
    weights = (vector, vector, matrix, vector, matrix, vector, vector, vector, matrix, vector, matrix, vector)
    return jax.shard_map(
        shards,
        mesh=fine,
        in_specs=(rows, vector) + weights + (rows,),
        out_specs=(rows, rows) + weights,
        check_vma=False,
    )
```

```python
import functools

import jax
import jax.numpy as jnp
from jax import lax
from jax.experimental import pallas as pl
from jax.experimental.pallas import tpu as pltpu
from jax.sharding import Mesh
from jax.sharding import PartitionSpec as P

HEAD_DIM = 64
LANES = 128
GROUPS = 2
TILES = 4
EPSILON = 1e-06
BF16 = jnp.bfloat16
F32 = jnp.float32
FSDP, SEQ = ("z", "y"), ("x", "c")


def cost(microseconds, nbytes=0):
    return pl.CostEstimate(flops=int(microseconds * 1.1e9), bytes_accessed=nbytes, transcendentals=0)


def norm_back(grad_norm, gain, normal, inv_std):
    scaled = grad_norm * gain
    return inv_std * (
        scaled
        - jnp.mean(scaled, axis=-1, keepdims=True)
        - normal * jnp.mean(scaled * normal, axis=-1, keepdims=True)
    )


def contract(a, b, ca, cb):
    return lax.dot_general(a, b, (((ca,), (cb,)), ((), ())), preferred_element_type=F32)


def lanes_of(shape):
    lane = lax.broadcasted_iota(jnp.int32, shape, 1)
    return lane // HEAD_DIM, lane % HEAD_DIM


def spread_over(places, place, columns, rest=0.0):
    out = jnp.full(place.shape, rest, F32)
    for i in places:
        out = jnp.where(place == i, columns[i], out)
    return out


def parts_of(value, count):
    parts = []
    for _ in range(count):
        parts.append(value.astype(BF16).astype(F32))
        value = value - parts[-1]
    return parts


SCALE = HEAD_DIM ** (-0.5)


def attend_kernel(bias_ref, q_ref, k_ref, v_ref, out_ref, lse_ref):
    bias = bias_ref[0]
    for tile in range(q_ref.shape[2] // LANES):
        at = slice(tile * LANES, (tile + 1) * LANES)
        q, k, v = (ref[0, :, at].astype(F32) for ref in (q_ref, k_ref, v_ref))
        head_of, place = lanes_of(q.shape)
        context, lse = jnp.zeros(q.shape, F32), jnp.zeros(q.shape, F32)
        for head in range(LANES // HEAD_DIM):
            own = head_of == head
            left = jnp.where(own, q * SCALE, spread_over((0,), place, (1.0,))).astype(BF16)
            right = jnp.where(own, k, spread_over((0,), place, (bias,))).astype(BF16)
            scores = contract(left, right, 1, 1)
            top = jnp.max(scores, axis=-1, keepdims=True)
            exps = jnp.exp(scores - top).astype(BF16)
            both = contract(exps, jnp.where(own, v, 1.0).astype(BF16), 1, 0)
            other = (1 - head) * HEAD_DIM
            total = both[:, other : other + 1]
            context = jnp.where(own, both * (1.0 / total), context)
            lse = jnp.where(own, lse, top + jnp.log(total))
        out_ref[0, :, at] = context.astype(BF16)
        lse_ref[0, :, at] = lse


def attend_back_kernel(bias_ref, q_ref, k_ref, v_ref, lse_ref, context_ref, g_ref, out_ref):
    bias = bias_ref[0]
    tiles = q_ref.shape[2] // LANES
    width = out_ref.shape[2] // 3
    for tile in range(tiles):
        at = slice(tile * LANES, (tile + 1) * LANES)
        q_low, k_low, g_low = q_ref[0, :, at], k_ref[0, :, at], g_ref[0, :, at]
        q, k, v, g, context = (ref[0, :, at].astype(F32) for ref in (q_ref, k_ref, v_ref, g_ref, context_ref))
        head_of, place = lanes_of(q.shape)
        dq, dk, dv = (jnp.zeros(q.shape, F32) for _ in range(3))
        lse_parts = [-part for part in parts_of(lse_ref[0, :, at], 3)] + [1.0]
        product = g * context
        for head in range(LANES // HEAD_DIM):
            own = head_of == head
            left = jnp.where(own, q * SCALE, spread_over(range(4), place, lse_parts)).astype(BF16)
            right = jnp.where(own, k, spread_over(range(4), place, (1.0, 1.0, 1.0, bias))).astype(BF16)
            probs = jnp.exp(contract(left, right, 1, 1))
            inner = jnp.sum(jnp.where(own, product, 0.0), axis=-1, keepdims=True)
            inner_parts = [-part for part in parts_of(inner, 2)]
            left = jnp.where(own, g, spread_over(range(2), place, inner_parts)).astype(BF16)
            right = jnp.where(own, v, spread_over(range(2), place, (1.0, 1.0))).astype(BF16)
            grad_scores = (probs * contract(left, right, 1, 1)).astype(BF16)
            dq = jnp.where(own, contract(grad_scores, k_low, 1, 0), dq)
            dk = jnp.where(own, contract(grad_scores, q_low, 0, 0), dk)
            dv = jnp.where(own, contract(probs.astype(BF16), g_low, 0, 0), dv)
        for block, value in enumerate((dq * SCALE, dk * SCALE, dv)):
            start = block * width + (pl.program_id(1) * tiles + tile) * LANES
            out_ref[0, :, pl.ds(pl.multiple_of(start, LANES), LANES)] = value.astype(BF16)


def attention(key_bias, joint, saved=(), group=0):
    images, slots, width = joint.shape[0], joint.shape[1], joint.shape[2] // 3
    lanes = TILES * LANES
    in_group = width // lanes // GROUPS
    back = len(saved) > 0
    pairs = in_group if back else in_group * GROUPS
    block = (1, slots, lanes)

    def spec(part):
        def index(i, h):
            h = h + group * in_group
            return i, 0, (h // in_group * 3 + part) * in_group + h % in_group

        return pl.BlockSpec(block, index)

    plain = pl.BlockSpec(block, lambda i, h: (i, 0, h + group * in_group))
    bias = pl.BlockSpec((1, slots, 1), lambda i, h: (i, 0, 0))
    whole = pl.BlockSpec((1, slots, 3 * pairs * lanes), lambda i, h: (i, 0, 0))
    shape = lambda columns, kind: jax.ShapeDtypeStruct((images, slots, columns), kind)
    return pl.pallas_call(
        attend_back_kernel if back else attend_kernel,
        grid=(images, pairs),
        in_specs=[bias] + [spec(part) for part in range(3)] + [plain] * len(saved),
        out_specs=whole if back else [plain, plain],
        out_shape=shape(3 * pairs * lanes, BF16) if back else [shape(width, BF16), shape(width, F32)],
        cost_estimate=cost((1.3 if back else 0.8) * images * pairs * TILES),
    )(key_bias, joint, joint, joint, *saved)


STEP = 1024


def stats(values):
    center = values - jnp.mean(values, axis=-1, keepdims=True)
    inv_std = lax.rsqrt(jnp.mean(center * center, axis=-1, keepdims=True) + EPSILON)
    return center * inv_std, inv_std


def column_sums(values):
    return jnp.sum(values, axis=0, keepdims=True)


def block_spec(shape, index=lambda j: 0, at=1):
    def position(j, place):
        value = index(j, place) if index.__code__.co_argcount == 2 else index(j)
        return (0, value) if at else (value, 0)

    return pl.BlockSpec(shape, position)


def whole_spec(array):
    return block_spec(array.shape)


def columns_spec(rows, index=lambda j: j, step=STEP):
    return block_spec((rows, step), index)


class Weight:
    def __init__(self, arrays, by_rows=False, base=0, blocks=None, step=STEP):
        self.arrays, self.by_rows, self.base, self.blocks, self.step = tuple(arrays), by_rows, base, blocks, step

    def specs(self):
        return [pl.BlockSpec(memory_space=pl.ANY)] * len(self.arrays)

    def copies(self, refs, place_ref, j, block, buf, sem):
        copy = lambda source, target: pltpu.make_async_copy(source, target, sem)
        if len(refs) == 1:
            at = pl.ds(pl.multiple_of(block * self.step, self.step), self.step)
            return [(None, [copy(refs[0].at[at] if self.by_rows else refs[0].at[:, at], buf)])]
        y, x, c = place_ref[0], place_ref[1], place_ref[2]
        depth, rows = refs[0].shape[0], refs[0].shape[1]

        def piece(owner, i, z):
            five = refs[5 * owner : 5 * owner + 5]
            if i < 3:
                return five[i].at[z]
            return five[3].at[z] if z < depth // 2 else five[4].at[z - depth // 2]

        found = []
        if not self.by_rows:
            half = self.blocks // 2
            lanes = pl.ds(pl.multiple_of(self.base + block % half * self.step, LANES), self.step)
            for owner in range(2):
                some = []
                for i in range(4):
                    for z in range(depth):
                        row = (2 * z + (y ^ (i // 2))) * 2 * rows + (x ^ (i % 2)) * rows
                        target = buf.at[pl.ds(pl.multiple_of(row, rows), rows)]
                        some.append(copy(piece(owner, i, z).at[:, lanes], target))
                found.append(((block // half == c) == (owner == 0), some))
            return found
        width = buf.shape[1]
        segments = refs[0].shape[2] // width
        for z in range(depth):
            some = []
            for owner in range(2):
                for i in range(4):
                    for k in range(segments):
                        row = (((y ^ (i // 2)) * 2 + (c ^ owner)) * 2 + (x ^ (i % 2))) * segments * rows + k * rows
                        source = piece(owner, i, z).at[:, pl.ds(k * width, width)]
                        some.append(copy(source, buf.at[pl.ds(pl.multiple_of(row, rows), rows)]))
            found.append((j == z, some))
        return found

    def start(self, *where):
        for condition, some in self.copies(*where):
            go = lambda some=some: [one.start() for one in some] and None
            go() if condition is None else pl.when(condition)(go)

    def wait(self, *where):
        for condition, some in self.copies(*where):
            go = lambda some=some: [one.wait() for one in some] and None
            go() if condition is None else pl.when(condition)(go)


def stream(weight, refs, place_ref, buf, sems):
    j = pl.program_id(0)

    def where(step):
        slot = step % 2
        return refs, place_ref, step, step, buf.at[slot], sems.at[slot]

    @pl.when(j == 0)
    def _():
        weight.start(*where(j))

    @pl.when(j + 1 < pl.num_programs(0))
    def _():
        weight.start(*where(j + 1))

    weight.wait(*where(j))
    return buf[j % 2]


def split_refs(refs, weights):
    groups = []
    for weight in weights:
        groups.append(refs[: len(weight.arrays)])
        refs = refs[len(weight.arrays) :]
    return groups, refs


def stepped(kernel, steps, place, weights, in_specs, operands, out_specs, out_shape, scratch, microseconds):
    specs = [spec for weight in weights for spec in weight.specs()]
    arrays = [v for weight in weights for v in weight.arrays]
    return pl.pallas_call(
        functools.partial(kernel, weights),
        grid_spec=pltpu.PrefetchScalarGridSpec(
            num_scalar_prefetch=1,
            grid=(steps,),
            in_specs=specs + in_specs,
            out_specs=out_specs,
            scratch_shapes=scratch,
        ),
        out_shape=out_shape,
        compiler_params=pltpu.CompilerParams(vmem_limit_bytes=56 << 20),
        cost_estimate=cost(microseconds),
    )(place, *arrays, *operands)


def streamed(rows, columns):
    return [pltpu.VMEM((2, rows, columns), BF16), pltpu.SemaphoreType.DMA((2,))]


def project_kernel(weights, place_ref, *refs):
    (weight_refs,), refs = split_refs(refs, weights)
    tokens_ref, gain_ref, shift_ref, query_ref, value_ref, normed_ref, joint_ref, buf, sems = refs

    @pl.when(pl.program_id(0) == 0)
    def _():
        normal, _ = stats(tokens_ref[...].astype(F32))
        normed_ref[...] = (normal * gain_ref[...] + shift_ref[...]).astype(BF16)

    weight = stream(weights[0], weight_refs, place_ref, buf, sems)
    bias = jnp.concatenate([query_ref[...], jnp.zeros_like(query_ref[...]), value_ref[...]], axis=1)
    joint_ref[...] = (contract(normed_ref[...], weight, 1, 0) + bias).astype(BF16)


def project(place, tokens, gain, shift, weight, bias_qv):
    rows, width = tokens.shape
    part = width // GROUPS
    return stepped(
        project_kernel,
        GROUPS,
        place,
        [weight],
        [whole_spec(tokens), whole_spec(gain), whole_spec(shift)]
        + [columns_spec(1, index, part) for index in (lambda j: j, lambda j: GROUPS + j)],
        (tokens, gain, shift, bias_qv, bias_qv),
        [whole_spec(tokens), columns_spec(rows, step=3 * part)],
        [jax.ShapeDtypeStruct((rows, width), BF16), jax.ShapeDtypeStruct((rows, 3 * width), BF16)],
        streamed(width, 3 * part),
        10,
    )


def out_blocks(weight, refs, place_ref, buf, sem):
    for block in range(buf.shape[0]):
        yield weight, (refs, place_ref, 0, block, buf.at[block], sem)


def expand_kernel(weights, place_ref, *refs):
    (up_refs, out_w_refs), refs = split_refs(refs, weights)
    tokens_ref, context_ref, bias_out_ref, gain_ref, shift_ref, bias_ref, *refs = refs
    middle_ref, normed_ref, hidden_ref, slope_ref, other_ref, buf, sems, out_buf, out_sem = refs

    @pl.when(pl.program_id(0) == 0)
    def _():
        blocks = list(out_blocks(weights[1], out_w_refs, place_ref, out_buf, out_sem))
        for weight, where in blocks:
            weight.start(*where)
        for weight, where in blocks:
            weight.wait(*where)
        context = context_ref[...]
        branch = jnp.concatenate([contract(context, out_buf[b], 1, 0) for b in range(out_buf.shape[0])], axis=1)
        middle = tokens_ref[...].astype(F32) + (branch + bias_out_ref[...])
        middle_ref[...] = middle
        normal, _ = stats(middle)
        normed_ref[...] = (normal * gain_ref[...] + shift_ref[...]).astype(BF16)

    weight = stream(weights[0], up_refs, place_ref, buf, sems)
    pre = contract(normed_ref[...], weight, 1, 0) + bias_ref[...]
    cumul = 0.5 * (1.0 + lax.erf(pre * 0.7071067811865476))
    hidden = (pre * cumul).astype(BF16)
    hidden_ref[...] = hidden
    half = 2 * LANES
    for i in range(other_ref.shape[1] // half):
        low, high = (hidden[:, (2 * i + k) * half : (2 * i + k + 1) * half] for k in range(2))
        other_ref[:, i * half : (i + 1) * half] = jnp.where(place_ref[2] == 0, high, low)
    slope = cumul + pre * (jnp.exp(-0.5 * pre * pre) * 0.3989422804014327)
    slope_ref[...] = slope.astype(BF16)


def expand(place, tokens, context, out_weight, bias_out, gain, shift, up, bias_up):
    rows, width = tokens.shape
    hidden = bias_up.shape[1]
    return stepped(
        expand_kernel,
        hidden // STEP,
        place,
        [up, out_weight],
        [whole_spec(v) for v in (tokens, context, bias_out, gain, shift)] + [columns_spec(1)],
        (tokens, context, bias_out, gain, shift, bias_up),
        [whole_spec(tokens)] * 2 + [columns_spec(rows)] * 2 + [columns_spec(rows, step=STEP // 2)],
        [jax.ShapeDtypeStruct((rows, width), F32), jax.ShapeDtypeStruct((rows, width), BF16)]
        + [jax.ShapeDtypeStruct((rows, n), BF16) for n in (hidden, hidden, hidden // 2)],
        streamed(width, STEP) + [pltpu.VMEM((width // out_weight.step, width, out_weight.step), BF16), pltpu.SemaphoreType.DMA],
        20,
    )


def accumulate(total_ref, part, first=None):
    j = pl.program_id(0)

    @pl.when(j == 0)
    def _():
        total_ref[...] = part if first is None else first() + part

    @pl.when(j > 0)
    def _():
        total_ref[...] += part


def finish_kernel(weights, place_ref, *refs):
    (down_refs,), refs = split_refs(refs, weights)
    hidden_ref, middle_ref, bias_ref, valid_ref, result_ref, total_ref, buf, sems = refs
    weight = stream(weights[0], down_refs, place_ref, buf, sems)
    part = contract(hidden_ref[...], weight, 1, 0)
    accumulate(total_ref, part, lambda: middle_ref[...] + bias_ref[...])

    @pl.when(pl.program_id(0) == pl.num_programs(0) - 1)
    def _():
        result_ref[...] = jnp.where(valid_ref[...] > 0.5, total_ref[...], 0.0).astype(BF16)


def finish(place, hidden, down, middle, bias_down, valid):
    rows, width = middle.shape
    return stepped(
        finish_kernel,
        hidden.shape[1] // STEP,
        place,
        [down],
        [columns_spec(rows)] + [whole_spec(v) for v in (middle, bias_down, valid)],
        (hidden, middle, bias_down, valid),
        whole_spec(middle),
        jax.ShapeDtypeStruct((rows, width), BF16),
        [pltpu.VMEM((rows, width), F32)] + streamed(STEP, width),
        11,
    )


def back_kernel(weights, place_ref, *refs):
    (down_refs, up_refs, out_w_refs), refs = split_refs(refs, weights)
    grad_ref, slope_ref, middle_ref, gain_ref, *refs = refs
    pre_ref, bias_up_ref, grad_middle_ref, branch_ref, context_ref, sums_ref, total_ref, *refs = refs
    down_buf, down_sems, up_buf, up_sems, out_buf, out_sem = refs
    j = pl.program_id(0)
    blocks = lambda: out_blocks(weights[2], out_w_refs, place_ref, out_buf, out_sem)

    @pl.when(j == 0)
    def _():
        for weight, where in blocks():
            weight.start(*where)

    down = stream(weights[0], down_refs, place_ref, down_buf, down_sems)
    up = stream(weights[1], up_refs, place_ref, up_buf, up_sems)
    pre = (contract(grad_ref[...], down, 1, 1) * slope_ref[...].astype(F32)).astype(BF16)
    pre_ref[...] = pre
    bias_up_ref[...] = column_sums(pre.astype(F32))
    accumulate(total_ref, contract(pre, up, 1, 1))

    @pl.when(j == pl.num_programs(0) - 1)
    def _():
        for weight, where in blocks():
            weight.wait(*where)
        normal, inv_std = stats(middle_ref[...])
        total = total_ref[...]
        grad_middle = grad_ref[...].astype(F32) + norm_back(total, gain_ref[...], normal, inv_std)
        grad_middle_ref[...] = grad_middle
        branch = grad_middle.astype(BF16)
        branch_ref[...] = branch
        context_ref[...] = sum(
            contract(branch[:, b * out_buf.shape[2] : (b + 1) * out_buf.shape[2]], out_buf[b], 1, 1)
            for b in range(out_buf.shape[0])
        ).astype(BF16)
        sums_ref[0:1] = column_sums(total * normal)
        sums_ref[1:2] = column_sums(total)
        sums_ref[2:3] = column_sums(branch.astype(F32))


def back(place, grad_out, down, slope, up, middle, gain, out_weight):
    rows, width = middle.shape
    hidden = slope.shape[1]
    return stepped(
        back_kernel,
        hidden // STEP,
        place,
        [down, up, out_weight],
        [whole_spec(grad_out), columns_spec(rows), whole_spec(middle), whole_spec(gain)],
        (grad_out, slope, middle, gain),
        [columns_spec(rows), columns_spec(1)]
        + [whole_spec(middle)] * 3
        + [block_spec((8, width))],
        [
            jax.ShapeDtypeStruct((rows, hidden), BF16),
            jax.ShapeDtypeStruct((1, hidden), F32),
            jax.ShapeDtypeStruct((rows, width), F32),
            jax.ShapeDtypeStruct((rows, width), BF16),
            jax.ShapeDtypeStruct((rows, width), BF16),
            jax.ShapeDtypeStruct((8, width), F32),
        ],
        [pltpu.VMEM((rows, width), F32)]
        + streamed(STEP, width)
        + streamed(width, STEP)
        + [pltpu.VMEM((width // out_weight.step, width, out_weight.step), BF16), pltpu.SemaphoreType.DMA],
        23,
    )


def input_kernel(weights, place_ref, *refs):
    (weight_refs,), refs = split_refs(refs, weights)
    joint_0_ref, joint_1_ref, tokens_ref, gain_ref, grad_middle_ref, *refs = refs
    input_ref, bias_ref, sums_ref, total_ref, buf, sems = refs
    j = pl.program_id(0)
    first = jnp.broadcast_to(j == 0, joint_0_ref.shape)
    joint = jnp.where(first, joint_0_ref[...], joint_1_ref[...])
    bias_ref[...] = column_sums(joint.astype(F32))
    weight = stream(weights[0], weight_refs, place_ref, buf, sems)
    accumulate(total_ref, contract(joint, weight, 1, 1))

    @pl.when(j == pl.num_programs(0) - 1)
    def _():
        normal, inv_std = stats(tokens_ref[...].astype(F32))
        total = total_ref[...]
        grad = grad_middle_ref[...] + norm_back(total, gain_ref[...], normal, inv_std)
        input_ref[...] = grad.astype(BF16)
        sums_ref[0:1] = column_sums(total * normal)
        sums_ref[1:2] = column_sums(total)


def back_input(place, joint_0, joint_1, weight, tokens, gain, grad_middle):
    rows, width = tokens.shape
    group = 3 * width // GROUPS
    return stepped(
        input_kernel,
        GROUPS,
        place,
        [weight],
        [whole_spec(v) for v in (joint_0, joint_1, tokens, gain, grad_middle)],
        (joint_0, joint_1, tokens, gain, grad_middle),
        [whole_spec(tokens), columns_spec(1, step=group), block_spec((8, width))],
        [
            jax.ShapeDtypeStruct((rows, width), BF16),
            jax.ShapeDtypeStruct((1, 3 * width), F32),
            jax.ShapeDtypeStruct((8, width), F32),
        ],
        [pltpu.VMEM((rows, width), F32)] + streamed(width, group),
        13,
    )


def grouped(value):
    width = value.shape[-1] // 3
    part = width // GROUPS
    return jnp.concatenate(
        [value[..., t * width + g * part :][..., :part] for g in range(GROUPS) for t in range(3)], axis=-1
    )


def ungrouped(values):
    part = values[0].shape[-1] // 3
    return jnp.concatenate(
        [v[..., t * part : (t + 1) * part] for t in range(3) for v in values], axis=-1
    )


def swap(value, axis):
    return lax.ppermute(value, axis, [(0, 1), (1, 0)])


def send(value, axis, step):
    return lax.ppermute(value, axis, [(i, i ^ step) for i in range(lax.axis_size(axis))])


def pick(blocks, index):
    return lax.dynamic_index_in_dim(blocks, index, 0, keepdims=False)


def tie(*values):
    return lax.optimization_barrier(values)


def after(value, *others):
    return lax.optimization_barrier((value,) + others)[0]


def my_place():
    return jnp.stack([lax.axis_index(n) for n in ("y", "x", "c")]).astype(jnp.int32)


class Split:
    def __init__(self, shard, by_rows=False, columns=None):
        self.shard_rows, self.columns = shard[0], columns or shard[1]
        self.by_rows = by_rows
        self.rows = self.shard_rows // 4 if by_rows else self.shard_rows // 2
        self.wide = self.columns if by_rows else self.columns // 2

def exchange(blocks, axis):
    return lax.all_to_all(blocks, axis, split_axis=0, concat_axis=0, tiled=True)


def pieces_kernel(depth, rows, place_ref, qkv_ref, out_ref, up_ref, down_ref, *refs):
    *vector_refs, first_ref, second_ref, third_ref = refs
    x, c = place_ref[1], place_ref[2]
    at = pl.ds(pl.multiple_of(x * rows, rows), rows)

    def put(ref, lane, value):
        for z in range(depth):
            ref[z, : value.shape[0], lane : lane + value.shape[1]] = value
        return lane + value.shape[1]

    def columns(ref, start, count):
        return ref[at, pl.ds(pl.multiple_of(start, LANES), count)]

    width = out_ref.shape[1]
    part = width // 2
    lane = 0
    for t in range(3):
        lane = put(first_ref, lane, columns(qkv_ref, t * width + c * part, part))
    packed = jnp.concatenate([ref[...] for ref in vector_refs], axis=0)
    padding = jnp.zeros((rows - packed.shape[0], LANES), packed.dtype)
    put(first_ref, lane, jnp.concatenate([packed, padding], axis=0))
    half = up_ref.shape[1] // 2
    lane = put(second_ref, 0, columns(up_ref, c * half, half))
    put(second_ref, lane, columns(out_ref, c * part, part))
    blocks = down_ref.shape[0] // 4 // rows
    lane = 0
    for block in range(blocks):
        start = ((2 * c + x) * blocks + block) * rows
        lane = put(third_ref, lane, down_ref[pl.ds(pl.multiple_of(start, rows), rows), :])


def pieces(qkv, out, up, down, vectors):
    depth, rows = lax.axis_size("z"), qkv.shape[0] // 2
    vectors = [v.reshape(-1, LANES) for v in vectors]
    width = out.shape[1]
    wide = (3 * width // 2 + LANES, (up.shape[1] + width) // 2, down.shape[0] // 4 // rows * width)
    vmem = pl.BlockSpec(memory_space=pltpu.VMEM)
    return pl.pallas_call(
        functools.partial(pieces_kernel, depth, rows),
        in_specs=[pl.BlockSpec(memory_space=pltpu.SMEM)] + [vmem] * (4 + len(vectors)),
        out_specs=[vmem] * 3,
        out_shape=[jax.ShapeDtypeStruct((depth, rows, n), BF16) for n in wide],
        cost_estimate=cost(3),
    )(my_place(), qkv, out, up, down, *vectors)


def corner(from_x, from_y):
    half = from_x.shape[0] // 2
    return swap(from_x[:half], "y"), swap(from_y[half:], "x")


def core_swap(*pieces):
    return tuple(swap(v, "c") for v in pieces)


def my_place():
    return jnp.stack([lax.axis_index(n) for n in ("y", "x", "c")]).astype(jnp.int32)


def part_refs(x, near, far, rows, refs, at):
    own_ref, to_x_ref, to_y_ref, corner_ref = refs
    low, high = near[:rows], near[rows:]
    own_ref[at] = jnp.where(x == 0, low, high)
    to_x_ref[at] = jnp.where(x == 0, high, low)
    low, high = far[:rows], far[rows:]
    to_y_ref[at] = jnp.where(x == 0, low, high)
    corner_ref[at] = jnp.where(x == 0, high, low)


def grad_columns_kernel(ends, cut, place_ref, *refs):
    y, x = place_ref[0], place_ref[1]
    out_refs = refs[-4:]
    j = pl.program_id(0)

    def one(a_ref, a_sib_ref, g_ref, g_sib_ref):
        total = contract(a_ref[...], g_ref[...], 0, 0) + contract(a_sib_ref[...], g_sib_ref[...], 0, 0)
        total = total.reshape(-1, 2, cut.shard_rows, total.shape[1])
        for z in range(total.shape[0]):
            near = jnp.where(y == 0, total[z, 0], total[z, 1]).astype(BF16)
            far = jnp.where(y == 0, total[z, 1], total[z, 0]).astype(BF16)
            part_refs(x, near, far, cut.rows, out_refs, z)

    if len(ends) == 1:
        one(*refs[:4])
        return
    for i, end in enumerate(ends):
        first = 0 if i == 0 else ends[i - 1]
        pl.when((j >= first) & (j < end))(functools.partial(one, *refs[4 * i : 4 * i + 4]))


def grad_rows_kernel(cut, place_ref, a0_ref, a1_ref, a0_sib_ref, a1_sib_ref, g_ref, g_sib_ref, *out_refs):
    y, x = place_ref[0], place_ref[1]
    by_y = [
        contract(ref[...], g_ref[...], 0, 0)
        + contract(sib_ref[...], g_sib_ref[...], 0, 0)
        for ref, sib_ref in ((a0_ref, a0_sib_ref), (a1_ref, a1_sib_ref))
    ]
    near = jnp.where(y == 0, by_y[0], by_y[1]).astype(BF16)
    far = jnp.where(y == 0, by_y[1], by_y[0]).astype(BF16)
    part_refs(x, near, far, cut.rows, out_refs, 0)


def grad_parts(jobs, cut, depth, step=512):
    tokens = jobs[0][0].shape[0]
    specs, operands, ends = [], [], []
    if cut.by_rows:
        ((a, a_sib, g, g_sib, _, _),) = jobs
        half = 2 * cut.rows
        every = pl.BlockSpec((tokens, cut.wide), lambda j, place: (0, 0))
        specs = [
            pl.BlockSpec((tokens, half), lambda j, place: (0, 4 * j + place[2])),
            pl.BlockSpec((tokens, half), lambda j, place: (0, 4 * j + 2 + place[2])),
            pl.BlockSpec((tokens, half), lambda j, place: (0, 2 * j)),
            pl.BlockSpec((tokens, half), lambda j, place: (0, 2 * j + 1)),
            every,
            every,
        ]
        operands, kernel, grid, wide = [a, a, a_sib, a_sib, g, g_sib], functools.partial(grad_rows_kernel, cut), depth, cut.wide
        out_spec = lambda n: pl.BlockSpec((1, n, wide), lambda j, place: (j, 0, 0))
    else:
        grid = 0
        for a, a_sib, g, g_sib, start, steps in jobs:
            in_half = g.shape[1] // 2 // step
            every = pl.BlockSpec((tokens, a.shape[1]), lambda j, place: (0, 0))
            at = lambda j, first=grid, steps=steps: jnp.clip(j - first, 0, steps - 1)
            specs += [
                every,
                every,
            ] + [
                pl.BlockSpec(
                    (tokens, step), lambda j, place, at=at, n=in_half, s=start: (0, place[2] * n + s + at(j))
                )
            ] * 2
            operands += [a, a_sib, g, g_sib]
            grid += steps
            ends.append(grid)
        kernel, wide = functools.partial(grad_columns_kernel, ends, cut), grid * step
        out_spec = lambda n: pl.BlockSpec((depth, n, step), lambda j, place: (0, 0, j))
    total = 8 * depth * cut.rows * wide
    return pl.pallas_call(
        kernel,
        grid_spec=pltpu.PrefetchScalarGridSpec(
            num_scalar_prefetch=1,
            grid=(grid,),
            in_specs=specs,
            out_specs=[out_spec(cut.rows)] * 4,
        ),
        out_shape=[jax.ShapeDtypeStruct((depth, cut.rows, wide), BF16)] * 4,
        compiler_params=pltpu.CompilerParams(vmem_limit_bytes=52 << 20),
        cost_estimate=cost(total * 2.2e-6),
    )(my_place(), *operands)


def add(one, other):
    return (one.astype(F32) + other.astype(F32)).astype(BF16)


def grad_z(parts, from_x, from_y):
    return exchange(sum(v.astype(F32) for v in (parts[0], from_x, from_y)).astype(BF16), "z")


def grad_x(blocks):
    mine = jnp.sum(blocks.astype(F32), axis=0).astype(BF16)
    return mine, swap(mine, "x")


def grad_core(mine, from_x):
    return mine, from_x, swap(mine, "c"), swap(from_x, "c")


def shard_kernel(plan, place_ref, *refs):
    x, c = place_ref[1], place_ref[2]
    parts, out_refs = refs[: -len(plan)], refs[-len(plan) :]
    for (by_rows, sources), out_ref in zip(plan, out_refs):
        column = 0
        for core in range(2):
            for number, start, count, at in sources:
                four = parts[4 * number : 4 * number + 4]
                rows = four[0].shape[0]
                for half in range(2):
                    both = [
                        jnp.where(c == core, four[i][:, start : start + count], four[2 + i][:, start : start + count])
                        for i in range(2)
                    ]
                    value = jnp.where(x == half, both[0], both[1]).astype(F32)
                    if by_rows:
                        row = (2 * core + half) * rows
                        out_ref[row : row + rows, :] = value
                    else:
                        out_ref[half * rows : (half + 1) * rows, at[core] : at[core] + count] = value


def shards_of(gradients, plan):
    parts = [v for gradient in gradients for v in gradient]
    vmem = pl.BlockSpec(memory_space=pltpu.VMEM)
    return pl.pallas_call(
        functools.partial(shard_kernel, [(by_rows, sources) for by_rows, _, sources in plan]),
        in_specs=[pl.BlockSpec(memory_space=pltpu.SMEM)] + [vmem] * len(parts),
        out_specs=[vmem] * len(plan),
        out_shape=[jax.ShapeDtypeStruct(shape, F32) for _, shape, _ in plan],
        cost_estimate=cost(2),
    )(my_place(), *parts)


def pack_kernel(sums_a_ref, joint_ref, sums_b_ref, up_ref, down_ref, out_ref):
    shards = out_ref.shape[0]
    width = down_ref.shape[1]
    part = width // GROUPS

    def put(at, count, source):
        for i in range(shards):
            out_ref[i : i + 1, at : at + count] = source(i, count)
        return at + count

    def plain(ref, row):
        return lambda i, n: ref[row : row + 1, i * n : (i + 1) * n]

    def query_value(i, n):
        value, at = divmod(i * n, width)
        group, at = divmod(at, part)
        start = (3 * group + 2 * value) * part + at
        return joint_ref[0:1, start : start + n]

    n = width // shards
    at = put(0, n, plain(sums_a_ref, 0))
    at = put(at, n, plain(sums_a_ref, 1))
    at = put(at, 2 * n, query_value)
    at = put(at, n, plain(sums_b_ref, 2))
    at = put(at, n, plain(sums_b_ref, 0))
    at = put(at, n, plain(sums_b_ref, 1))
    at = put(at, up_ref.shape[1] // shards, plain(up_ref, 0))
    put(at, n, plain(down_ref, 0))


def pack(shards, sums_a, joint_sums, sums_b, up_sums, down_sums):
    vmem = pl.BlockSpec(memory_space=pltpu.VMEM)
    columns = (9 - 1) * down_sums.shape[1] + up_sums.shape[1]
    return pl.pallas_call(
        pack_kernel,
        in_specs=[vmem] * 5,
        out_specs=vmem,
        out_shape=jax.ShapeDtypeStruct((shards, columns // shards), F32),
        cost_estimate=cost(1),
    )(sums_a, joint_sums, sums_b, up_sums, down_sums)


def in_order(index, mine, theirs, axis):
    first, second = jnp.where(index == 0, mine, theirs), jnp.where(index == 0, theirs, mine)
    return jnp.concatenate([first, second], axis=axis)


def order_vectors(own_y, other_y):
    y = lax.axis_index("y")
    rows = [jnp.where(y == 0, own_y, other_y), jnp.where(y == 0, other_y, own_y)]
    return jnp.stack(rows, axis=1).reshape(2 * own_y.shape[0], -1)


def over_rows(packed):
    y = lax.axis_index("y")
    packed = packed.reshape(lax.axis_size("z"), 2, -1)
    row = lambda yy: lax.dynamic_index_in_dim(packed, yy, 1, keepdims=False)
    return row(y) + swap(row(1 - y), "y")


def over_line(packed):
    z = lax.axis_index("z")
    return pick(packed, z) + sum(send(pick(packed, z ^ k), "z", k) for k in range(1, lax.axis_size("z")))


def scatter_plain(a, g):
    grad = lax.psum_scatter(contract(a, g, 0, 0).astype(BF16), FSDP, scatter_dimension=0, tiled=True)
    return lax.psum(grad, SEQ).astype(F32)


def shards(
    tokens,
    lengths,
    attn_gain,
    attn_shift,
    attn_weight,
    attn_bias,
    out_weight,
    out_bias,
    mlp_gain,
    mlp_shift,
    up_weight,
    up_bias,
    down_weight,
    down_bias,
    cotangent,
):
    width = tokens.shape[2]
    members = lax.axis_size(SEQ)
    staged = lax.axis_size("z") <= 8 and attn_weight.shape[0] % 128 == 0
    images = tokens.shape[0] // members
    slots = tokens.shape[1] * members
    rows = images * slots

    small = (attn_gain, attn_shift, attn_bias, out_bias, mlp_gain, mlp_shift, up_bias, down_bias)
    sizes = [v.shape[0] for v in small]
    cuts = [sum(sizes[:i]) for i in range(len(sizes))]
    packed = jnp.concatenate(small)

    few = tokens.shape[1]
    here = lax.axis_index(SEQ)
    lens = lax.dynamic_slice_in_dim(lengths, here * images, images, 0)
    slot = jnp.arange(slots, dtype=jnp.int32)
    slot = (slot // few ^ here) * few + slot % few
    valid = slot[None, :] < lens[:, None]
    key_bias = jnp.where(valid, 0.0, -1000000000.0)[:, :, None]
    valid = valid.reshape(rows, 1)

    def by_image(value, which=range(members)):
        value = value.reshape(members, images, few, width)
        return [send(pick(value, here ^ k), SEQ, k) if k else pick(value, here) for k in which]

    def by_slot(*values):
        value = jnp.concatenate([v.reshape(images, members, few, width) for v in values])
        return [send(value[:, k], SEQ, k) if k else value[:, 0] for k in range(members)]

    def in_images(blocks):
        return jnp.stack(blocks, axis=1).reshape(rows, width)

    def in_slots(blocks):
        blocks = jnp.stack(blocks)
        kinds = blocks.shape[1] // images
        blocks = jnp.concatenate([pick(blocks, here ^ k).reshape(kinds, images, few, width) for k in range(members)], axis=1)
        return [blocks[i] for i in range(kinds)]

    def unpack(vectors):
        vectors = vectors.astype(F32)
        return [vectors[:, c : c + n].reshape(1, -1) for c, n in zip(cuts, sizes)]

    if staged:
        cut_qkv, cut_out, cut_up = (Split(w.shape) for w in (attn_weight, out_weight, up_weight))
        cut_down = Split(down_weight.shape, by_rows=True)
        cut_group = Split(attn_weight.shape, columns=3 * width // GROUPS)
        place = my_place()
        first, second, third = pieces(attn_weight, out_weight, up_weight, down_weight, small)
        cot = by_image(cotangent, range(members - 1))
        tokens, cot, cotangent, z1, second, third = tie(
            by_image(tokens), cot, cotangent, exchange(first, "z"), second, third
        )
        tokens = in_images(tokens)
        x1, y1 = swap(z1, "x"), swap(z1, "y")
        z2 = exchange(second, "z")
        x1, y1, z1, third = tie(x1, y1, z1, third)
        vec_z, vec_y = (v[:, : sum(sizes) // LANES, -LANES:].reshape(v.shape[0], -1) for v in (z1, y1))
        vectors = unpack(order_vectors(vec_z, vec_y))
        d1, c1, z2, vectors, third, tokens = tie(
            corner(x1, y1), core_swap(z1, x1, y1), z2, vectors, third, tokens
        )
        gain_a, shift_a, bias_qv, bias_out, gain_b, shift_b, bias_up, bias_down = vectors
        arrays = (z1, x1, y1, *d1, *c1, *core_swap(*d1))
        qkv_full = Weight(arrays, blocks=GROUPS, step=3 * width // GROUPS)
        x2, y2 = swap(z2, "x"), swap(z2, "y")
        normed_a, joint = project(place, tokens, gain_a, shift_a, qkv_full, bias_qv)
        joint, third = tie(joint, third)
        z3 = exchange(third, "z")
        joint, x2, y2, c_z2, normed_a, cotangent = tie(joint, x2, y2, swap(z2, "c"), normed_a, cotangent)
        joint = joint.reshape(images, slots, 3 * width)
        d2, c2 = corner(x2, y2), (c_z2, *core_swap(x2, y2))
        context, lse = attention(key_bias, joint)
        context, d2, c2, z3, cot = tie(
            context.reshape(rows, width), d2, c2, z3, cot + by_image(cotangent, [members - 1])
        )
        cot = in_images(cot)
        x3, y3 = swap(z3, "x"), swap(z3, "y")
        arrays = (z2, x2, y2, *d2, *c2, *core_swap(*d2))
        up_full = Weight(arrays, blocks=cut_up.columns // STEP)
        out_full = Weight(arrays, base=cut_up.wide, blocks=2, step=cut_out.wide)
        middle, normed_b, hidden, slope, hidden_other = expand(
            place, tokens, context, out_full, bias_out, gain_b, shift_b, up_full, bias_up
        )
        grad_out = jnp.where(valid, cot, jnp.zeros_like(cot))
        hidden, hidden_other, slope, x3, y3, c_z3, grad_out, out_sib = tie(
            hidden, hidden_other, slope, x3, y3, swap(z3, "c"), grad_out, swap(grad_out, "c")
        )
    else:
        vectors = unpack(lax.all_gather(packed, FSDP, axis=0))
        gain_a, shift_a, bias_qv, bias_out, gain_b, shift_b, bias_up, bias_down = vectors
        place = jnp.zeros((3,), jnp.int32)
        qkv_full, out_full, up_full, down_full = (
            Weight([lax.all_gather(w, FSDP, axis=0, tiled=True)], by_rows=w is down_weight)
            for w in (grouped(attn_weight), out_weight, up_weight, down_weight)
        )
        qkv_full.step, out_full.step = 3 * width // GROUPS, width // 2
        tokens = in_images(by_image(tokens))
        cot = in_images(by_image(cotangent))
        grad_out = jnp.where(valid, cot, jnp.zeros_like(cot))
        normed_a, joint = project(place, tokens, gain_a, shift_a, qkv_full, bias_qv)
        joint = joint.reshape(images, slots, 3 * width)
        context, lse = attention(key_bias, joint)
        context = context.reshape(rows, width)
        middle, normed_b, hidden, slope, hidden_other = expand(
            place, tokens, context, out_full, bias_out, gain_b, shift_b, up_full, bias_up
        )

    g_bias_down = jnp.sum(grad_out.astype(F32), axis=0, keepdims=True)
    valid_wide = valid.astype(F32)

    def back_attention(grad_context, group):
        saved = (lse, context.reshape(images, slots, width), grad_context)
        grad = attention(key_bias, joint, saved, group)
        return grad.reshape(rows, 3 * width // GROUPS)

    shard_count = lax.axis_size(FSDP)
    depth = lax.axis_size("z")
    if staged:
        d3, c3 = corner(x3, y3), (c_z3, *core_swap(x3, y3))
        down_parts = grad_parts([(hidden, swap(hidden_other, "c"), grad_out, out_sib, 0, 0)], cut_down, depth)
        down_parts, slope, d3, c3, hidden, g_bias_down, valid_wide = tie(
            down_parts, slope, d3, c3, hidden, g_bias_down, valid_wide
        )
        down_full = Weight((z3, x3, y3, *d3, *c3, *core_swap(*d3)), by_rows=True)
        down_e = swap(down_parts[3], "y")
        grad_pre, bias_up_sums, grad_middle, grad_branch, grad_context, sums_b = back(
            place, grad_out, down_full, slope, up_full, middle, gain_b, out_full
        )
        grad_pre, down_e, grad_context, grad_branch, context_sib, normed_sib_b, normed_sib = tie(
            grad_pre, down_e, grad_context, grad_branch, swap(context, "c"), swap(normed_b, "c"), swap(normed_a, "c")
        )
        grad_context = grad_context.reshape(images, slots, width)
        pre_sib, branch_sib = swap(grad_pre, "c"), swap(grad_branch, "c")
        down_x, down_y = swap(add(down_parts[1], down_e), "x"), swap(down_parts[2], "y")
        joint_0 = back_attention(grad_context, 0)
        joint_0, grad_context, pre_sib, branch_sib = tie(joint_0, grad_context, pre_sib, branch_sib)
        half = cut_up.wide // 512 // 2
        up_job = (normed_b, normed_sib_b, grad_pre, pre_sib)
        a_parts = grad_parts([up_job + (0, half)], cut_up, depth)
        joint_0_sib = swap(joint_0, "c")
        a_parts, grad_context = tie(a_parts, grad_context)
        a_e = swap(a_parts[3], "y")
        out_job = (context, context_sib, grad_branch, branch_sib, 0, cut_out.wide // 512)
        b_parts = grad_parts([up_job + (half, half), out_job], cut_up, depth)
        b_parts, grad_context, a_e, down_x, down_y = tie(b_parts, grad_context, a_e, down_x, down_y)
        a_x, a_y = swap(add(a_parts[1], a_e), "x"), swap(a_parts[2], "y")
        b_e = swap(b_parts[3], "y")
        down_b = grad_z(down_parts, down_x, down_y)
        qkv_job = lambda joint, sib: [(normed_a, normed_sib, joint, sib, 0, 1)]
        parts_0 = grad_parts(qkv_job(joint_0, joint_0_sib), cut_group, depth, cut_group.wide)
        parts_0, grad_context = tie(parts_0, grad_context)
        e_0 = swap(parts_0[3], "x")
        joint_1 = back_attention(grad_context, 1)
        joint_1, e_0, a_x, a_y, b_e, down_b, hidden = tie(joint_1, e_0, a_x, a_y, b_e, down_b, hidden)
        b_x, b_y = swap(add(b_parts[1], b_e), "x"), swap(b_parts[2], "y")
        a_z = grad_z(a_parts, a_x, a_y)
        x_0, y_0 = swap(parts_0[1], "x"), swap(add(parts_0[2], e_0), "y")
        parts_1 = grad_parts(qkv_job(joint_1, swap(joint_1, "c")), cut_group, depth, cut_group.wide)
        parts_1, joint_1 = tie(parts_1, joint_1)
        e_1 = swap(parts_1[3], "y")
        input_grad, joint_sums, sums_a = back_input(place, joint_0, joint_1, qkv_full, tokens, gain_a, grad_middle)
        packed = pack(shard_count, sums_a, joint_sums, sums_b, bias_up_sums, g_bias_down)
        input_grad, e_1, x_0, y_0, b_x, b_y, a_z, hidden, down_b, packed = tie(
            input_grad, e_1, x_0, y_0, b_x, b_y, a_z, hidden, down_b, packed
        )
        x_1, y_1 = swap(add(parts_1[1], e_1), "x"), swap(parts_1[2], "y")
        b_z = grad_z(b_parts, b_x, b_y)
        result = finish(place, hidden, down_full, middle, bias_down, valid_wide)
    else:
        grad_pre, bias_up_sums, grad_middle, grad_branch, grad_context, sums_b = back(
            place,
            grad_out, down_full, slope, up_full, middle, gain_b, out_full
        )
        grad_context = grad_context.reshape(images, slots, width)
        joint_0, joint_1 = (back_attention(grad_context, g) for g in range(GROUPS))
        input_grad, joint_sums, sums_a = back_input(place, joint_0, joint_1, qkv_full, tokens, gain_a, grad_middle)
        grad_joint = jnp.concatenate([joint_0, joint_1], axis=1)
        result = finish(place, hidden, down_full, middle, bias_down, valid_wide)

    if not staged:
        group = 3 * width // GROUPS
        joint_sums = ungrouped([joint_sums[:, g * group : (g + 1) * group] for g in range(GROUPS)])
        g_bias_qv = jnp.concatenate([joint_sums[:, :width], joint_sums[:, 2 * width :]], axis=1)
        small_grads = (sums_a[0], sums_a[1], g_bias_qv, sums_b[2], sums_b[0], sums_b[1], bias_up_sums, g_bias_down)
        packed = jnp.concatenate([v.reshape(shard_count, -1) for v in small_grads], axis=1)
    if staged:
        packed = packed + swap(packed, "c")
        packed = packed + swap(packed, "x")
        x_1, y_1, b_z, result, input_grad, packed, a_g, down_g = tie(
            x_1, y_1, b_z, result, input_grad, packed, grad_x(a_z), grad_x(down_b)
        )
        qkv_b = grad_z(
            tuple(jnp.concatenate([p, q], axis=2) for p, q in zip(parts_0[:1], parts_1[:1])),
            jnp.concatenate([x_0, x_1], axis=2),
            jnp.concatenate([y_0, y_1], axis=2),
        )
        outs = by_slot(input_grad, result)
        early, late = outs[:-1], outs[-1]
        qkv_b, b_g, packed, a_g, down_g, early = tie(qkv_b, grad_x(b_z), over_line(over_rows(packed)), a_g, down_g, early)
        b_g, a_g, down_g = (grad_core(*v) for v in (b_g, a_g, down_g))
        mine, from_x = grad_x(qkv_b)
        half, n_out, n_qkv = cut_up.wide // 2, cut_out.wide, cut_group.wide
        up_plan = [(0, 0, half, (0, 2 * half)), (1, 0, half, (half, 3 * half))]
        g_up, g_out, g_down = shards_of(
            (a_g, b_g, down_g),
            [
                (False, up_weight.shape, up_plan),
                (False, out_weight.shape, [(1, half, n_out, (0, n_out))]),
                (True, down_weight.shape, [(2, 0, width, None)]),
            ],
        )
        g_up, g_out, g_down, packed, late, from_x = tie(g_up, g_out, g_down, packed, late, from_x)
        outs = early + [late]
        qkv_g = grad_core(mine, from_x)
        part = width // GROUPS
        qkv_plan = []
        for g in range(GROUPS):
            for low in range(0, n_qkv, LANES):
                places = [divmod(c * n_qkv + low, part) for c in range(2)]
                places = [t * width + g * part + at for t, at in places]
                qkv_plan.append((0, g * n_qkv + low, LANES, places))
        (g_qkv,) = shards_of([qkv_g], [(False, attn_weight.shape, qkv_plan)])
    else:
        outs = by_slot(input_grad, result)
        packed = lax.psum_scatter(packed, FSDP, scatter_dimension=0)
        packed = lax.psum(packed, SEQ)
        g_qkv, g_out, g_up, g_down = (
            scatter_plain(a, g)
            for a, g in ((normed_a, grad_joint), (context, grad_branch), (normed_b, grad_pre), (hidden, grad_out))
        )
        g_qkv = ungrouped([g_qkv[:, : 3 * width // GROUPS], g_qkv[:, 3 * width // GROUPS :]])
    input_grad, layer_out = in_slots(outs)
    (g_gain_a, g_shift_a, g_bias_qv, g_bias_out, g_gain_b, g_shift_b, g_bias_up, g_bias_down) = (
        packed[c : c + n] for c, n in zip(cuts, sizes)
    )
    return (
        layer_out,
        input_grad,
        g_gain_a,
        g_shift_a,
        g_qkv,
        g_bias_qv,
        g_out,
        g_bias_out,
        g_gain_b,
        g_shift_b,
        g_up,
        g_bias_up,
        g_down,
        g_bias_down,
    )


def solution(mesh):
    shard_count, members = mesh.devices.shape
    fine = Mesh(mesh.devices.reshape(shard_count // 2, 2, members // 2, 2), FSDP + SEQ)
    rows, vector, matrix = P(FSDP, SEQ, None), P(FSDP), P(FSDP, None)
    weights = (vector, vector, matrix, vector, matrix, vector, vector, vector, matrix, vector, matrix, vector)
    return jax.shard_map(
        shards,
        mesh=fine,
        in_specs=(rows, vector) + weights + (rows,),
        out_specs=(rows, rows) + weights,
        check_vma=False,
    )
```

```python
import functools

import jax
import jax.numpy as jnp
from jax import lax
from jax.experimental import pallas as pl
from jax.experimental.pallas import tpu as pltpu
from jax.sharding import Mesh
from jax.sharding import PartitionSpec as P

HEAD_DIM = 64
LANES = 128
GROUPS = 2
TILES = 2
EPSILON = 1e-06
BF16 = jnp.bfloat16
F32 = jnp.float32
FSDP, SEQ = ("z", "y"), ("x", "c")


def cost(microseconds, nbytes=0):
    return pl.CostEstimate(flops=int(microseconds * 1.1e9), bytes_accessed=nbytes, transcendentals=0)


def norm_back(grad_norm, gain, normal, inv_std):
    scaled = grad_norm * gain
    return inv_std * (
        scaled
        - jnp.mean(scaled, axis=-1, keepdims=True)
        - normal * jnp.mean(scaled * normal, axis=-1, keepdims=True)
    )


def contract(a, b, ca, cb):
    return lax.dot_general(a, b, (((ca,), (cb,)), ((), ())), preferred_element_type=F32)


def lanes_of(shape):
    lane = lax.broadcasted_iota(jnp.int32, shape, 1)
    return lane // HEAD_DIM, lane % HEAD_DIM


def spread_over(places, place, columns, rest=0.0):
    out = jnp.full(place.shape, rest, F32)
    for i in places:
        out = jnp.where(place == i, columns[i], out)
    return out


def parts_of(value, count):
    parts = []
    for _ in range(count):
        parts.append(value.astype(BF16).astype(F32))
        value = value - parts[-1]
    return parts


SCALE = HEAD_DIM ** (-0.5)


def attend_kernel(bias_ref, q_ref, k_ref, v_ref, out_ref, lse_ref):
    bias = bias_ref[0]
    for tile in range(q_ref.shape[2] // LANES):
        at = slice(tile * LANES, (tile + 1) * LANES)
        q, k, v = (ref[0, :, at].astype(F32) for ref in (q_ref, k_ref, v_ref))
        head_of, place = lanes_of(q.shape)
        context, lse = jnp.zeros(q.shape, F32), jnp.zeros(q.shape, F32)
        for head in range(LANES // HEAD_DIM):
            own = head_of == head
            left = jnp.where(own, q * SCALE, spread_over((0,), place, (1.0,))).astype(BF16)
            right = jnp.where(own, k, spread_over((0,), place, (bias,))).astype(BF16)
            scores = contract(left, right, 1, 1)
            top = jnp.max(scores, axis=-1, keepdims=True)
            exps = jnp.exp(scores - top).astype(BF16)
            both = contract(exps, jnp.where(own, v, 1.0).astype(BF16), 1, 0)
            other = (1 - head) * HEAD_DIM
            total = both[:, other : other + 1]
            context = jnp.where(own, both * (1.0 / total), context)
            lse = jnp.where(own, lse, top + jnp.log(total))
        out_ref[0, :, at] = context.astype(BF16)
        lse_ref[0, :, at] = lse


def attend_back_kernel(bias_ref, q_ref, k_ref, v_ref, lse_ref, context_ref, g_ref, out_ref):
    bias = bias_ref[0]
    tiles = q_ref.shape[2] // LANES
    width = out_ref.shape[2] // 3
    for tile in range(tiles):
        at = slice(tile * LANES, (tile + 1) * LANES)
        q_low, k_low, g_low = q_ref[0, :, at], k_ref[0, :, at], g_ref[0, :, at]
        q, k, v, g, context = (ref[0, :, at].astype(F32) for ref in (q_ref, k_ref, v_ref, g_ref, context_ref))
        head_of, place = lanes_of(q.shape)
        dq, dk, dv = (jnp.zeros(q.shape, F32) for _ in range(3))
        lse_parts = [-part for part in parts_of(lse_ref[0, :, at], 3)] + [1.0]
        product = g * context
        for head in range(LANES // HEAD_DIM):
            own = head_of == head
            left = jnp.where(own, q * SCALE, spread_over(range(4), place, lse_parts)).astype(BF16)
            right = jnp.where(own, k, spread_over(range(4), place, (1.0, 1.0, 1.0, bias))).astype(BF16)
            probs = jnp.exp(contract(left, right, 1, 1))
            inner = jnp.sum(jnp.where(own, product, 0.0), axis=-1, keepdims=True)
            inner_parts = [-part for part in parts_of(inner, 2)]
            left = jnp.where(own, g, spread_over(range(2), place, inner_parts)).astype(BF16)
            right = jnp.where(own, v, spread_over(range(2), place, (1.0, 1.0))).astype(BF16)
            grad_scores = (probs * contract(left, right, 1, 1)).astype(BF16)
            dq = jnp.where(own, contract(grad_scores, k_low, 1, 0), dq)
            dk = jnp.where(own, contract(grad_scores, q_low, 0, 0), dk)
            dv = jnp.where(own, contract(probs.astype(BF16), g_low, 0, 0), dv)
        for block, value in enumerate((dq * SCALE, dk * SCALE, dv)):
            start = block * width + (pl.program_id(1) * tiles + tile) * LANES
            out_ref[0, :, pl.ds(pl.multiple_of(start, LANES), LANES)] = value.astype(BF16)


def attention(key_bias, joint, saved=(), group=0):
    images, slots, width = joint.shape[0], joint.shape[1], joint.shape[2] // 3
    lanes = TILES * LANES
    in_group = width // lanes // GROUPS
    back = len(saved) > 0
    pairs = in_group if back else in_group * GROUPS
    block = (1, slots, lanes)

    def spec(part):
        def index(i, h):
            h = h + group * in_group
            return i, 0, (h // in_group * 3 + part) * in_group + h % in_group

        return pl.BlockSpec(block, index)

    plain = pl.BlockSpec(block, lambda i, h: (i, 0, h + group * in_group))
    bias = pl.BlockSpec((1, slots, 1), lambda i, h: (i, 0, 0))
    whole = pl.BlockSpec((1, slots, 3 * pairs * lanes), lambda i, h: (i, 0, 0))
    shape = lambda columns, kind: jax.ShapeDtypeStruct((images, slots, columns), kind)
    return pl.pallas_call(
        attend_back_kernel if back else attend_kernel,
        grid=(images, pairs),
        in_specs=[bias] + [spec(part) for part in range(3)] + [plain] * len(saved),
        out_specs=whole if back else [plain, plain],
        out_shape=shape(3 * pairs * lanes, BF16) if back else [shape(width, BF16), shape(width, F32)],
        cost_estimate=cost((1.3 if back else 0.8) * images * pairs * TILES),
    )(key_bias, joint, joint, joint, *saved)


STEP = 1024


def stats(values):
    center = values - jnp.mean(values, axis=-1, keepdims=True)
    inv_std = lax.rsqrt(jnp.mean(center * center, axis=-1, keepdims=True) + EPSILON)
    return center * inv_std, inv_std


def column_sums(values):
    return jnp.sum(values, axis=0, keepdims=True)


def block_spec(shape, index=lambda j: 0, at=1):
    def position(j, place):
        value = index(j, place) if index.__code__.co_argcount == 2 else index(j)
        return (0, value) if at else (value, 0)

    return pl.BlockSpec(shape, position)


def whole_spec(array):
    return block_spec(array.shape)


def columns_spec(rows, index=lambda j: j, step=STEP):
    return block_spec((rows, step), index)


class Weight:
    def __init__(self, arrays, by_rows=False, base=0, blocks=None, step=STEP):
        self.arrays, self.by_rows, self.base, self.blocks, self.step = tuple(arrays), by_rows, base, blocks, step

    def specs(self):
        return [pl.BlockSpec(memory_space=pl.ANY)] * len(self.arrays)

    def copies(self, refs, place_ref, j, block, buf, sem):
        copy = lambda source, target: pltpu.make_async_copy(source, target, sem)
        if len(refs) == 1:
            at = pl.ds(pl.multiple_of(block * self.step, self.step), self.step)
            return [(None, [copy(refs[0].at[at] if self.by_rows else refs[0].at[:, at], buf)])]
        y, x, c = place_ref[0], place_ref[1], place_ref[2]
        depth, rows = refs[0].shape[0], refs[0].shape[1]

        def piece(owner, i, z):
            five = refs[5 * owner : 5 * owner + 5]
            if i < 3:
                return five[i].at[z]
            return five[3].at[z] if z < depth // 2 else five[4].at[z - depth // 2]

        found = []
        if not self.by_rows:
            half = self.blocks // 2
            lanes = pl.ds(pl.multiple_of(self.base + block % half * self.step, LANES), self.step)
            for owner in range(2):
                some = []
                for i in range(4):
                    for z in range(depth):
                        row = (2 * z + (y ^ (i // 2))) * 2 * rows + (x ^ (i % 2)) * rows
                        target = buf.at[pl.ds(pl.multiple_of(row, rows), rows)]
                        some.append(copy(piece(owner, i, z).at[:, lanes], target))
                found.append(((block // half == c) == (owner == 0), some))
            return found
        width = buf.shape[1]
        segments = refs[0].shape[2] // width
        for z in range(depth):
            some = []
            for owner in range(2):
                for i in range(4):
                    for k in range(segments):
                        row = (((y ^ (i // 2)) * 2 + (c ^ owner)) * 2 + (x ^ (i % 2))) * segments * rows + k * rows
                        source = piece(owner, i, z).at[:, pl.ds(k * width, width)]
                        some.append(copy(source, buf.at[pl.ds(pl.multiple_of(row, rows), rows)]))
            found.append((j == z, some))
        return found

    def start(self, *where):
        for condition, some in self.copies(*where):
            go = lambda some=some: [one.start() for one in some] and None
            go() if condition is None else pl.when(condition)(go)

    def wait(self, *where):
        for condition, some in self.copies(*where):
            go = lambda some=some: [one.wait() for one in some] and None
            go() if condition is None else pl.when(condition)(go)


def stream(weight, refs, place_ref, buf, sems):
    j = pl.program_id(0)

    def where(step):
        slot = step % 2
        return refs, place_ref, step, step, buf.at[slot], sems.at[slot]

    @pl.when(j == 0)
    def _():
        weight.start(*where(j))

    @pl.when(j + 1 < pl.num_programs(0))
    def _():
        weight.start(*where(j + 1))

    weight.wait(*where(j))
    return buf[j % 2]


def split_refs(refs, weights):
    groups = []
    for weight in weights:
        groups.append(refs[: len(weight.arrays)])
        refs = refs[len(weight.arrays) :]
    return groups, refs


def stepped(kernel, steps, place, weights, in_specs, operands, out_specs, out_shape, scratch, microseconds):
    specs = [spec for weight in weights for spec in weight.specs()]
    arrays = [v for weight in weights for v in weight.arrays]
    return pl.pallas_call(
        functools.partial(kernel, weights),
        grid_spec=pltpu.PrefetchScalarGridSpec(
            num_scalar_prefetch=1,
            grid=(steps,),
            in_specs=specs + in_specs,
            out_specs=out_specs,
            scratch_shapes=scratch,
        ),
        out_shape=out_shape,
        compiler_params=pltpu.CompilerParams(vmem_limit_bytes=56 << 20),
        cost_estimate=cost(microseconds),
    )(place, *arrays, *operands)


def streamed(rows, columns):
    return [pltpu.VMEM((2, rows, columns), BF16), pltpu.SemaphoreType.DMA((2,))]


def project_kernel(weights, place_ref, *refs):
    (weight_refs,), refs = split_refs(refs, weights)
    tokens_ref, gain_ref, shift_ref, query_ref, value_ref, normed_ref, joint_ref, buf, sems = refs

    @pl.when(pl.program_id(0) == 0)
    def _():
        normal, _ = stats(tokens_ref[...].astype(F32))
        normed_ref[...] = (normal * gain_ref[...] + shift_ref[...]).astype(BF16)

    weight = stream(weights[0], weight_refs, place_ref, buf, sems)
    bias = jnp.concatenate([query_ref[...], jnp.zeros_like(query_ref[...]), value_ref[...]], axis=1)
    joint_ref[...] = (contract(normed_ref[...], weight, 1, 0) + bias).astype(BF16)


def project(place, tokens, gain, shift, weight, bias_qv):
    rows, width = tokens.shape
    part = width // GROUPS
    return stepped(
        project_kernel,
        GROUPS,
        place,
        [weight],
        [whole_spec(tokens), whole_spec(gain), whole_spec(shift)]
        + [columns_spec(1, index, part) for index in (lambda j: j, lambda j: GROUPS + j)],
        (tokens, gain, shift, bias_qv, bias_qv),
        [whole_spec(tokens), columns_spec(rows, step=3 * part)],
        [jax.ShapeDtypeStruct((rows, width), BF16), jax.ShapeDtypeStruct((rows, 3 * width), BF16)],
        streamed(width, 3 * part),
        10,
    )


def out_blocks(weight, refs, place_ref, buf, sem):
    for block in range(buf.shape[0]):
        yield weight, (refs, place_ref, 0, block, buf.at[block], sem)


def expand_kernel(weights, place_ref, *refs):
    (up_refs, out_w_refs), refs = split_refs(refs, weights)
    tokens_ref, context_ref, bias_out_ref, gain_ref, shift_ref, bias_ref, *refs = refs
    middle_ref, normed_ref, hidden_ref, slope_ref, other_ref, buf, sems, out_buf, out_sem = refs

    @pl.when(pl.program_id(0) == 0)
    def _():
        blocks = list(out_blocks(weights[1], out_w_refs, place_ref, out_buf, out_sem))
        for weight, where in blocks:
            weight.start(*where)
        for weight, where in blocks:
            weight.wait(*where)
        context = context_ref[...]
        branch = jnp.concatenate([contract(context, out_buf[b], 1, 0) for b in range(out_buf.shape[0])], axis=1)
        middle = tokens_ref[...].astype(F32) + (branch + bias_out_ref[...])
        middle_ref[...] = middle
        normal, _ = stats(middle)
        normed_ref[...] = (normal * gain_ref[...] + shift_ref[...]).astype(BF16)

    weight = stream(weights[0], up_refs, place_ref, buf, sems)
    pre = contract(normed_ref[...], weight, 1, 0) + bias_ref[...]
    cumul = 0.5 * (1.0 + lax.erf(pre * 0.7071067811865476))
    hidden = (pre * cumul).astype(BF16)
    hidden_ref[...] = hidden
    half = 2 * LANES
    for i in range(other_ref.shape[1] // half):
        low, high = (hidden[:, (2 * i + k) * half : (2 * i + k + 1) * half] for k in range(2))
        other_ref[:, i * half : (i + 1) * half] = jnp.where(place_ref[2] == 0, high, low)
    slope = cumul + pre * (jnp.exp(-0.5 * pre * pre) * 0.3989422804014327)
    slope_ref[...] = slope.astype(BF16)


def expand(place, tokens, context, out_weight, bias_out, gain, shift, up, bias_up):
    rows, width = tokens.shape
    hidden = bias_up.shape[1]
    return stepped(
        expand_kernel,
        hidden // STEP,
        place,
        [up, out_weight],
        [whole_spec(v) for v in (tokens, context, bias_out, gain, shift)] + [columns_spec(1)],
        (tokens, context, bias_out, gain, shift, bias_up),
        [whole_spec(tokens)] * 2 + [columns_spec(rows)] * 2 + [columns_spec(rows, step=STEP // 2)],
        [jax.ShapeDtypeStruct((rows, width), F32), jax.ShapeDtypeStruct((rows, width), BF16)]
        + [jax.ShapeDtypeStruct((rows, n), BF16) for n in (hidden, hidden, hidden // 2)],
        streamed(width, STEP) + [pltpu.VMEM((width // out_weight.step, width, out_weight.step), BF16), pltpu.SemaphoreType.DMA],
        20,
    )


def accumulate(total_ref, part, first=None):
    j = pl.program_id(0)

    @pl.when(j == 0)
    def _():
        total_ref[...] = part if first is None else first() + part

    @pl.when(j > 0)
    def _():
        total_ref[...] += part


def finish_kernel(weights, place_ref, *refs):
    (down_refs,), refs = split_refs(refs, weights)
    hidden_ref, middle_ref, bias_ref, valid_ref, result_ref, total_ref, buf, sems = refs
    weight = stream(weights[0], down_refs, place_ref, buf, sems)
    part = contract(hidden_ref[...], weight, 1, 0)
    accumulate(total_ref, part, lambda: middle_ref[...] + bias_ref[...])

    @pl.when(pl.program_id(0) == pl.num_programs(0) - 1)
    def _():
        result_ref[...] = jnp.where(valid_ref[...] > 0.5, total_ref[...], 0.0).astype(BF16)


def finish(place, hidden, down, middle, bias_down, valid):
    rows, width = middle.shape
    return stepped(
        finish_kernel,
        hidden.shape[1] // STEP,
        place,
        [down],
        [columns_spec(rows)] + [whole_spec(v) for v in (middle, bias_down, valid)],
        (hidden, middle, bias_down, valid),
        whole_spec(middle),
        jax.ShapeDtypeStruct((rows, width), BF16),
        [pltpu.VMEM((rows, width), F32)] + streamed(STEP, width),
        11,
    )


def back_kernel(weights, place_ref, *refs):
    (down_refs, up_refs, out_w_refs), refs = split_refs(refs, weights)
    grad_ref, slope_ref, middle_ref, gain_ref, *refs = refs
    pre_ref, bias_up_ref, grad_middle_ref, branch_ref, context_ref, sums_ref, total_ref, *refs = refs
    down_buf, down_sems, up_buf, up_sems, out_buf, out_sem = refs
    j = pl.program_id(0)
    blocks = lambda: out_blocks(weights[2], out_w_refs, place_ref, out_buf, out_sem)

    @pl.when(j == 0)
    def _():
        for weight, where in blocks():
            weight.start(*where)

    down = stream(weights[0], down_refs, place_ref, down_buf, down_sems)
    up = stream(weights[1], up_refs, place_ref, up_buf, up_sems)
    pre = (contract(grad_ref[...], down, 1, 1) * slope_ref[...].astype(F32)).astype(BF16)
    pre_ref[...] = pre
    bias_up_ref[...] = column_sums(pre.astype(F32))
    accumulate(total_ref, contract(pre, up, 1, 1))

    @pl.when(j == pl.num_programs(0) - 1)
    def _():
        for weight, where in blocks():
            weight.wait(*where)
        normal, inv_std = stats(middle_ref[...])
        total = total_ref[...]
        grad_middle = grad_ref[...].astype(F32) + norm_back(total, gain_ref[...], normal, inv_std)
        grad_middle_ref[...] = grad_middle
        branch = grad_middle.astype(BF16)
        branch_ref[...] = branch
        context_ref[...] = sum(
            contract(branch[:, b * out_buf.shape[2] : (b + 1) * out_buf.shape[2]], out_buf[b], 1, 1)
            for b in range(out_buf.shape[0])
        ).astype(BF16)
        sums_ref[0:1] = column_sums(total * normal)
        sums_ref[1:2] = column_sums(total)
        sums_ref[2:3] = column_sums(branch.astype(F32))


def back(place, grad_out, down, slope, up, middle, gain, out_weight):
    rows, width = middle.shape
    hidden = slope.shape[1]
    return stepped(
        back_kernel,
        hidden // STEP,
        place,
        [down, up, out_weight],
        [whole_spec(grad_out), columns_spec(rows), whole_spec(middle), whole_spec(gain)],
        (grad_out, slope, middle, gain),
        [columns_spec(rows), columns_spec(1)]
        + [whole_spec(middle)] * 3
        + [block_spec((8, width))],
        [
            jax.ShapeDtypeStruct((rows, hidden), BF16),
            jax.ShapeDtypeStruct((1, hidden), F32),
            jax.ShapeDtypeStruct((rows, width), F32),
            jax.ShapeDtypeStruct((rows, width), BF16),
            jax.ShapeDtypeStruct((rows, width), BF16),
            jax.ShapeDtypeStruct((8, width), F32),
        ],
        [pltpu.VMEM((rows, width), F32)]
        + streamed(STEP, width)
        + streamed(width, STEP)
        + [pltpu.VMEM((width // out_weight.step, width, out_weight.step), BF16), pltpu.SemaphoreType.DMA],
        23,
    )


def input_kernel(weights, place_ref, *refs):
    (weight_refs,), refs = split_refs(refs, weights)
    joint_0_ref, joint_1_ref, tokens_ref, gain_ref, grad_middle_ref, *refs = refs
    input_ref, bias_ref, sums_ref, total_ref, buf, sems = refs
    j = pl.program_id(0)
    first = jnp.broadcast_to(j == 0, joint_0_ref.shape)
    joint = jnp.where(first, joint_0_ref[...], joint_1_ref[...])
    bias_ref[...] = column_sums(joint.astype(F32))
    weight = stream(weights[0], weight_refs, place_ref, buf, sems)
    accumulate(total_ref, contract(joint, weight, 1, 1))

    @pl.when(j == pl.num_programs(0) - 1)
    def _():
        normal, inv_std = stats(tokens_ref[...].astype(F32))
        total = total_ref[...]
        grad = grad_middle_ref[...] + norm_back(total, gain_ref[...], normal, inv_std)
        input_ref[...] = grad.astype(BF16)
        sums_ref[0:1] = column_sums(total * normal)
        sums_ref[1:2] = column_sums(total)


def back_input(place, joint_0, joint_1, weight, tokens, gain, grad_middle):
    rows, width = tokens.shape
    group = 3 * width // GROUPS
    return stepped(
        input_kernel,
        GROUPS,
        place,
        [weight],
        [whole_spec(v) for v in (joint_0, joint_1, tokens, gain, grad_middle)],
        (joint_0, joint_1, tokens, gain, grad_middle),
        [whole_spec(tokens), columns_spec(1, step=group), block_spec((8, width))],
        [
            jax.ShapeDtypeStruct((rows, width), BF16),
            jax.ShapeDtypeStruct((1, 3 * width), F32),
            jax.ShapeDtypeStruct((8, width), F32),
        ],
        [pltpu.VMEM((rows, width), F32)] + streamed(width, group),
        13,
    )


def grouped(value):
    width = value.shape[-1] // 3
    part = width // GROUPS
    return jnp.concatenate(
        [value[..., t * width + g * part :][..., :part] for g in range(GROUPS) for t in range(3)], axis=-1
    )


def ungrouped(values):
    part = values[0].shape[-1] // 3
    return jnp.concatenate(
        [v[..., t * part : (t + 1) * part] for t in range(3) for v in values], axis=-1
    )


def swap(value, axis):
    return lax.ppermute(value, axis, [(0, 1), (1, 0)])


def send(value, axis, step):
    return lax.ppermute(value, axis, [(i, i ^ step) for i in range(lax.axis_size(axis))])


def pick(blocks, index):
    return lax.dynamic_index_in_dim(blocks, index, 0, keepdims=False)


def tie(*values):
    return lax.optimization_barrier(values)


def after(value, *others):
    return lax.optimization_barrier((value,) + others)[0]


def my_place():
    return jnp.stack([lax.axis_index(n) for n in ("y", "x", "c")]).astype(jnp.int32)


class Split:
    def __init__(self, shard, by_rows=False, columns=None):
        self.shard_rows, self.columns = shard[0], columns or shard[1]
        self.by_rows = by_rows
        self.rows = self.shard_rows // 4 if by_rows else self.shard_rows // 2
        self.wide = self.columns if by_rows else self.columns // 2

def exchange(blocks, axis):
    return lax.all_to_all(blocks, axis, split_axis=0, concat_axis=0, tiled=True)


def pieces_kernel(depth, rows, place_ref, qkv_ref, out_ref, up_ref, down_ref, *refs):
    *vector_refs, first_ref, second_ref, third_ref = refs
    x, c = place_ref[1], place_ref[2]
    at = pl.ds(pl.multiple_of(x * rows, rows), rows)

    def put(ref, lane, value):
        for z in range(depth):
            ref[z, : value.shape[0], lane : lane + value.shape[1]] = value
        return lane + value.shape[1]

    def columns(ref, start, count):
        return ref[at, pl.ds(pl.multiple_of(start, LANES), count)]

    width = out_ref.shape[1]
    part = width // 2
    lane = 0
    for t in range(3):
        lane = put(first_ref, lane, columns(qkv_ref, t * width + c * part, part))
    packed = jnp.concatenate([ref[...] for ref in vector_refs], axis=0)
    padding = jnp.zeros((rows - packed.shape[0], LANES), packed.dtype)
    put(first_ref, lane, jnp.concatenate([packed, padding], axis=0))
    half = up_ref.shape[1] // 2
    lane = put(second_ref, 0, columns(up_ref, c * half, half))
    put(second_ref, lane, columns(out_ref, c * part, part))
    blocks = down_ref.shape[0] // 4 // rows
    lane = 0
    for block in range(blocks):
        start = ((2 * c + x) * blocks + block) * rows
        lane = put(third_ref, lane, down_ref[pl.ds(pl.multiple_of(start, rows), rows), :])


def pieces(qkv, out, up, down, vectors):
    depth, rows = lax.axis_size("z"), qkv.shape[0] // 2
    vectors = [v.reshape(-1, LANES) for v in vectors]
    width = out.shape[1]
    wide = (3 * width // 2 + LANES, (up.shape[1] + width) // 2, down.shape[0] // 4 // rows * width)
    vmem = pl.BlockSpec(memory_space=pltpu.VMEM)
    return pl.pallas_call(
        functools.partial(pieces_kernel, depth, rows),
        in_specs=[pl.BlockSpec(memory_space=pltpu.SMEM)] + [vmem] * (4 + len(vectors)),
        out_specs=[vmem] * 3,
        out_shape=[jax.ShapeDtypeStruct((depth, rows, n), BF16) for n in wide],
        cost_estimate=cost(3),
    )(my_place(), qkv, out, up, down, *vectors)


def corner(from_x, from_y):
    half = from_x.shape[0] // 2
    return swap(from_x[:half], "y"), swap(from_y[half:], "x")


def core_swap(*pieces):
    return tuple(swap(v, "c") for v in pieces)


def my_place():
    return jnp.stack([lax.axis_index(n) for n in ("y", "x", "c")]).astype(jnp.int32)


def part_refs(x, near, far, rows, refs, at):
    own_ref, to_x_ref, to_y_ref, corner_ref = refs
    low, high = near[:rows], near[rows:]
    own_ref[at] = jnp.where(x == 0, low, high)
    to_x_ref[at] = jnp.where(x == 0, high, low)
    low, high = far[:rows], far[rows:]
    to_y_ref[at] = jnp.where(x == 0, low, high)
    corner_ref[at] = jnp.where(x == 0, high, low)


def grad_columns_kernel(ends, cut, place_ref, *refs):
    y, x = place_ref[0], place_ref[1]
    out_refs = refs[-4:]
    j = pl.program_id(0)

    def one(a_ref, a_sib_ref, g_ref, g_sib_ref):
        total = contract(a_ref[...], g_ref[...], 0, 0) + contract(a_sib_ref[...], g_sib_ref[...], 0, 0)
        total = total.reshape(-1, 2, cut.shard_rows, total.shape[1])
        for z in range(total.shape[0]):
            near = jnp.where(y == 0, total[z, 0], total[z, 1]).astype(BF16)
            far = jnp.where(y == 0, total[z, 1], total[z, 0]).astype(BF16)
            part_refs(x, near, far, cut.rows, out_refs, z)

    if len(ends) == 1:
        one(*refs[:4])
        return
    for i, end in enumerate(ends):
        first = 0 if i == 0 else ends[i - 1]
        pl.when((j >= first) & (j < end))(functools.partial(one, *refs[4 * i : 4 * i + 4]))


def grad_rows_kernel(cut, place_ref, a0_ref, a1_ref, a0_sib_ref, a1_sib_ref, g_ref, g_sib_ref, *out_refs):
    y, x = place_ref[0], place_ref[1]
    by_y = [
        contract(ref[...], g_ref[...], 0, 0)
        + contract(sib_ref[...], g_sib_ref[...], 0, 0)
        for ref, sib_ref in ((a0_ref, a0_sib_ref), (a1_ref, a1_sib_ref))
    ]
    near = jnp.where(y == 0, by_y[0], by_y[1]).astype(BF16)
    far = jnp.where(y == 0, by_y[1], by_y[0]).astype(BF16)
    part_refs(x, near, far, cut.rows, out_refs, 0)


def grad_parts(jobs, cut, depth, step=512):
    tokens = jobs[0][0].shape[0]
    specs, operands, ends = [], [], []
    if cut.by_rows:
        ((a, a_sib, g, g_sib, _, _),) = jobs
        half = 2 * cut.rows
        every = pl.BlockSpec((tokens, cut.wide), lambda j, place: (0, 0))
        specs = [
            pl.BlockSpec((tokens, half), lambda j, place: (0, 4 * j + place[2])),
            pl.BlockSpec((tokens, half), lambda j, place: (0, 4 * j + 2 + place[2])),
            pl.BlockSpec((tokens, half), lambda j, place: (0, 2 * j)),
            pl.BlockSpec((tokens, half), lambda j, place: (0, 2 * j + 1)),
            every,
            every,
        ]
        operands, kernel, grid, wide = [a, a, a_sib, a_sib, g, g_sib], functools.partial(grad_rows_kernel, cut), depth, cut.wide
        out_spec = lambda n: pl.BlockSpec((1, n, wide), lambda j, place: (j, 0, 0))
    else:
        grid = 0
        for a, a_sib, g, g_sib, start, steps in jobs:
            in_half = g.shape[1] // 2 // step
            every = pl.BlockSpec((tokens, a.shape[1]), lambda j, place: (0, 0))
            at = lambda j, first=grid, steps=steps: jnp.clip(j - first, 0, steps - 1)
            specs += [
                every,
                every,
            ] + [
                pl.BlockSpec(
                    (tokens, step), lambda j, place, at=at, n=in_half, s=start: (0, place[2] * n + s + at(j))
                )
            ] * 2
            operands += [a, a_sib, g, g_sib]
            grid += steps
            ends.append(grid)
        kernel, wide = functools.partial(grad_columns_kernel, ends, cut), grid * step
        out_spec = lambda n: pl.BlockSpec((depth, n, step), lambda j, place: (0, 0, j))
    total = 8 * depth * cut.rows * wide
    return pl.pallas_call(
        kernel,
        grid_spec=pltpu.PrefetchScalarGridSpec(
            num_scalar_prefetch=1,
            grid=(grid,),
            in_specs=specs,
            out_specs=[out_spec(cut.rows)] * 4,
        ),
        out_shape=[jax.ShapeDtypeStruct((depth, cut.rows, wide), BF16)] * 4,
        compiler_params=pltpu.CompilerParams(vmem_limit_bytes=52 << 20),
        cost_estimate=cost(total * 2.2e-6),
    )(my_place(), *operands)


def add(one, other):
    return (one.astype(F32) + other.astype(F32)).astype(BF16)


def grad_z(parts, from_x, from_y):
    return exchange(sum(v.astype(F32) for v in (parts[0], from_x, from_y)).astype(BF16), "z")


def grad_x(blocks):
    mine = jnp.sum(blocks.astype(F32), axis=0).astype(BF16)
    return mine, swap(mine, "x")


def grad_core(mine, from_x):
    return mine, from_x, swap(mine, "c"), swap(from_x, "c")


def shard_kernel(plan, place_ref, *refs):
    x, c = place_ref[1], place_ref[2]
    parts, out_refs = refs[: -len(plan)], refs[-len(plan) :]
    for (by_rows, sources), out_ref in zip(plan, out_refs):
        column = 0
        for core in range(2):
            for number, start, count, at in sources:
                four = parts[4 * number : 4 * number + 4]
                rows = four[0].shape[0]
                for half in range(2):
                    both = [
                        jnp.where(c == core, four[i][:, start : start + count], four[2 + i][:, start : start + count])
                        for i in range(2)
                    ]
                    value = jnp.where(x == half, both[0], both[1]).astype(F32)
                    if by_rows:
                        row = (2 * core + half) * rows
                        out_ref[row : row + rows, :] = value
                    else:
                        out_ref[half * rows : (half + 1) * rows, at[core] : at[core] + count] = value


def shards_of(gradients, plan):
    parts = [v for gradient in gradients for v in gradient]
    vmem = pl.BlockSpec(memory_space=pltpu.VMEM)
    return pl.pallas_call(
        functools.partial(shard_kernel, [(by_rows, sources) for by_rows, _, sources in plan]),
        in_specs=[pl.BlockSpec(memory_space=pltpu.SMEM)] + [vmem] * len(parts),
        out_specs=[vmem] * len(plan),
        out_shape=[jax.ShapeDtypeStruct(shape, F32) for _, shape, _ in plan],
        cost_estimate=cost(2),
    )(my_place(), *parts)


def pack_kernel(sums_a_ref, joint_ref, sums_b_ref, up_ref, down_ref, out_ref):
    shards = out_ref.shape[0]
    width = down_ref.shape[1]
    part = width // GROUPS

    def put(at, count, source):
        for i in range(shards):
            out_ref[i : i + 1, at : at + count] = source(i, count)
        return at + count

    def plain(ref, row):
        return lambda i, n: ref[row : row + 1, i * n : (i + 1) * n]

    def query_value(i, n):
        value, at = divmod(i * n, width)
        group, at = divmod(at, part)
        start = (3 * group + 2 * value) * part + at
        return joint_ref[0:1, start : start + n]

    n = width // shards
    at = put(0, n, plain(sums_a_ref, 0))
    at = put(at, n, plain(sums_a_ref, 1))
    at = put(at, 2 * n, query_value)
    at = put(at, n, plain(sums_b_ref, 2))
    at = put(at, n, plain(sums_b_ref, 0))
    at = put(at, n, plain(sums_b_ref, 1))
    at = put(at, up_ref.shape[1] // shards, plain(up_ref, 0))
    put(at, n, plain(down_ref, 0))


def pack(shards, sums_a, joint_sums, sums_b, up_sums, down_sums):
    vmem = pl.BlockSpec(memory_space=pltpu.VMEM)
    columns = (9 - 1) * down_sums.shape[1] + up_sums.shape[1]
    return pl.pallas_call(
        pack_kernel,
        in_specs=[vmem] * 5,
        out_specs=vmem,
        out_shape=jax.ShapeDtypeStruct((shards, columns // shards), F32),
        cost_estimate=cost(1),
    )(sums_a, joint_sums, sums_b, up_sums, down_sums)


def in_order(index, mine, theirs, axis):
    first, second = jnp.where(index == 0, mine, theirs), jnp.where(index == 0, theirs, mine)
    return jnp.concatenate([first, second], axis=axis)


def order_vectors(own_y, other_y):
    y = lax.axis_index("y")
    rows = [jnp.where(y == 0, own_y, other_y), jnp.where(y == 0, other_y, own_y)]
    return jnp.stack(rows, axis=1).reshape(2 * own_y.shape[0], -1)


def over_rows(packed):
    y = lax.axis_index("y")
    packed = packed.reshape(lax.axis_size("z"), 2, -1)
    row = lambda yy: lax.dynamic_index_in_dim(packed, yy, 1, keepdims=False)
    return row(y) + swap(row(1 - y), "y")


def over_line(packed):
    z = lax.axis_index("z")
    return pick(packed, z) + sum(send(pick(packed, z ^ k), "z", k) for k in range(1, lax.axis_size("z")))


def scatter_plain(a, g):
    grad = lax.psum_scatter(contract(a, g, 0, 0).astype(BF16), FSDP, scatter_dimension=0, tiled=True)
    return lax.psum(grad, SEQ).astype(F32)


def shards(
    tokens,
    lengths,
    attn_gain,
    attn_shift,
    attn_weight,
    attn_bias,
    out_weight,
    out_bias,
    mlp_gain,
    mlp_shift,
    up_weight,
    up_bias,
    down_weight,
    down_bias,
    cotangent,
):
    width = tokens.shape[2]
    members = lax.axis_size(SEQ)
    staged = lax.axis_size("z") <= 8 and attn_weight.shape[0] % 128 == 0
    images = tokens.shape[0] // members
    slots = tokens.shape[1] * members
    rows = images * slots

    small = (attn_gain, attn_shift, attn_bias, out_bias, mlp_gain, mlp_shift, up_bias, down_bias)
    sizes = [v.shape[0] for v in small]
    cuts = [sum(sizes[:i]) for i in range(len(sizes))]
    packed = jnp.concatenate(small)

    few = tokens.shape[1]
    here = lax.axis_index(SEQ)
    lens = lax.dynamic_slice_in_dim(lengths, here * images, images, 0)
    slot = jnp.arange(slots, dtype=jnp.int32)
    slot = (slot // few ^ here) * few + slot % few
    valid = slot[None, :] < lens[:, None]
    key_bias = jnp.where(valid, 0.0, -1000000000.0)[:, :, None]
    valid = valid.reshape(rows, 1)

    def by_image(value, which=range(members)):
        value = value.reshape(members, images, few, width)
        return [send(pick(value, here ^ k), SEQ, k) if k else pick(value, here) for k in which]

    def by_slot(*values):
        value = jnp.concatenate([v.reshape(images, members, few, width) for v in values])
        return [send(value[:, k], SEQ, k) if k else value[:, 0] for k in range(members)]

    def in_images(blocks):
        return jnp.stack(blocks, axis=1).reshape(rows, width)

    def in_slots(blocks):
        blocks = jnp.stack(blocks)
        kinds = blocks.shape[1] // images
        blocks = jnp.concatenate([pick(blocks, here ^ k).reshape(kinds, images, few, width) for k in range(members)], axis=1)
        return [blocks[i] for i in range(kinds)]

    def unpack(vectors):
        vectors = vectors.astype(F32)
        return [vectors[:, c : c + n].reshape(1, -1) for c, n in zip(cuts, sizes)]

    if staged:
        cut_qkv, cut_out, cut_up = (Split(w.shape) for w in (attn_weight, out_weight, up_weight))
        cut_down = Split(down_weight.shape, by_rows=True)
        cut_group = Split(attn_weight.shape, columns=3 * width // GROUPS)
        place = my_place()
        first, second, third = pieces(attn_weight, out_weight, up_weight, down_weight, small)
        cot = by_image(cotangent, range(members - 1))
        tokens, cot, cotangent, z1, second, third = tie(
            by_image(tokens), cot, cotangent, exchange(first, "z"), second, third
        )
        tokens = in_images(tokens)
        x1, y1 = swap(z1, "x"), swap(z1, "y")
        z2 = exchange(second, "z")
        x1, y1, z1, third = tie(x1, y1, z1, third)
        vec_z, vec_y = (v[:, : sum(sizes) // LANES, -LANES:].reshape(v.shape[0], -1) for v in (z1, y1))
        vectors = unpack(order_vectors(vec_z, vec_y))
        d1, c1, z2, vectors, third, tokens = tie(
            corner(x1, y1), core_swap(z1, x1, y1), z2, vectors, third, tokens
        )
        gain_a, shift_a, bias_qv, bias_out, gain_b, shift_b, bias_up, bias_down = vectors
        arrays = (z1, x1, y1, *d1, *c1, *core_swap(*d1))
        qkv_full = Weight(arrays, blocks=GROUPS, step=3 * width // GROUPS)
        x2, y2 = swap(z2, "x"), swap(z2, "y")
        normed_a, joint = project(place, tokens, gain_a, shift_a, qkv_full, bias_qv)
        joint, third = tie(joint, third)
        z3 = exchange(third, "z")
        joint, x2, y2, c_z2, normed_a, cotangent = tie(joint, x2, y2, swap(z2, "c"), normed_a, cotangent)
        joint = joint.reshape(images, slots, 3 * width)
        d2, c2 = corner(x2, y2), (c_z2, *core_swap(x2, y2))
        context, lse = attention(key_bias, joint)
        context, d2, c2, z3, cot = tie(
            context.reshape(rows, width), d2, c2, z3, cot + by_image(cotangent, [members - 1])
        )
        cot = in_images(cot)
        x3, y3 = swap(z3, "x"), swap(z3, "y")
        arrays = (z2, x2, y2, *d2, *c2, *core_swap(*d2))
        up_full = Weight(arrays, blocks=cut_up.columns // STEP)
        out_full = Weight(arrays, base=cut_up.wide, blocks=2, step=cut_out.wide)
        middle, normed_b, hidden, slope, hidden_other = expand(
            place, tokens, context, out_full, bias_out, gain_b, shift_b, up_full, bias_up
        )
        grad_out = jnp.where(valid, cot, jnp.zeros_like(cot))
        hidden, hidden_other, slope, x3, y3, c_z3, grad_out, out_sib = tie(
            hidden, hidden_other, slope, x3, y3, swap(z3, "c"), grad_out, swap(grad_out, "c")
        )
    else:
        vectors = unpack(lax.all_gather(packed, FSDP, axis=0))
        gain_a, shift_a, bias_qv, bias_out, gain_b, shift_b, bias_up, bias_down = vectors
        place = jnp.zeros((3,), jnp.int32)
        qkv_full, out_full, up_full, down_full = (
            Weight([lax.all_gather(w, FSDP, axis=0, tiled=True)], by_rows=w is down_weight)
            for w in (grouped(attn_weight), out_weight, up_weight, down_weight)
        )
        qkv_full.step, out_full.step = 3 * width // GROUPS, width // 2
        tokens = in_images(by_image(tokens))
        cot = in_images(by_image(cotangent))
        grad_out = jnp.where(valid, cot, jnp.zeros_like(cot))
        normed_a, joint = project(place, tokens, gain_a, shift_a, qkv_full, bias_qv)
        joint = joint.reshape(images, slots, 3 * width)
        context, lse = attention(key_bias, joint)
        context = context.reshape(rows, width)
        middle, normed_b, hidden, slope, hidden_other = expand(
            place, tokens, context, out_full, bias_out, gain_b, shift_b, up_full, bias_up
        )

    g_bias_down = jnp.sum(grad_out.astype(F32), axis=0, keepdims=True)
    valid_wide = valid.astype(F32)

    def back_attention(grad_context, group):
        saved = (lse, context.reshape(images, slots, width), grad_context)
        grad = attention(key_bias, joint, saved, group)
        return grad.reshape(rows, 3 * width // GROUPS)

    shard_count = lax.axis_size(FSDP)
    depth = lax.axis_size("z")
    if staged:
        d3, c3 = corner(x3, y3), (c_z3, *core_swap(x3, y3))
        down_parts = grad_parts([(hidden, swap(hidden_other, "c"), grad_out, out_sib, 0, 0)], cut_down, depth)
        down_parts, slope, d3, c3, hidden, g_bias_down, valid_wide = tie(
            down_parts, slope, d3, c3, hidden, g_bias_down, valid_wide
        )
        down_full = Weight((z3, x3, y3, *d3, *c3, *core_swap(*d3)), by_rows=True)
        down_e = swap(down_parts[3], "y")
        grad_pre, bias_up_sums, grad_middle, grad_branch, grad_context, sums_b = back(
            place, grad_out, down_full, slope, up_full, middle, gain_b, out_full
        )
        grad_pre, down_e, grad_context, grad_branch, context_sib, normed_sib_b, normed_sib = tie(
            grad_pre, down_e, grad_context, grad_branch, swap(context, "c"), swap(normed_b, "c"), swap(normed_a, "c")
        )
        grad_context = grad_context.reshape(images, slots, width)
        pre_sib, branch_sib = swap(grad_pre, "c"), swap(grad_branch, "c")
        down_x, down_y = swap(add(down_parts[1], down_e), "x"), swap(down_parts[2], "y")
        joint_0 = back_attention(grad_context, 0)
        joint_0, grad_context, pre_sib, branch_sib = tie(joint_0, grad_context, pre_sib, branch_sib)
        half = cut_up.wide // 512 // 2
        up_job = (normed_b, normed_sib_b, grad_pre, pre_sib)
        a_parts = grad_parts([up_job + (0, half)], cut_up, depth)
        joint_0_sib = swap(joint_0, "c")
        a_parts, grad_context = tie(a_parts, grad_context)
        a_e = swap(a_parts[3], "y")
        out_job = (context, context_sib, grad_branch, branch_sib, 0, cut_out.wide // 512)
        b_parts = grad_parts([up_job + (half, half), out_job], cut_up, depth)
        b_parts, grad_context, a_e, down_x, down_y = tie(b_parts, grad_context, a_e, down_x, down_y)
        a_x, a_y = swap(add(a_parts[1], a_e), "x"), swap(a_parts[2], "y")
        b_e = swap(b_parts[3], "y")
        down_b = grad_z(down_parts, down_x, down_y)
        qkv_job = lambda joint, sib: [(normed_a, normed_sib, joint, sib, 0, 1)]
        parts_0 = grad_parts(qkv_job(joint_0, joint_0_sib), cut_group, depth, cut_group.wide)
        parts_0, grad_context = tie(parts_0, grad_context)
        e_0 = swap(parts_0[3], "x")
        joint_1 = back_attention(grad_context, 1)
        joint_1, e_0, a_x, a_y, b_e, down_b, hidden = tie(joint_1, e_0, a_x, a_y, b_e, down_b, hidden)
        b_x, b_y = swap(add(b_parts[1], b_e), "x"), swap(b_parts[2], "y")
        a_z = grad_z(a_parts, a_x, a_y)
        x_0, y_0 = swap(parts_0[1], "x"), swap(add(parts_0[2], e_0), "y")
        parts_1 = grad_parts(qkv_job(joint_1, swap(joint_1, "c")), cut_group, depth, cut_group.wide)
        parts_1, joint_1 = tie(parts_1, joint_1)
        e_1 = swap(parts_1[3], "y")
        input_grad, joint_sums, sums_a = back_input(place, joint_0, joint_1, qkv_full, tokens, gain_a, grad_middle)
        packed = pack(shard_count, sums_a, joint_sums, sums_b, bias_up_sums, g_bias_down)
        input_grad, e_1, x_0, y_0, b_x, b_y, a_z, hidden, down_b, packed = tie(
            input_grad, e_1, x_0, y_0, b_x, b_y, a_z, hidden, down_b, packed
        )
        x_1, y_1 = swap(add(parts_1[1], e_1), "x"), swap(parts_1[2], "y")
        b_z = grad_z(b_parts, b_x, b_y)
        result = finish(place, hidden, down_full, middle, bias_down, valid_wide)
    else:
        grad_pre, bias_up_sums, grad_middle, grad_branch, grad_context, sums_b = back(
            place,
            grad_out, down_full, slope, up_full, middle, gain_b, out_full
        )
        grad_context = grad_context.reshape(images, slots, width)
        joint_0, joint_1 = (back_attention(grad_context, g) for g in range(GROUPS))
        input_grad, joint_sums, sums_a = back_input(place, joint_0, joint_1, qkv_full, tokens, gain_a, grad_middle)
        grad_joint = jnp.concatenate([joint_0, joint_1], axis=1)
        result = finish(place, hidden, down_full, middle, bias_down, valid_wide)

    if not staged:
        group = 3 * width // GROUPS
        joint_sums = ungrouped([joint_sums[:, g * group : (g + 1) * group] for g in range(GROUPS)])
        g_bias_qv = jnp.concatenate([joint_sums[:, :width], joint_sums[:, 2 * width :]], axis=1)
        small_grads = (sums_a[0], sums_a[1], g_bias_qv, sums_b[2], sums_b[0], sums_b[1], bias_up_sums, g_bias_down)
        packed = jnp.concatenate([v.reshape(shard_count, -1) for v in small_grads], axis=1)
    if staged:
        packed = packed + swap(packed, "c")
        packed = packed + swap(packed, "x")
        x_1, y_1, b_z, result, input_grad, packed, a_g, down_g = tie(
            x_1, y_1, b_z, result, input_grad, packed, grad_x(a_z), grad_x(down_b)
        )
        qkv_b = grad_z(
            tuple(jnp.concatenate([p, q], axis=2) for p, q in zip(parts_0[:1], parts_1[:1])),
            jnp.concatenate([x_0, x_1], axis=2),
            jnp.concatenate([y_0, y_1], axis=2),
        )
        outs = by_slot(input_grad, result)
        early, late = outs[:-1], outs[-1]
        qkv_b, b_g, packed, a_g, down_g, early = tie(qkv_b, grad_x(b_z), over_line(over_rows(packed)), a_g, down_g, early)
        b_g, a_g, down_g = (grad_core(*v) for v in (b_g, a_g, down_g))
        mine, from_x = grad_x(qkv_b)
        half, n_out, n_qkv = cut_up.wide // 2, cut_out.wide, cut_group.wide
        up_plan = [(0, 0, half, (0, 2 * half)), (1, 0, half, (half, 3 * half))]
        g_up, g_out, g_down = shards_of(
            (a_g, b_g, down_g),
            [
                (False, up_weight.shape, up_plan),
                (False, out_weight.shape, [(1, half, n_out, (0, n_out))]),
                (True, down_weight.shape, [(2, 0, width, None)]),
            ],
        )
        g_up, g_out, g_down, packed, late, from_x = tie(g_up, g_out, g_down, packed, late, from_x)
        outs = early + [late]
        qkv_g = grad_core(mine, from_x)
        part = width // GROUPS
        qkv_plan = []
        for g in range(GROUPS):
            for low in range(0, n_qkv, LANES):
                places = [divmod(c * n_qkv + low, part) for c in range(2)]
                places = [t * width + g * part + at for t, at in places]
                qkv_plan.append((0, g * n_qkv + low, LANES, places))
        (g_qkv,) = shards_of([qkv_g], [(False, attn_weight.shape, qkv_plan)])
    else:
        outs = by_slot(input_grad, result)
        packed = lax.psum_scatter(packed, FSDP, scatter_dimension=0)
        packed = lax.psum(packed, SEQ)
        g_qkv, g_out, g_up, g_down = (
            scatter_plain(a, g)
            for a, g in ((normed_a, grad_joint), (context, grad_branch), (normed_b, grad_pre), (hidden, grad_out))
        )
        g_qkv = ungrouped([g_qkv[:, : 3 * width // GROUPS], g_qkv[:, 3 * width // GROUPS :]])
    input_grad, layer_out = in_slots(outs)
    (g_gain_a, g_shift_a, g_bias_qv, g_bias_out, g_gain_b, g_shift_b, g_bias_up, g_bias_down) = (
        packed[c : c + n] for c, n in zip(cuts, sizes)
    )
    return (
        layer_out,
        input_grad,
        g_gain_a,
        g_shift_a,
        g_qkv,
        g_bias_qv,
        g_out,
        g_bias_out,
        g_gain_b,
        g_shift_b,
        g_up,
        g_bias_up,
        g_down,
        g_bias_down,
    )


def solution(mesh):
    shard_count, members = mesh.devices.shape
    fine = Mesh(mesh.devices.reshape(shard_count // 2, 2, members // 2, 2), FSDP + SEQ)
    rows, vector, matrix = P(FSDP, SEQ, None), P(FSDP), P(FSDP, None)
    weights = (vector, vector, matrix, vector, matrix, vector, vector, vector, matrix, vector, matrix, vector)
    return jax.shard_map(
        shards,
        mesh=fine,
        in_specs=(rows, vector) + weights + (rows,),
        out_specs=(rows, rows) + weights,
        check_vma=False,
    )
```
